128 devices in a mesh: cam: 4 (over y), ex: 8 (over x_hi, z), ey: 4 (over x_lo, core).
Axes of the slice: x: 4 (x_hi: 2, x_lo: 2; x = x_hi * 2 + x_lo), y: 4, z: 4, core: 2. Of those that a mesh axis runs over, the one named last changes fastest.
Arguments:
- scalar: float32 [32, 8, 32, 8, 512], P('ex', None, 'ey', None, 'cam'), may hold values from -3 to 3
- velocity: float32 [3, 32, 8, 32, 8, 512], P(None, 'ex', None, 'ey', None, 'cam'), may hold values from -6 to 6
- lumped_mass: float32 [32, 8, 32, 8, 512], P('ex', None, 'ey', None, 'cam'), may hold values from 0.3 to 3
- pixel_weights: bfloat16 [8, 512, 128], replicated, may hold values from -0.25 to 0.25
- cut_element: int32 [8, 16384], P(None, ('cam', 'ex', 'ey')), may hold values from 0 to 511
- pixel_block: int32 [8, 16384], P(None, ('cam', 'ex', 'ey')), may hold values from 0 to 1024, as said below
Outputs:
- advected: float32 [32, 8, 32, 8, 512], P('ex', None, 'ey', None, 'cam')
- images: float32 [8, 32768, 128], P('cam', ('ex', 'ey'))
The draws below stay inside these ranges and needn't reach their ends.
Inputs may be any that keep to these rules, and one draw needn't show every extreme that they name: `pixel_block`: A value of 1024 marks an empty slot; in each device's 128 slots of one camera the filled ones come first. `cut_element`: A local element number of the owning device, with the radial index fastest, then the azimuthal, then the axial.
All inputs are finite; a program needn't handle non-finite values.
Results may differ from the reference program's by a relative error of at most 0.0028.
Values may be sent and summed in bfloat16 or wider, within the bound.
A program may use at most 64 MiB of HBM per device.

```python
import math
import jax
import jax.numpy as jnp
import numpy as np
from jax import lax

EA = 4
EB = 8
EC = 16
SLOTS = 128
NBLK = 1024
PIX = 128
NA = 32
NB = 32
NC = 64
CAMS = 8
N_CAM = 4
N_EX = 8
N_EY = 4


def node_parity_sign():
    nodes = jnp.arange(8, dtype=jnp.int32)
    depth = jnp.arange(NC * 8, dtype=jnp.int32) % 8
    parity = nodes[None, :, None, None, None] + nodes[None, None, None, :, None] + depth[None, None, None, None, :]
    return (1 - 2 * (parity % 2)).astype(jnp.float32)


def draw_scalar(key, part):
    size_key, noise_key = jax.random.split(jax.random.fold_in(key, 11))
    shape = (NA, 8, NB, 8, NC * 8)
    sign = node_parity_sign()
    magnitude = jax.random.uniform(size_key, shape, jnp.float32, 0.4, 1.2)
    noise = 0.6 * jnp.clip(jax.random.normal(noise_key, shape, jnp.float32), -3.0, 3.0)
    return (sign * magnitude + noise).astype(jnp.float32)


def draw_velocity(key, part):
    size_key, sign_key = jax.random.split(jax.random.fold_in(key, 23))
    shape = (3, NA, 8, NB, 8, NC * 8)
    magnitude = jax.random.uniform(size_key, shape, jnp.float32, 3.0, 6.0)
    sign = (2 * jax.random.randint(sign_key, shape, 0, 2) - 1).astype(jnp.float32)
    return (sign * magnitude).astype(jnp.float32)


def draw_pixel_block(key, part):
    count_key, block_key = jax.random.split(key)
    devices_all = N_CAM * N_EX * N_EY
    counts = jax.random.randint(count_key, (CAMS, devices_all), SLOTS // 4, SLOTS + 1)
    blocks = jax.random.randint(block_key, (CAMS, SLOTS * devices_all), 0, NBLK)
    position = jnp.arange(SLOTS * devices_all) % SLOTS
    owner_dev = jnp.arange(SLOTS * devices_all) // SLOTS
    is_live = position[None, :] < counts[:, owner_dev]
    return jnp.where(is_live, blocks, NBLK).astype(jnp.int32)


def with_ends(entries, rng, low, top_value):
    longest = entries.shape.index(max(entries.shape))
    spots = []
    for shift in (0, 1):
        where = [jax.random.randint(jax.random.fold_in(rng, axis), (), 0, length) for axis, length in enumerate(entries.shape)]
        where[longest] = (where[longest] + shift) % entries.shape[longest]
        spots.append(tuple(where))
    return entries.at[spots[0]].set(low).at[spots[1]].set(top_value)


def shard_levels(rng, dims, pieces, smallest, high):
    def one(dim, parts):
        heights = jax.random.uniform(jax.random.fold_in(jax.random.fold_in(rng, 6), dim), (parts,), jnp.float32, smallest / len(pieces), high / len(pieces))
        return jnp.repeat(jnp.exp(heights), dims[dim] // parts).reshape((-1,) + (1,) * (len(dims) - dim - 1))

    factor_of = one(*pieces[0])
    for cut in pieces[1:]:
        factor_of = factor_of * one(*cut)
    return factor_of


def bell_draw(stream_key, shape, scale, most, kind=jnp.bfloat16):
    values = jax.random.normal(stream_key, shape, jnp.float32) * scale
    return jnp.minimum(jnp.maximum(values, -most), most).astype(kind)


def setup_inputs(seed: int = 0) -> dict:
    key_list = jax.random.split(jax.random.key(seed), 7)
    return {
        "scalar": draw_scalar(jax.random.fold_in(key_list[6], 71), 0),
        "velocity": draw_velocity(jax.random.fold_in(key_list[6], 71), 0),
        "lumped_mass": jnp.clip(jnp.exp(math.log(3.0) - 2.3025851 * jax.random.uniform(key_list[2], (NA, 8, NB, 8, NC * 8), jnp.float32) ** shard_levels(key_list[2], (NA, 8, NB, 8, NC * 8), ((0, 8), (2, 4), (4, 4)), -0.2, 0.2)), 0.3, 3.0),
        "pixel_weights": bell_draw(key_list[3], (CAMS, 512, PIX), 512 ** -0.5, 0.25),
        "cut_element": with_ends(jax.random.randint(key_list[4], (CAMS, SLOTS * N_CAM * N_EX * N_EY), 0, EA * EB * EC), jax.random.fold_in(key_list[4], 1), 0, (EA * EB * EC) - 1).astype(jnp.int32),
        "pixel_block": draw_pixel_block(jax.random.fold_in(key_list[6], 71), 0),
    }


time_step = 0.01


def legendre_seven(points):
    previous = points * 0.0 + 1.0
    current = points * 1.0
    for order in range(1, 7):
        following = ((2 * order + 1) * points * current - order * previous) / (order + 1)
        previous = current
        current = following
    return current


def gll_derivative():
    degree = 7
    gll_nodes = np.array([-1.0, -0.8717401485096066, -0.5917001814331423, -0.2092992179024789, 0.2092992179024789, 0.5917001814331423, 0.8717401485096066, 1.0])
    values = legendre_seven(gll_nodes)
    derivative = np.zeros((degree + 1, degree + 1))
    for target in range(degree + 1):
        for source in range(degree + 1):
            if target != source:
                derivative[target, source] = values[target] / (values[source] * (gll_nodes[target] - gll_nodes[source]))
    derivative[0, 0] = -degree * (degree + 1) / 4.0
    derivative[degree, degree] = degree * (degree + 1) / 4.0
    return derivative


def pair_sum(extended, dim):
    length = extended.shape[dim] - 2
    middle = lax.slice_in_dim(extended, 1, length + 1, 1, dim)
    following = lax.slice_in_dim(extended, 2, length + 2, 1, dim)
    preceding = lax.slice_in_dim(extended, 0, length, 1, dim)
    shape = [1] * extended.ndim
    shape[dim] = length
    node = (jnp.arange(length, dtype=jnp.int32) % 8).reshape(shape)
    is_last = (node == 7).astype(jnp.float32)
    is_first = (node == 0).astype(jnp.float32)
    return middle + is_last * following + is_first * preceding


def wrap_pad(stack, dim):
    length = stack.shape[dim]
    return jnp.concatenate([lax.slice_in_dim(stack, length - 1, length, 1, dim), stack, lax.slice_in_dim(stack, 0, 1, 1, dim)], axis=dim)


def assemble(stack):
    summed = pair_sum(wrap_pad(stack, 1), 1)
    summed = pair_sum(wrap_pad(summed, 2), 2)
    zero_plane = jnp.zeros(summed.shape[:3] + (1,), jnp.float32)
    return pair_sum(jnp.concatenate([zero_plane, summed, zero_plane], axis=3), 3)


def convect(field, velocity, derivative):
    along_axial = jnp.einsum("pi,aibjz->apbjz", derivative, field, precision=lax.Precision.HIGHEST)
    along_azimuth = jnp.einsum("qj,aibjz->aibqz", derivative, field, precision=lax.Precision.HIGHEST)
    shape = field.shape
    split = field.reshape(shape[:4] + (shape[4] // 8, 8))
    along_radius = jnp.einsum("rk,aibjck->aibjcr", derivative, split, precision=lax.Precision.HIGHEST).reshape(shape)
    return velocity[0] * along_axial + velocity[1] * along_azimuth + velocity[2] * along_radius


def reference(scalar, velocity, lumped_mass, pixel_weights, cut_element, pixel_block):
    derivative = jnp.asarray(gll_derivative(), jnp.float32)
    shape = scalar.shape
    flat = (shape[0] * 8, shape[2] * 8, shape[4])
    first_stack = jnp.stack([(lumped_mass * convect(scalar, velocity, derivative)).reshape(flat), lumped_mass.reshape(flat)])
    first_sums = assemble(first_stack)
    assembled_mass = first_sums[1]
    rate_first = (first_sums[0] / assembled_mass).reshape(shape)
    first = scalar - time_step * rate_first
    second_stack = (lumped_mass * convect(first, velocity, derivative)).reshape((1,) + flat)
    rate_second = (assemble(second_stack)[0] / assembled_mass).reshape(shape)
    second = first - time_step * rate_second
    advected = 0.5 * (scalar + second)

    elements = advected.astype(jnp.bfloat16).reshape(NA, 8, NB, 8, NC, 8).transpose(0, 2, 4, 1, 3, 5).reshape(NA * NB * NC, 512)
    total = SLOTS * N_CAM * N_EX * N_EY
    owner_dev = jnp.arange(total, dtype=jnp.int32) // SLOTS
    cam_index = owner_dev // (N_EX * N_EY)
    ex_index = (owner_dev // N_EY) % N_EX
    ey_index = owner_dev % N_EY
    axial = ex_index[None, :] * EA + cut_element // (EB * EC)
    azimuth = ey_index[None, :] * EB + (cut_element // EC) % EB
    radial = cam_index[None, :] * EC + cut_element % EC
    flat_index = ((axial * NB + azimuth) * NC + radial).astype(jnp.int32)
    column = ex_index[None, :] * N_EY + ey_index[None, :]
    columns_all = N_EX * N_EY * NBLK
    target = jnp.where(pixel_block < NBLK, column * NBLK + pixel_block, columns_all).astype(jnp.int32)

    def render(packed):
        indices, targets, weight_rows = packed
        picked_rows = jnp.take(elements, indices, axis=0)
        values = jnp.dot(picked_rows, weight_rows, preferred_element_type=jnp.float32)
        return jnp.zeros((columns_all, PIX), jnp.float32).at[targets].add(values, mode="drop")

    images = lax.map(render, (flat_index, target, pixel_weights))
    return advected, images
```

```python
import functools

import jax
import jax.numpy as jnp
import ml_dtypes
import numpy as np
from jax import lax
from jax.experimental import pallas as pl
from jax.experimental.pallas import tpu as pltpu
from jax.sharding import PartitionSpec as P

NBLK = 1024
STEP = 0.01
F32 = jnp.float32
BF16 = jnp.bfloat16


def legendre_seven(points):
    previous = points * 0.0 + 1.0
    current = points * 1.0
    for order in range(1, 7):
        following = ((2 * order + 1) * points * current - order * previous) / (order + 1)
        previous = current
        current = following
    return current


def gll_derivative():
    degree = 7
    gll_nodes = np.array(
        [
            -1.0,
            -0.8717401485096066,
            -0.5917001814331423,
            -0.2092992179024789,
            0.2092992179024789,
            0.5917001814331423,
            0.8717401485096066,
            1.0,
        ]
    )
    values = legendre_seven(gll_nodes)
    derivative = np.zeros((degree + 1, degree + 1))
    for target in range(degree + 1):
        for source in range(degree + 1):
            if target != source:
                derivative[target, source] = values[target] / (
                    values[source] * (gll_nodes[target] - gll_nodes[source])
                )
    derivative[0, 0] = -degree * (degree + 1) / 4.0
    derivative[degree, degree] = degree * (degree + 1) / 4.0
    return derivative


DERIV = gll_derivative()


def radial_matrix():
    table = np.kron(np.eye(16), DERIV.T).astype(np.float32)
    high = table.astype(ml_dtypes.bfloat16)
    low = (table - high.astype(np.float32)).astype(ml_dtypes.bfloat16)
    return np.block([[high, low], [high, np.zeros_like(low)]])


def azimuth_table():
    rows = np.arange(8)
    shifts = np.stack([DERIV[rows, (rows + d) % 8] for d in range(8)])
    return np.broadcast_to(shifts[:, :, None], (8, 8, 128)).astype(np.float32)


SIGNS = [
    (sx, sy, sz)
    for sx in (-1, 0, 1)
    for sy in (-1, 0, 1)
    for sz in (-1, 0, 1)
    if (sx, sy, sz) != (0, 0, 0)
]


def kernel(
    sizes,
    scalar_h,
    vel_h,
    mass_h,
    wts_h,
    cut_h,
    blk_h,
    tab_h,
    azi_h,
    adv_h,
    img_h,
    fld,
    vel,
    mass,
    wts,
    cut,
    blk,
    tab,
    azi,
    g_ref,
    first,
    winv,
    radial,
    adv,
    plane,
    rows,
    cols,
    lines,
    r_plane,
    r_rows,
    r_cols,
    r_xy,
    r_xz,
    r_yz,
    r_xyz,
    xcol,
    wide,
    wts_p,
    cut_hot,
    img_hot,
    elems,
    v_send,
    v_recv,
    blk_recv,
    img,
    in_sem,
    vel_sem,
    out_sem,
    send_sem,
    recv_sem,
    v_send_sem,
    v_recv_sem,
    b_send_sem,
    b_recv_sem,
):
    n_cam, n_ex, n_ey = sizes
    cam, ex, ey = lax.axis_index("cam"), lax.axis_index("ex"), lax.axis_index("ey")

    def peer(sx, sy, sz):
        return {
            "cam": lax.rem(cam + (sz + n_cam), n_cam),
            "ex": lax.rem(ex + (sx + n_ex), n_ex),
            "ey": lax.rem(ey + (sy + n_ey), n_ey),
        }

    def load(src, dst, sem):
        copy = pltpu.make_async_copy(src, dst, sem)
        copy.start()
        return copy

    load_mass = load(mass_h, mass, in_sem.at[0])
    load_fld = load(scalar_h, fld, in_sem.at[1])
    load_tab = load(tab_h, tab, in_sem.at[2])
    load_azi = load(azi_h, azi, in_sem.at[3])
    for a in range(4):
        load(vel_h.at[:, pl.ds(8 * a, 8)], vel.at[:, pl.ds(8 * a, 8)], vel_sem.at[a])
    load_blk = load(blk_h, blk, in_sem.at[4])
    load_cut = load(cut_h, cut, in_sem.at[5])
    load_wts = load(wts_h, wts, in_sem.at[6])

    barrier = pltpu.get_barrier_semaphore()
    for s in SIGNS:
        pl.semaphore_signal(barrier, inc=1, device_id=peer(*s), device_id_type=pl.DeviceIdType.MESH)
    for d in range(2, n_cam - 1):
        pl.semaphore_signal(
            barrier, inc=1, device_id=peer(0, 0, d), device_id_type=pl.DeviceIdType.MESH
        )

    lane = lax.broadcasted_iota(jnp.int32, (8, 128), 1)
    sub = lax.broadcasted_iota(jnp.int32, (8, 128), 0)
    even = lane % 2 == 0
    take_next = (lane % 8 == 7) & (lane != 127)
    take_prev = (lane % 8 == 0) & (lane != 0)
    edge = (lane == 0) | (lane == 127)
    zero = jnp.zeros((8, 128), F32)

    def lane_pairs(g):
        return (
            g
            + jnp.where(take_next, pltpu.roll(g, 127, 1), zero)
            + jnp.where(take_prev, pltpu.roll(g, 1, 1), zero)
        )

    copies = []

    def send(src, dst, e, s):
        which = e * 26 + SIGNS.index(s)
        copy = pltpu.make_async_remote_copy(
            src_ref=src,
            dst_ref=dst,
            send_sem=send_sem.at[which],
            recv_sem=recv_sem.at[which],
            device_id=peer(*s),
            device_id_type=pl.DeviceIdType.MESH,
        )
        copy.start()
        copies.append(copy)
        return copy

    def gather_faces(ref, e, wait_entry):
        @pl.loop(0, 4)
        def _(a):
            for i in range(8):
                n = 8 * a + i
                both = ref[n, pl.ds(7, 7, stride=8), :] + ref[n, pl.ds(8, 7, stride=8), :]
                ref[n, pl.ds(7, 7, stride=8), :] = both
                ref[n, pl.ds(8, 7, stride=8), :] = both

        for a in range(3):
            both = ref[8 * a + 7] + ref[8 * a + 8]
            ref[8 * a + 7] = both
            ref[8 * a + 8] = both
        plane[e, 0] = ref[0]
        plane[e, 1] = ref[31]
        wait_entry()
        started = []
        for px in (0, 1):
            started.append(send(plane.at[e, px], r_plane.at[e, px], e, (2 * px - 1, 0, 0)))
            for py in (0, 1):
                started.append(
                    send(
                        plane.at[e, px, pl.ds(56 * py, 8)],
                        r_xy.at[e, px, py],
                        e,
                        (2 * px - 1, 2 * py - 1, 0),
                    )
                )
        for n in range(32):
            rows[e, 0, n : n + 1, :] = ref[n, 0:1, :]
            rows[e, 1, n : n + 1, :] = ref[n, 63:64, :]
        for py in (0, 1):
            started.append(send(rows.at[e, py], r_rows.at[e, py], e, (0, 2 * py - 1, 0)))

        @pl.loop(0, 4)
        def _(a):
            acc = zero
            for i in range(8):
                for b in range(8):
                    spot = 8 * i + b
                    moved = pltpu.roll(ref[8 * a + i, 8 * b : 8 * b + 8, :], 2 * spot + 1, 1)
                    acc = jnp.where((lane == 2 * spot) | (lane == 2 * spot + 1), moved, acc)
            cols[e, a] = acc

        low, high = zero, zero
        for a in range(4):
            low = jnp.where(sub == a, jnp.broadcast_to(cols[e, a, 0:1, :], (8, 128)), low)
            high = jnp.where(sub == a, jnp.broadcast_to(cols[e, a, 7:8, :], (8, 128)), high)
        lines[e, 0] = low
        lines[e, 1] = high
        for pz in (0, 1):
            sz = 2 * pz - 1
            started.append(send(cols.at[e], r_cols.at[e, pz], e, (0, 0, sz)))
            for px in (0, 1):
                started.append(
                    send(cols.at[e, 3 * px], r_xz.at[e, px, pz], e, (2 * px - 1, 0, sz))
                )
                for py in (0, 1):
                    started.append(
                        send(
                            lines.at[e, py],
                            r_xyz.at[e, px, py, pz],
                            e,
                            (2 * px - 1, 2 * py - 1, sz),
                        )
                    )
            for py in (0, 1):
                started.append(send(lines.at[e, py], r_yz.at[e, py, pz], e, (0, 2 * py - 1, sz)))
        return started

    def add_faces(ref, e, started):
        for copy in started:
            copy.wait_recv()
        ref[0] = ref[0] + r_plane[e, 1]
        ref[31] = ref[31] + r_plane[e, 0]
        for n in range(32):
            ref[n, 0:1, :] = ref[n, 0:1, :] + r_rows[e, 1, n : n + 1, :]
            ref[n, 63:64, :] = ref[n, 63:64, :] + r_rows[e, 0, n : n + 1, :]
        for px in (0, 1):
            for py in (0, 1):
                n, row, got = (0 if px else 31), (0 if py else 63), (7 if py else 0)
                ref[n, row : row + 1, :] = (
                    ref[n, row : row + 1, :] + r_xy[e, px, py, got : got + 1, :]
                )
        across = []
        for py in (0, 1):
            t = jnp.where(even, r_yz[e, py, 1], r_yz[e, py, 0])
            for px in (0, 1):
                c = jnp.where(even, r_xyz[e, px, py, 1], r_xyz[e, px, py, 0])
                if px:
                    c = pltpu.roll(pltpu.roll(c, 16, 1), 5, 0)
                    t = t + jnp.where((lane < 16) & (sub == 0), c, zero)
                else:
                    c = pltpu.roll(pltpu.roll(c, 112, 1), 3, 0)
                    t = t + jnp.where((lane >= 112) & (sub == 3), c, zero)
            t = pltpu.roll(t, 114 if py else 14, 1)
            t = jnp.where((lane % 16 < 2) if py else (lane % 16 >= 14), t, zero)
            across.append(t)
        from_upper = jnp.where(cam < n_cam - 1, 1.0, 0.0).astype(F32)
        from_lower = jnp.where(cam > 0, 1.0, 0.0).astype(F32)
        keep = jnp.where(even, jnp.full((8, 128), from_upper), jnp.full((8, 128), from_lower))
        for a in range(4):
            q = jnp.where(even, r_cols[e, 1, a], r_cols[e, 0, a])
            q = q + jnp.where(sub == 0, jnp.broadcast_to(across[1][a : a + 1, :], (8, 128)), zero)
            q = q + jnp.where(sub == 7, jnp.broadcast_to(across[0][a : a + 1, :], (8, 128)), zero)
            if a == 0:
                c = jnp.where(even, r_xz[e, 1, 1], r_xz[e, 1, 0])
                q = q + jnp.where(lane < 16, pltpu.roll(c, 16, 1), zero)
            if a == 3:
                c = jnp.where(even, r_xz[e, 0, 1], r_xz[e, 0, 0])
                q = q + jnp.where(lane >= 112, pltpu.roll(c, 112, 1), zero)
            x = jnp.where(even, pltpu.roll(q, 127, 1), pltpu.roll(q, 1, 1))
            xcol[a] = x * keep

    def total(ref, x, n, i, b):
        spot = 8 * i + b
        return ref[n, 8 * b : 8 * b + 8, :] + jnp.where(
            edge, pltpu.roll(x, 127 - 2 * spot, 1), zero
        )

    def convect(src, a):
        block = src[pl.ds(8 * a, 8)].reshape(512, 128)
        high = block.astype(BF16)
        low = (block - high.astype(F32)).astype(BF16)
        both = jnp.dot(
            jnp.concatenate([high, low], axis=1), tab[...], preferred_element_type=F32
        )
        radial[...] = (both[:, :128] + both[:, 128:]).reshape(8, 64, 128)
        for b in range(8):
            part = slice(8 * b, 8 * b + 8)
            f = [src[8 * a + i, part, :] for i in range(8)]
            plus = [f[p] + f[7 - p] for p in range(4)]
            minus = [f[p] - f[7 - p] for p in range(4)]
            axial = [None] * 8
            for i in range(4):
                x = y = None
                for p in range(4):
                    alpha = float((DERIV[i, p] + DERIV[i, 7 - p]) / 2)
                    beta = float((DERIV[i, p] - DERIV[i, 7 - p]) / 2)
                    x = alpha * plus[p] if x is None else x + alpha * plus[p]
                    y = beta * minus[p] if y is None else y + beta * minus[p]
                axial[i] = x + y
                axial[7 - i] = y - x
            for i in range(8):
                n = 8 * a + i
                turned = azi[0] * f[i]
                for d in range(1, 8):
                    turned = turned + azi[d] * pltpu.roll(f[i], 8 - d, 0)
                c = (
                    vel[0, n, part, :] * axial[i]
                    + vel[1, n, part, :] * turned
                    + vel[2, n, part, :] * radial[i, part, :]
                )
                g_ref[n, part, :] = lane_pairs(mass[n, part, :] * c)

    load_mass.wait()

    @pl.loop(0, 4)
    def _(a):
        for i in range(8):
            for b in range(8):
                n, part = 8 * a + i, slice(8 * b, 8 * b + 8)
                winv[n, part, :] = lane_pairs(mass[n, part, :])

    sent_mass = gather_faces(winv, 0, lambda: pl.semaphore_wait(barrier, 26 + n_cam - 3))

    load_blk.wait()
    blk_copies = []
    for d in range(1, n_cam):
        copy = pltpu.make_async_remote_copy(
            src_ref=blk,
            dst_ref=blk_recv.at[d],
            send_sem=b_send_sem.at[d],
            recv_sem=b_recv_sem.at[d],
            device_id=peer(0, 0, d),
            device_id_type=pl.DeviceIdType.MESH,
        )
        copy.start()
        blk_copies.append(copy)

    load_fld.wait()
    load_tab.wait()
    load_azi.wait()

    @pl.loop(0, 4)
    def _(a):
        part = pl.ds(pl.multiple_of(8 * a, 8), 8)
        pltpu.make_async_copy(vel_h.at[:, part], vel.at[:, part], vel_sem.at[a]).wait()
        convect(fld, a)

    sent_one = gather_faces(g_ref, 1, lambda: None)

    add_faces(winv, 0, sent_mass)

    @pl.loop(0, 4)
    def _(a):
        x = xcol[a]
        for i in range(8):
            for b in range(8):
                n = 8 * a + i
                winv[n, 8 * b : 8 * b + 8, :] = -STEP / total(winv, x, n, i, b)

    add_faces(g_ref, 1, sent_one)

    @pl.loop(0, 4)
    def _(a):
        x = xcol[a]
        for i in range(8):
            for b in range(8):
                n, part = 8 * a + i, slice(8 * b, 8 * b + 8)
                first[n, part, :] = fld[n, part, :] + winv[n, part, :] * total(g_ref, x, n, i, b)
        convect(first, a)

    sent_two = gather_faces(g_ref, 2, lambda: None)

    load_cut.wait()
    load_wts.wait()

    @pl.loop(0, 8)
    def _(m):
        wide[...] = wts[m].astype(F32)
        for k in range(8):
            wts_p[m, 64 * k : 64 * k + 64, :] = wide[pl.ds(k, 64, stride=8), :].astype(BF16)
        chosen = jnp.broadcast_to(cut[pl.ds(m, 1), :].astype(F32), (128, 128)).T
        place = lax.broadcasted_iota(jnp.int32, (128, 128), 1).astype(F32)
        for q in range(4):
            cut_hot[m, :, 128 * q : 128 * q + 128] = jnp.where(
                chosen == place + 128.0 * q, 1.0, 0.0
            ).astype(BF16)

    for copy in blk_copies:
        copy.wait_recv()
    for d in range(n_cam):
        for t in range(2):
            if d == 0:
                ids = blk[pl.ds(2 * cam + t, 1), :]
            else:
                ids = blk_recv[d, pl.ds(2 * cam + t, 1), :]
            ids = jnp.broadcast_to(ids, (128, 128))
            for h in range(8):
                block_id = lax.broadcasted_iota(jnp.int32, (128, 128), 0) + 128 * h
                img_hot[t, 128 * h : 128 * h + 128, 128 * d : 128 * d + 128] = jnp.where(
                    ids == block_id, 1.0, 0.0
                ).astype(BF16)

    add_faces(g_ref, 2, sent_two)

    wide_lane = lax.broadcasted_iota(jnp.int32, (64, 128), 1)
    row64 = lax.broadcasted_iota(jnp.int32, (64, 128), 0)
    select = jnp.where(
        (wide_lane // 8 == row64 % 16) & ((wide_lane % 8) // 2 == row64 // 16), 1.0, 0.0
    ).astype(BF16)

    @pl.loop(0, 4)
    def _(a):
        x = xcol[a]
        for i in range(8):
            for b in range(8):
                n, part = 8 * a + i, slice(8 * b, 8 * b + 8)
                second = first[n, part, :] + winv[n, part, :] * total(g_ref, x, n, i, b)
                adv[n, part, :] = 0.5 * (fld[n, part, :] + second)
        part = pl.ds(pl.multiple_of(8 * a, 8), 8)
        pltpu.make_async_copy(adv.at[part], adv_h.at[part], out_sem.at[a]).start()
        for b in range(0, 8, 2):
            pieces = []
            for c in (b, b + 1):
                block = adv[pl.ds(8 * a, 8), 8 * c : 8 * c + 8, :].reshape(64, 128)
                pieces.append(jnp.where(wide_lane % 2 == 0, block, 0.0).astype(BF16))
                pieces.append(jnp.where(wide_lane % 2 == 1, block, 0.0).astype(BF16))
            out = lax.dot_general(
                select,
                jnp.concatenate(pieces, axis=0),
                (((1,), (1,)), ((), ())),
                preferred_element_type=F32,
            ).astype(BF16)
            for c in (0, 1):
                at = pl.multiple_of(128 * a + 16 * (b + c), 16)
                for h in range(4):
                    elems[pl.ds(at, 16), 128 * h : 128 * h + 128] = out[
                        16 * h : 16 * h + 16, 128 * c : 128 * c + 128
                    ]

    v_copies = []
    for d in list(range(1, n_cam)) + [0]:
        q = lax.rem(cam + d, n_cam)
        for t in range(2):
            m = 2 * q + t
            picked = jnp.dot(cut_hot[m], elems[...], preferred_element_type=F32).astype(BF16)
            value = jnp.dot(picked, wts_p[m], preferred_element_type=F32).astype(BF16)
            if d:
                v_send[d, t] = value
            else:
                v_recv[0, t] = value
        if d:
            copy = pltpu.make_async_remote_copy(
                src_ref=v_send.at[d],
                dst_ref=v_recv.at[d],
                send_sem=v_send_sem.at[d],
                recv_sem=v_recv_sem.at[d],
                device_id=peer(0, 0, d),
                device_id_type=pl.DeviceIdType.MESH,
            )
            copy.start()
            v_copies.append(copy)

    for copy in v_copies:
        copy.wait_recv()
    for t in range(2):
        values = jnp.concatenate([v_recv[d, t] for d in range(n_cam)], axis=0)
        img[t] = jnp.dot(img_hot[t], values, preferred_element_type=F32)
        pltpu.make_async_copy(img.at[t], img_h.at[t], out_sem.at[4 + t]).start()

    for copy in copies + blk_copies + v_copies:
        copy.wait_send()
    for a in range(4):
        part = pl.ds(8 * a, 8)
        pltpu.make_async_copy(adv.at[part], adv_h.at[part], out_sem.at[a]).wait()
    for t in range(2):
        pltpu.make_async_copy(img.at[t], img_h.at[t], out_sem.at[4 + t]).wait()


def per_device(sizes, scalar, velocity, lumped_mass, pixel_weights, cut_element, pixel_block):
    n_cam = sizes[0]
    flat = (32, 64, 128)
    hbm = pl.BlockSpec(memory_space=pl.ANY)
    big = pltpu.VMEM(flat, F32)
    dma = pltpu.SemaphoreType.DMA
    advected, images = pl.pallas_call(
        functools.partial(kernel, sizes),
        out_shape=(
            jax.ShapeDtypeStruct(flat, F32),
            jax.ShapeDtypeStruct((2, NBLK, 128), F32),
        ),
        in_specs=[hbm] * 8,
        out_specs=(hbm, hbm),
        scratch_shapes=[
            big,
            pltpu.VMEM((3,) + flat, F32),
            big,
            pltpu.VMEM((8, 512, 128), BF16),
            pltpu.VMEM((8, 128), jnp.int32),
            pltpu.VMEM((8, 128), jnp.int32),
            pltpu.VMEM((256, 256), BF16),
            pltpu.VMEM((8, 8, 128), F32),
            big,
            big,
            big,
            pltpu.VMEM((8, 64, 128), F32),
            big,
            pltpu.VMEM((3, 2, 64, 128), F32),
            pltpu.VMEM((3, 2, 32, 128), F32),
            pltpu.VMEM((3, 4, 8, 128), F32),
            pltpu.VMEM((3, 2, 8, 128), F32),
            pltpu.VMEM((3, 2, 64, 128), F32),
            pltpu.VMEM((3, 2, 32, 128), F32),
            pltpu.VMEM((3, 2, 4, 8, 128), F32),
            pltpu.VMEM((3, 2, 2, 8, 128), F32),
            pltpu.VMEM((3, 2, 2, 8, 128), F32),
            pltpu.VMEM((3, 2, 2, 8, 128), F32),
            pltpu.VMEM((3, 2, 2, 2, 8, 128), F32),
            pltpu.VMEM((4, 8, 128), F32),
            pltpu.VMEM((512, 128), F32),
            pltpu.VMEM((8, 512, 128), BF16),
            pltpu.VMEM((8, 128, 512), BF16),
            pltpu.VMEM((2, NBLK, 128 * n_cam), BF16),
            pltpu.VMEM((512, 512), BF16),
            pltpu.VMEM((n_cam, 2, 128, 128), BF16),
            pltpu.VMEM((n_cam, 2, 128, 128), BF16),
            pltpu.VMEM((n_cam, 8, 128), jnp.int32),
            pltpu.VMEM((2, NBLK, 128), F32),
            dma((7,)),
            dma((4,)),
            dma((6,)),
            dma((78,)),
            dma((78,)),
            dma((n_cam,)),
            dma((n_cam,)),
            dma((n_cam,)),
            dma((n_cam,)),
        ],
        compiler_params=pltpu.CompilerParams(
            collective_id=0, has_side_effects=True, vmem_limit_bytes=48 * 1024 * 1024
        ),
    )(
        scalar.reshape(flat),
        velocity.reshape((3,) + flat),
        lumped_mass.reshape(flat),
        pixel_weights,
        cut_element,
        pixel_block,
        jnp.asarray(radial_matrix()),
        jnp.asarray(azimuth_table()),
    )
    return advected.reshape(scalar.shape), images


def solution(mesh):
    sizes = tuple(mesh.shape[name] for name in ("cam", "ex", "ey"))
    placed = (
        P("ex", None, "ey", None, "cam"),
        P(None, "ex", None, "ey", None, "cam"),
        P("ex", None, "ey", None, "cam"),
        P(),
        P(None, ("cam", "ex", "ey")),
        P(None, ("cam", "ex", "ey")),
    )
    return jax.shard_map(
        functools.partial(per_device, sizes),
        mesh=mesh,
        in_specs=placed,
        out_specs=(P("ex", None, "ey", None, "cam"), P("cam", ("ex", "ey"), None)),
        check_vma=False,
    )
```

```python
import functools

import jax
import jax.numpy as jnp
import ml_dtypes
import numpy as np
from jax import lax
from jax.experimental import pallas as pl
from jax.experimental.pallas import tpu as pltpu
from jax.sharding import PartitionSpec as P

NBLK = 1024
STEP = 0.01
F32 = jnp.float32
BF16 = jnp.bfloat16


def legendre_seven(points):
    previous = points * 0.0 + 1.0
    current = points * 1.0
    for order in range(1, 7):
        following = ((2 * order + 1) * points * current - order * previous) / (order + 1)
        previous = current
        current = following
    return current


def gll_derivative():
    degree = 7
    gll_nodes = np.array(
        [
            -1.0,
            -0.8717401485096066,
            -0.5917001814331423,
            -0.2092992179024789,
            0.2092992179024789,
            0.5917001814331423,
            0.8717401485096066,
            1.0,
        ]
    )
    values = legendre_seven(gll_nodes)
    derivative = np.zeros((degree + 1, degree + 1))
    for target in range(degree + 1):
        for source in range(degree + 1):
            if target != source:
                derivative[target, source] = values[target] / (
                    values[source] * (gll_nodes[target] - gll_nodes[source])
                )
    derivative[0, 0] = -degree * (degree + 1) / 4.0
    derivative[degree, degree] = degree * (degree + 1) / 4.0
    return derivative


DERIV = gll_derivative()


def radial_matrix():
    table = np.kron(np.eye(16), DERIV.T).astype(np.float32)
    high = table.astype(ml_dtypes.bfloat16)
    low = (table - high.astype(np.float32)).astype(ml_dtypes.bfloat16)
    return np.block([[high, low], [high, np.zeros_like(low)]])


def azimuth_table():
    rows = np.arange(8)
    shifts = np.stack([DERIV[rows, (rows + d) % 8] for d in range(8)])
    return np.broadcast_to(shifts[:, :, None], (8, 8, 128)).astype(np.float32)


SIGNS = [
    (sx, sy, sz)
    for sx in (-1, 0, 1)
    for sy in (-1, 0, 1)
    for sz in (-1, 0, 1)
    if (sx, sy, sz) != (0, 0, 0)
]


def kernel(
    sizes,
    scalar_h,
    vel_h,
    mass_h,
    wts_h,
    cut_h,
    blk_h,
    tab_h,
    azi_h,
    adv_h,
    img_h,
    fld,
    vel,
    mass,
    wts,
    cut,
    blk,
    tab,
    azi,
    g_ref,
    first,
    winv,
    radial,
    adv,
    faces_one,
    faces_two,
    xcol,
    wide,
    wts_p,
    cut_hot,
    img_hot,
    elems,
    v_send,
    v_recv,
    blk_recv,
    img,
    in_sem,
    vel_sem,
    out_sem,
    send_sem,
    recv_sem,
    v_send_sem,
    v_recv_sem,
    b_send_sem,
    b_recv_sem,
):
    n_cam, n_ex, n_ey = sizes
    cam, ex, ey = lax.axis_index("cam"), lax.axis_index("ex"), lax.axis_index("ey")
    faces = (faces_one, faces_two)

    def peer(sx, sy, sz):
        return {
            "cam": lax.rem(cam + (sz + n_cam), n_cam),
            "ex": lax.rem(ex + (sx + n_ex), n_ex),
            "ey": lax.rem(ey + (sy + n_ey), n_ey),
        }

    def load(src, dst, sem):
        copy = pltpu.make_async_copy(src, dst, sem)
        copy.start()
        return copy

    load_mass = load(mass_h, mass, in_sem.at[0])
    load_fld = load(scalar_h, fld, in_sem.at[1])
    load_tab = load(tab_h, tab, in_sem.at[2])
    load_azi = load(azi_h, azi, in_sem.at[3])
    for a in (0, 3, 1, 2):
        load(vel_h.at[:, pl.ds(8 * a, 8)], vel.at[:, pl.ds(8 * a, 8)], vel_sem.at[a])
    load_blk = load(blk_h, blk, in_sem.at[4])
    load_cut = load(cut_h, cut, in_sem.at[5])
    load_wts = load(wts_h, wts, in_sem.at[6])

    barrier = pltpu.get_barrier_semaphore()
    for s in SIGNS:
        pl.semaphore_signal(barrier, inc=1, device_id=peer(*s), device_id_type=pl.DeviceIdType.MESH)
    for d in range(2, n_cam - 1):
        pl.semaphore_signal(
            barrier, inc=1, device_id=peer(0, 0, d), device_id_type=pl.DeviceIdType.MESH
        )

    lane = lax.broadcasted_iota(jnp.int32, (8, 128), 1)
    sub = lax.broadcasted_iota(jnp.int32, (8, 128), 0)
    even = lane % 2 == 0
    take_next = (lane % 8 == 7) & (lane != 127)
    take_prev = (lane % 8 == 0) & (lane != 0)
    edge = (lane == 0) | (lane == 127)
    zero = jnp.zeros((8, 128), F32)
    from_upper = jnp.where(cam < n_cam - 1, 1.0, 0.0).astype(F32)
    from_lower = jnp.where(cam > 0, 1.0, 0.0).astype(F32)
    keep = jnp.where(even, jnp.full((8, 128), from_upper), jnp.full((8, 128), from_lower))

    def lane_pairs(g):
        return (
            g
            + jnp.where(take_next, pltpu.roll(g, 127, 1), zero)
            + jnp.where(take_prev, pltpu.roll(g, 1, 1), zero)
        )

    def twice(body):
        def outer(which):
            @pl.loop(0, 2)
            def _(t):
                body(3 * t if which == "ends" else 1 + t)

        return outer

    copies = []
    waits = {}

    def send(src, dst, e, group, s):
        which = e * 26 + SIGNS.index(s)
        copy = pltpu.make_async_remote_copy(
            src_ref=src,
            dst_ref=dst,
            send_sem=send_sem.at[which],
            recv_sem=recv_sem.at[which],
            device_id=peer(*s),
            device_id_type=pl.DeviceIdType.MESH,
        )
        copy.start()
        copies.append(copy)
        waits.setdefault((e, group), []).append(copy)

    def wait_for(e, group):
        for copy in waits[e, group]:
            copy.wait_recv()

    def pair_azimuth(ref, a):
        for i in range(8):
            n = 8 * a + i
            both = ref[n, pl.ds(7, 7, stride=8), :] + ref[n, pl.ds(8, 7, stride=8), :]
            ref[n, pl.ds(7, 7, stride=8), :] = both
            ref[n, pl.ds(8, 7, stride=8), :] = both

    def pair_axial(ref):
        for a in range(3):
            both = ref[8 * a + 7] + ref[8 * a + 8]
            ref[8 * a + 7] = both
            ref[8 * a + 8] = both

    def gather_columns(pieces):
        parts = [zero] * 4
        for at, (spot, piece) in enumerate(pieces):
            here = (lane == 2 * spot) | (lane == 2 * spot + 1)
            parts[at % 4] = jnp.where(here, pltpu.roll(piece, 2 * spot + 1, 1), parts[at % 4])
        return (parts[0] + parts[1]) + (parts[2] + parts[3])

    def pack_ends(ref, e, kind):
        plane, tile = faces[e][0], faces[e][1]
        for px in (0, 1):
            plane[px, kind] = ref[31 * px]
            tile[px, kind] = gather_columns(
                [(56 * px + b, ref[31 * px, 8 * b : 8 * b + 8, :]) for b in range(8)]
            )

    def send_ends(e):
        plane, tile, _, _, _, r_plane, r_xy, r_xz, r_xyz, _, _, _ = faces[e]
        for px in (0, 1):
            sx = 2 * px - 1
            send(plane.at[px], r_plane.at[px], e, "ends", (sx, 0, 0))
            for py in (0, 1):
                send(
                    plane.at[px, :, pl.ds(56 * py, 8)],
                    r_xy.at[px, py],
                    e,
                    "ends",
                    (sx, 2 * py - 1, 0),
                )
            for pz in (0, 1):
                sz = 2 * pz - 1
                send(tile.at[px], r_xz.at[px, pz], e, "ends", (sx, 0, sz))
                for py in (0, 1):
                    send(tile.at[px], r_xyz.at[px, py, pz], e, "ends", (sx, 2 * py - 1, sz))

    def pack_rest(ref, e, kind):
        rows, cols, lines = faces[e][2:5]
        for n in range(32):
            rows[0, kind, n : n + 1, :] = ref[n, 0:1, :]
            rows[1, kind, n : n + 1, :] = ref[n, 63:64, :]

        @pl.loop(0, 4)
        def _(a):
            cols[a, kind] = gather_columns(
                [
                    (8 * i + b, ref[8 * a + i, 8 * b : 8 * b + 8, :])
                    for i in range(8)
                    for b in range(8)
                ]
            )

        low, high = zero, zero
        for a in range(4):
            low = jnp.where(sub == a, jnp.broadcast_to(cols[a, kind, 0:1, :], (8, 128)), low)
            high = jnp.where(sub == a, jnp.broadcast_to(cols[a, kind, 7:8, :], (8, 128)), high)
        lines[0, kind] = low
        lines[1, kind] = high

    def send_rest(e):
        rows, cols, lines = faces[e][2:5]
        r_rows, r_cols, r_yz = faces[e][9:12]
        for pz in (0, 1):
            sz = 2 * pz - 1
            send(cols, r_cols.at[pz], e, "rest", (0, 0, sz))
            for py in (0, 1):
                send(lines.at[py], r_yz.at[py, pz], e, "rest", (0, 2 * py - 1, sz))
        for py in (0, 1):
            send(rows.at[py], r_rows.at[py], e, "rest", (0, 2 * py - 1, 0))

    def across_azimuth(t, py):
        t = pltpu.roll(t, 114 if py else 14, 1)
        return jnp.where((lane % 16 < 2) if py else (lane % 16 >= 14), t, zero)

    def swap(q):
        return jnp.where(even, pltpu.roll(q, 127, 1), pltpu.roll(q, 1, 1)) * keep

    def add_rest(ref, e, kind):
        r_rows, r_cols, r_yz = faces[e][9:12]
        for n in range(32):
            ref[n, 0:1, :] = ref[n, 0:1, :] + r_rows[1, kind, n : n + 1, :]
            ref[n, 63:64, :] = ref[n, 63:64, :] + r_rows[0, kind, n : n + 1, :]
        across = [
            across_azimuth(jnp.where(even, r_yz[py, 1, kind], r_yz[py, 0, kind]), py)
            for py in (0, 1)
        ]
        for a in range(4):
            q = jnp.where(even, r_cols[1, a, kind], r_cols[0, a, kind])
            q = q + jnp.where(sub == 0, jnp.broadcast_to(across[1][a : a + 1, :], (8, 128)), zero)
            q = q + jnp.where(sub == 7, jnp.broadcast_to(across[0][a : a + 1, :], (8, 128)), zero)
            xcol[kind, a] = swap(q)

    def add_ends(ref, e, kind):
        r_plane, r_xy, r_xz, r_xyz = faces[e][5:9]
        for px in (0, 1):
            n, a = (0, 0) if px else (31, 3)
            ref[n] = ref[n] + r_plane[px, kind]
            for py in (0, 1):
                row, got = (0, 7) if py else (63, 0)
                ref[n, row : row + 1, :] = (
                    ref[n, row : row + 1, :] + r_xy[px, py, kind, got : got + 1, :]
                )
            q = jnp.where(even, r_xz[px, 1, kind], r_xz[px, 0, kind])
            for py in (0, 1):
                c = jnp.where(even, r_xyz[px, py, 1, kind], r_xyz[px, py, 0, kind])
                c = pltpu.roll(across_azimuth(c, py), 1 if py else 7, 0)
                q = q + jnp.where(sub == (0 if py else 7), c, zero)
            if px:
                q = jnp.where(lane < 16, pltpu.roll(q, 16, 1), zero)
            else:
                q = jnp.where(lane >= 112, pltpu.roll(q, 112, 1), zero)
            xcol[kind, a] = xcol[kind, a] + swap(q)

    def total(ref, x, n, i, b):
        spot = 8 * i + b
        return ref[n, 8 * b : 8 * b + 8, :] + jnp.where(
            edge, pltpu.roll(x, 127 - 2 * spot, 1), zero
        )

    def convect(src, a):
        block = src[pl.ds(8 * a, 8)].reshape(512, 128)
        high = block.astype(BF16)
        low = (block - high.astype(F32)).astype(BF16)
        both = jnp.dot(
            jnp.concatenate([high, low], axis=1), tab[...], preferred_element_type=F32
        )
        radial[...] = (both[:, :128] + both[:, 128:]).reshape(8, 64, 128)
        for b in range(8):
            part = slice(8 * b, 8 * b + 8)
            f = [src[8 * a + i, part, :] for i in range(8)]
            plus = [f[p] + f[7 - p] for p in range(4)]
            minus = [f[p] - f[7 - p] for p in range(4)]
            axial = [None] * 8
            for i in range(4):
                x = y = None
                for p in range(4):
                    alpha = float((DERIV[i, p] + DERIV[i, 7 - p]) / 2)
                    beta = float((DERIV[i, p] - DERIV[i, 7 - p]) / 2)
                    x = alpha * plus[p] if x is None else x + alpha * plus[p]
                    y = beta * minus[p] if y is None else y + beta * minus[p]
                axial[i] = x + y
                axial[7 - i] = y - x
            for i in range(8):
                n = 8 * a + i
                turned = azi[0] * f[i]
                for d in range(1, 8):
                    turned = turned + azi[d] * pltpu.roll(f[i], 8 - d, 0)
                c = (
                    vel[0, n, part, :] * axial[i]
                    + vel[1, n, part, :] * turned
                    + vel[2, n, part, :] * radial[i, part, :]
                )
                g_ref[n, part, :] = lane_pairs(mass[n, part, :] * c)
        pair_azimuth(g_ref, a)

    load_mass.wait()

    @pl.loop(0, 4)
    def _(a):
        for i in range(8):
            for b in range(8):
                n, part = 8 * a + i, slice(8 * b, 8 * b + 8)
                winv[n, part, :] = lane_pairs(mass[n, part, :])
        pair_azimuth(winv, a)

    pair_axial(winv)
    pack_ends(winv, 0, 1)
    pack_rest(winv, 0, 1)

    load_fld.wait()
    load_tab.wait()
    load_azi.wait()

    @twice
    def stage_one(a):
        part = pl.ds(pl.multiple_of(8 * a, 8), 8)
        pltpu.make_async_copy(vel_h.at[:, part], vel.at[:, part], vel_sem.at[a]).wait()
        convect(fld, a)

    stage_one("ends")
    pack_ends(g_ref, 0, 0)
    pl.semaphore_wait(barrier, 26 + n_cam - 3)
    send_ends(0)
    stage_one("middle")
    pair_axial(g_ref)
    pack_rest(g_ref, 0, 0)
    send_rest(0)

    load_blk.wait()
    blk_copies = []
    for d in range(1, n_cam):
        copy = pltpu.make_async_remote_copy(
            src_ref=blk,
            dst_ref=blk_recv.at[d],
            send_sem=b_send_sem.at[d],
            recv_sem=b_recv_sem.at[d],
            device_id=peer(0, 0, d),
            device_id_type=pl.DeviceIdType.MESH,
        )
        copy.start()
        blk_copies.append(copy)

    load_cut.wait()
    load_wts.wait()

    @pl.loop(0, 8)
    def _(m):
        wide[...] = wts[m].astype(F32)
        for k in range(8):
            wts_p[m, 64 * k : 64 * k + 64, :] = wide[pl.ds(k, 64, stride=8), :].astype(BF16)
        chosen = jnp.broadcast_to(cut[pl.ds(m, 1), :].astype(F32), (128, 128)).T
        place = lax.broadcasted_iota(jnp.int32, (128, 128), 1).astype(F32)
        for q in range(4):
            cut_hot[m, :, 128 * q : 128 * q + 128] = jnp.where(
                chosen == place + 128.0 * q, 1.0, 0.0
            ).astype(BF16)

    @twice
    def stage_two(a):
        x, y = xcol[0, a], xcol[1, a]
        for i in range(8):
            for b in range(8):
                n, part = 8 * a + i, slice(8 * b, 8 * b + 8)
                factor = -STEP / total(winv, y, n, i, b)
                winv[n, part, :] = factor
                first[n, part, :] = fld[n, part, :] + factor * total(g_ref, x, n, i, b)
        convect(first, a)

    wait_for(0, "rest")
    add_rest(winv, 0, 1)
    add_rest(g_ref, 0, 0)
    stage_two("middle")
    wait_for(0, "ends")
    add_ends(winv, 0, 1)
    add_ends(g_ref, 0, 0)
    stage_two("ends")
    pack_ends(g_ref, 1, 0)
    send_ends(1)
    pair_axial(g_ref)
    pack_rest(g_ref, 1, 0)
    send_rest(1)

    for copy in blk_copies:
        copy.wait_recv()
    for d in range(n_cam):
        for t in range(2):
            if d == 0:
                ids = blk[pl.ds(2 * cam + t, 1), :]
            else:
                ids = blk_recv[d, pl.ds(2 * cam + t, 1), :]
            ids = jnp.broadcast_to(ids, (128, 128))
            for h in range(8):
                block_id = lax.broadcasted_iota(jnp.int32, (128, 128), 0) + 128 * h
                img_hot[t, 128 * h : 128 * h + 128, 128 * d : 128 * d + 128] = jnp.where(
                    ids == block_id, 1.0, 0.0
                ).astype(BF16)

    wide_lane = lax.broadcasted_iota(jnp.int32, (64, 128), 1)
    row64 = lax.broadcasted_iota(jnp.int32, (64, 128), 0)
    select = jnp.where(
        (wide_lane // 8 == row64 % 16) & ((wide_lane % 8) // 2 == row64 // 16), 1.0, 0.0
    ).astype(BF16)

    @twice
    def finish(a):
        x = xcol[0, a]
        for i in range(8):
            for b in range(8):
                n, part = 8 * a + i, slice(8 * b, 8 * b + 8)
                second = first[n, part, :] + winv[n, part, :] * total(g_ref, x, n, i, b)
                adv[n, part, :] = 0.5 * (fld[n, part, :] + second)
        part = pl.ds(pl.multiple_of(8 * a, 8), 8)
        pltpu.make_async_copy(adv.at[part], adv_h.at[part], out_sem.at[a]).start()
        for b in range(0, 8, 2):
            pieces = []
            for c in (b, b + 1):
                block = adv[pl.ds(8 * a, 8), 8 * c : 8 * c + 8, :].reshape(64, 128)
                pieces.append(jnp.where(wide_lane % 2 == 0, block, 0.0).astype(BF16))
                pieces.append(jnp.where(wide_lane % 2 == 1, block, 0.0).astype(BF16))
            out = lax.dot_general(
                select,
                jnp.concatenate(pieces, axis=0),
                (((1,), (1,)), ((), ())),
                preferred_element_type=F32,
            ).astype(BF16)
            for c in (0, 1):
                at = pl.multiple_of(128 * a + 16 * (b + c), 16)
                for h in range(4):
                    elems[pl.ds(at, 16), 128 * h : 128 * h + 128] = out[
                        16 * h : 16 * h + 16, 128 * c : 128 * c + 128
                    ]

    wait_for(1, "rest")
    add_rest(g_ref, 1, 0)
    finish("middle")
    wait_for(1, "ends")
    add_ends(g_ref, 1, 0)
    finish("ends")

    v_copies = []
    for d in sorted(range(1, n_cam), key=lambda d: -min(d, n_cam - d)) + [0]:
        q = lax.rem(cam + d, n_cam)
        for t in range(2):
            m = 2 * q + t
            picked = jnp.dot(cut_hot[m], elems[...], preferred_element_type=F32).astype(BF16)
            value = jnp.dot(picked, wts_p[m], preferred_element_type=F32).astype(BF16)
            if d:
                v_send[d, t] = value
            else:
                v_recv[0, t] = value
        if d:
            copy = pltpu.make_async_remote_copy(
                src_ref=v_send.at[d],
                dst_ref=v_recv.at[d],
                send_sem=v_send_sem.at[d],
                recv_sem=v_recv_sem.at[d],
                device_id=peer(0, 0, d),
                device_id_type=pl.DeviceIdType.MESH,
            )
            copy.start()
            v_copies.append(copy)

    for copy in copies + blk_copies:
        copy.wait_send()
    for copy in v_copies:
        copy.wait_recv()
    for t in range(2):
        values = jnp.concatenate([v_recv[d, t] for d in range(n_cam)], axis=0)
        img[t] = jnp.dot(img_hot[t], values, preferred_element_type=F32)
        pltpu.make_async_copy(img.at[t], img_h.at[t], out_sem.at[4 + t]).start()

    for copy in v_copies:
        copy.wait_send()
    for a in range(4):
        part = pl.ds(8 * a, 8)
        pltpu.make_async_copy(adv.at[part], adv_h.at[part], out_sem.at[a]).wait()
    for t in range(2):
        pltpu.make_async_copy(img.at[t], img_h.at[t], out_sem.at[4 + t]).wait()


def face_buffers(kinds):
    shapes = [
        (2, kinds, 64, 128),
        (2, kinds, 8, 128),
        (2, kinds, 32, 128),
        (4, kinds, 8, 128),
        (2, kinds, 8, 128),
        (2, kinds, 64, 128),
        (2, 2, kinds, 8, 128),
        (2, 2, kinds, 8, 128),
        (2, 2, 2, kinds, 8, 128),
        (2, kinds, 32, 128),
        (2, 4, kinds, 8, 128),
        (2, 2, kinds, 8, 128),
    ]
    return tuple(pltpu.VMEM(shape, F32) for shape in shapes)


def per_device(sizes, scalar, velocity, lumped_mass, pixel_weights, cut_element, pixel_block):
    n_cam = sizes[0]
    flat = (32, 64, 128)
    hbm = pl.BlockSpec(memory_space=pltpu.HBM)
    big = pltpu.VMEM(flat, F32)
    dma = pltpu.SemaphoreType.DMA
    advected, images = pl.pallas_call(
        functools.partial(kernel, sizes),
        out_shape=(
            jax.ShapeDtypeStruct(flat, F32),
            jax.ShapeDtypeStruct((2, NBLK, 128), F32),
        ),
        in_specs=[hbm] * 8,
        out_specs=(hbm, hbm),
        scratch_shapes=[
            big,
            pltpu.VMEM((3,) + flat, F32),
            big,
            pltpu.VMEM((8, 512, 128), BF16),
            pltpu.VMEM((8, 128), jnp.int32),
            pltpu.VMEM((8, 128), jnp.int32),
            pltpu.VMEM((256, 256), BF16),
            pltpu.VMEM((8, 8, 128), F32),
            big,
            big,
            big,
            pltpu.VMEM((8, 64, 128), F32),
            big,
            face_buffers(2),
            face_buffers(1),
            pltpu.VMEM((2, 4, 8, 128), F32),
            pltpu.VMEM((512, 128), F32),
            pltpu.VMEM((8, 512, 128), BF16),
            pltpu.VMEM((8, 128, 512), BF16),
            pltpu.VMEM((2, NBLK, 128 * n_cam), BF16),
            pltpu.VMEM((512, 512), BF16),
            pltpu.VMEM((n_cam, 2, 128, 128), BF16),
            pltpu.VMEM((n_cam, 2, 128, 128), BF16),
            pltpu.VMEM((n_cam, 8, 128), jnp.int32),
            pltpu.VMEM((2, NBLK, 128), F32),
            dma((7,)),
            dma((4,)),
            dma((6,)),
            dma((52,)),
            dma((52,)),
            dma((n_cam,)),
            dma((n_cam,)),
            dma((n_cam,)),
            dma((n_cam,)),
        ],
        compiler_params=pltpu.CompilerParams(
            collective_id=0, has_side_effects=True, vmem_limit_bytes=62 * 1024 * 1024
        ),
    )(
        scalar.reshape(flat),
        velocity.reshape((3,) + flat),
        lumped_mass.reshape(flat),
        pixel_weights,
        cut_element,
        pixel_block,
        jnp.asarray(radial_matrix()),
        jnp.asarray(azimuth_table()),
    )
    return advected.reshape(scalar.shape), images


def solution(mesh):
    sizes = tuple(mesh.shape[name] for name in ("cam", "ex", "ey"))
    placed = (
        P("ex", None, "ey", None, "cam"),
        P(None, "ex", None, "ey", None, "cam"),
        P("ex", None, "ey", None, "cam"),
        P(),
        P(None, ("cam", "ex", "ey")),
        P(None, ("cam", "ex", "ey")),
    )
    return jax.shard_map(
        functools.partial(per_device, sizes),
        mesh=mesh,
        in_specs=placed,
        out_specs=(P("ex", None, "ey", None, "cam"), P("cam", ("ex", "ey"), None)),
        check_vma=False,
    )
```

```python
import functools

import jax
import jax.numpy as jnp
import ml_dtypes
import numpy as np
from jax import lax
from jax.experimental import pallas as pl
from jax.experimental.pallas import tpu as pltpu
from jax.sharding import PartitionSpec as P

NBLK = 1024
STEP = 0.01
F32 = jnp.float32
BF16 = jnp.bfloat16


def legendre_seven(points):
    previous = points * 0.0 + 1.0
    current = points * 1.0
    for order in range(1, 7):
        following = ((2 * order + 1) * points * current - order * previous) / (order + 1)
        previous = current
        current = following
    return current


def gll_derivative():
    degree = 7
    gll_nodes = np.array(
        [
            -1.0,
            -0.8717401485096066,
            -0.5917001814331423,
            -0.2092992179024789,
            0.2092992179024789,
            0.5917001814331423,
            0.8717401485096066,
            1.0,
        ]
    )
    values = legendre_seven(gll_nodes)
    derivative = np.zeros((degree + 1, degree + 1))
    for target in range(degree + 1):
        for source in range(degree + 1):
            if target != source:
                derivative[target, source] = values[target] / (
                    values[source] * (gll_nodes[target] - gll_nodes[source])
                )
    derivative[0, 0] = -degree * (degree + 1) / 4.0
    derivative[degree, degree] = degree * (degree + 1) / 4.0
    return derivative


DERIV = gll_derivative()


def radial_matrix():
    table = np.kron(np.eye(16), DERIV.T).astype(np.float32)
    high = table.astype(ml_dtypes.bfloat16)
    low = (table - high.astype(np.float32)).astype(ml_dtypes.bfloat16)
    return np.block([[high, low], [high, np.zeros_like(low)]])


def azimuth_table():
    rows = np.arange(8)
    shifts = np.stack([DERIV[rows, (rows + d) % 8] for d in range(8)])
    return np.broadcast_to(shifts[:, :, None], (8, 8, 128)).astype(np.float32)


SIGNS = [
    (sx, sy, sz)
    for sx in (-1, 0, 1)
    for sy in (-1, 0, 1)
    for sz in (-1, 0, 1)
    if (sx, sy, sz) != (0, 0, 0)
]


def kernel(
    sizes,
    scalar_h,
    vel_h,
    mass_h,
    wts_h,
    cut_h,
    blk_h,
    tab_h,
    azi_h,
    adv,
    v_recv,
    img_hot,
    fld,
    vel,
    mass,
    wts,
    cut,
    blk,
    tab,
    azi,
    g_ref,
    first,
    winv,
    radial,
    faces_one,
    faces_two,
    xcol,
    wide,
    wts_p,
    cut_hot,
    elems,
    v_send,
    blk_recv,
    in_sem,
    vel_sem,
    send_sem,
    recv_sem,
    v_send_sem,
    v_recv_sem,
    b_send_sem,
    b_recv_sem,
):
    n_cam, n_ex, n_ey = sizes
    cam, ex, ey = lax.axis_index("cam"), lax.axis_index("ex"), lax.axis_index("ey")
    faces = (faces_one, faces_two)

    def peer(sx, sy, sz):
        return {
            "cam": lax.rem(cam + (sz + n_cam), n_cam),
            "ex": lax.rem(ex + (sx + n_ex), n_ex),
            "ey": lax.rem(ey + (sy + n_ey), n_ey),
        }

    def load(src, dst, sem):
        copy = pltpu.make_async_copy(src, dst, sem)
        copy.start()
        return copy

    load_mass = load(mass_h, mass, in_sem.at[0])
    load_fld = load(scalar_h, fld, in_sem.at[1])
    load_tab = load(tab_h, tab, in_sem.at[2])
    load_azi = load(azi_h, azi, in_sem.at[3])
    for a in (0, 3, 1, 2):
        load(vel_h.at[:, pl.ds(8 * a, 8)], vel.at[:, pl.ds(8 * a, 8)], vel_sem.at[a])
    load_blk = load(blk_h, blk, in_sem.at[4])
    load_cut = load(cut_h, cut, in_sem.at[5])
    load_wts = load(wts_h, wts, in_sem.at[6])

    barrier = pltpu.get_barrier_semaphore()
    for s in SIGNS:
        pl.semaphore_signal(barrier, inc=1, device_id=peer(*s), device_id_type=pl.DeviceIdType.MESH)
    for d in range(2, n_cam - 1):
        pl.semaphore_signal(
            barrier, inc=1, device_id=peer(0, 0, d), device_id_type=pl.DeviceIdType.MESH
        )

    lane = lax.broadcasted_iota(jnp.int32, (8, 128), 1)
    sub = lax.broadcasted_iota(jnp.int32, (8, 128), 0)
    even = lane % 2 == 0
    take_next = (lane % 8 == 7) & (lane != 127)
    take_prev = (lane % 8 == 0) & (lane != 0)
    edge = (lane == 0) | (lane == 127)
    zero = jnp.zeros((8, 128), F32)
    from_upper = jnp.where(cam < n_cam - 1, 1.0, 0.0).astype(F32)
    from_lower = jnp.where(cam > 0, 1.0, 0.0).astype(F32)
    keep = jnp.where(even, jnp.full((8, 128), from_upper), jnp.full((8, 128), from_lower))

    def lane_pairs(g):
        return (
            g
            + jnp.where(take_next, pltpu.roll(g, 127, 1), zero)
            + jnp.where(take_prev, pltpu.roll(g, 1, 1), zero)
        )

    def twice(body):
        def outer(which):
            @pl.loop(0, 2)
            def _(t):
                body(3 * t if which == "ends" else 1 + t)

        return outer

    copies = []
    waits = {}

    def send(src, dst, e, group, s):
        which = e * 26 + SIGNS.index(s)
        copy = pltpu.make_async_remote_copy(
            src_ref=src,
            dst_ref=dst,
            send_sem=send_sem.at[which],
            recv_sem=recv_sem.at[which],
            device_id=peer(*s),
            device_id_type=pl.DeviceIdType.MESH,
        )
        copy.start()
        copies.append(copy)
        waits.setdefault((e, group), []).append(copy)

    def wait_for(e, group):
        for copy in waits[e, group]:
            copy.wait_recv()

    def pair_azimuth(ref, a):
        for i in range(8):
            n = 8 * a + i
            both = ref[n, pl.ds(7, 7, stride=8), :] + ref[n, pl.ds(8, 7, stride=8), :]
            ref[n, pl.ds(7, 7, stride=8), :] = both
            ref[n, pl.ds(8, 7, stride=8), :] = both

    def pair_axial(ref):
        for a in range(3):
            both = ref[8 * a + 7] + ref[8 * a + 8]
            ref[8 * a + 7] = both
            ref[8 * a + 8] = both

    def gather_columns(pieces):
        parts = [zero] * 4
        for at, (spot, piece) in enumerate(pieces):
            here = (lane == 2 * spot) | (lane == 2 * spot + 1)
            parts[at % 4] = jnp.where(here, pltpu.roll(piece, 2 * spot + 1, 1), parts[at % 4])
        return (parts[0] + parts[1]) + (parts[2] + parts[3])

    def pack_ends(ref, e, kind):
        plane, tile = faces[e][0], faces[e][1]
        for px in (0, 1):
            plane[px, kind] = ref[31 * px]
            tile[px, kind] = gather_columns(
                [(56 * px + b, ref[31 * px, 8 * b : 8 * b + 8, :]) for b in range(8)]
            )

    def send_ends(e):
        plane, tile, _, _, _, r_plane, r_xy, r_xz, r_xyz, _, _, _ = faces[e]
        for px in (0, 1):
            sx = 2 * px - 1
            send(plane.at[px], r_plane.at[px], e, "ends", (sx, 0, 0))
            for py in (0, 1):
                send(
                    plane.at[px, :, pl.ds(56 * py, 8)],
                    r_xy.at[px, py],
                    e,
                    "ends",
                    (sx, 2 * py - 1, 0),
                )
            for pz in (0, 1):
                sz = 2 * pz - 1
                send(tile.at[px], r_xz.at[px, pz], e, "ends", (sx, 0, sz))
                for py in (0, 1):
                    send(tile.at[px], r_xyz.at[px, py, pz], e, "ends", (sx, 2 * py - 1, sz))

    def pack_rest(ref, e, kind):
        rows, cols, lines = faces[e][2:5]
        for n in range(32):
            rows[0, kind, n : n + 1, :] = ref[n, 0:1, :]
            rows[1, kind, n : n + 1, :] = ref[n, 63:64, :]

        @pl.loop(0, 4)
        def _(a):
            cols[a, kind] = gather_columns(
                [
                    (8 * i + b, ref[8 * a + i, 8 * b : 8 * b + 8, :])
                    for i in range(8)
                    for b in range(8)
                ]
            )

        low, high = zero, zero
        for a in range(4):
            low = jnp.where(sub == a, jnp.broadcast_to(cols[a, kind, 0:1, :], (8, 128)), low)
            high = jnp.where(sub == a, jnp.broadcast_to(cols[a, kind, 7:8, :], (8, 128)), high)
        lines[0, kind] = low
        lines[1, kind] = high

    def send_rest(e):
        rows, cols, lines = faces[e][2:5]
        r_rows, r_cols, r_yz = faces[e][9:12]
        for pz in (0, 1):
            sz = 2 * pz - 1
            send(cols, r_cols.at[pz], e, "rest", (0, 0, sz))
            for py in (0, 1):
                send(lines.at[py], r_yz.at[py, pz], e, "rest", (0, 2 * py - 1, sz))
        for py in (0, 1):
            send(rows.at[py], r_rows.at[py], e, "rest", (0, 2 * py - 1, 0))

    def across_azimuth(t, py):
        t = pltpu.roll(t, 114 if py else 14, 1)
        return jnp.where((lane % 16 < 2) if py else (lane % 16 >= 14), t, zero)

    def swap(q):
        return jnp.where(even, pltpu.roll(q, 127, 1), pltpu.roll(q, 1, 1)) * keep

    def add_rest(ref, e, kind):
        r_rows, r_cols, r_yz = faces[e][9:12]
        for n in range(32):
            ref[n, 0:1, :] = ref[n, 0:1, :] + r_rows[1, kind, n : n + 1, :]
            ref[n, 63:64, :] = ref[n, 63:64, :] + r_rows[0, kind, n : n + 1, :]
        across = [
            across_azimuth(jnp.where(even, r_yz[py, 1, kind], r_yz[py, 0, kind]), py)
            for py in (0, 1)
        ]
        for a in range(4):
            q = jnp.where(even, r_cols[1, a, kind], r_cols[0, a, kind])
            q = q + jnp.where(sub == 0, jnp.broadcast_to(across[1][a : a + 1, :], (8, 128)), zero)
            q = q + jnp.where(sub == 7, jnp.broadcast_to(across[0][a : a + 1, :], (8, 128)), zero)
            xcol[kind, a] = swap(q)

    def add_ends(ref, e, kind):
        r_plane, r_xy, r_xz, r_xyz = faces[e][5:9]
        for px in (0, 1):
            n, a = (0, 0) if px else (31, 3)
            ref[n] = ref[n] + r_plane[px, kind]
            for py in (0, 1):
                row, got = (0, 7) if py else (63, 0)
                ref[n, row : row + 1, :] = (
                    ref[n, row : row + 1, :] + r_xy[px, py, kind, got : got + 1, :]
                )
            q = jnp.where(even, r_xz[px, 1, kind], r_xz[px, 0, kind])
            for py in (0, 1):
                c = jnp.where(even, r_xyz[px, py, 1, kind], r_xyz[px, py, 0, kind])
                c = pltpu.roll(across_azimuth(c, py), 1 if py else 7, 0)
                q = q + jnp.where(sub == (0 if py else 7), c, zero)
            if px:
                q = jnp.where(lane < 16, pltpu.roll(q, 16, 1), zero)
            else:
                q = jnp.where(lane >= 112, pltpu.roll(q, 112, 1), zero)
            xcol[kind, a] = xcol[kind, a] + swap(q)

    def total(ref, x, n, i, b):
        spot = 8 * i + b
        return ref[n, 8 * b : 8 * b + 8, :] + jnp.where(
            edge, pltpu.roll(x, 127 - 2 * spot, 1), zero
        )

    def convect(src, a):
        block = src[pl.ds(8 * a, 8)].reshape(512, 128)
        high = block.astype(BF16)
        low = (block - high.astype(F32)).astype(BF16)
        both = jnp.dot(
            jnp.concatenate([high, low], axis=1), tab[...], preferred_element_type=F32
        )
        radial[...] = (both[:, :128] + both[:, 128:]).reshape(8, 64, 128)
        for b in range(8):
            part = slice(8 * b, 8 * b + 8)
            f = [src[8 * a + i, part, :] for i in range(8)]
            plus = [f[p] + f[7 - p] for p in range(4)]
            minus = [f[p] - f[7 - p] for p in range(4)]
            axial = [None] * 8
            for i in range(4):
                x = y = None
                for p in range(4):
                    alpha = float((DERIV[i, p] + DERIV[i, 7 - p]) / 2)
                    beta = float((DERIV[i, p] - DERIV[i, 7 - p]) / 2)
                    x = alpha * plus[p] if x is None else x + alpha * plus[p]
                    y = beta * minus[p] if y is None else y + beta * minus[p]
                axial[i] = x + y
                axial[7 - i] = y - x
            for i in range(8):
                n = 8 * a + i
                turned = azi[0] * f[i]
                for d in range(1, 8):
                    turned = turned + azi[d] * pltpu.roll(f[i], 8 - d, 0)
                c = (
                    vel[0, n, part, :] * axial[i]
                    + vel[1, n, part, :] * turned
                    + vel[2, n, part, :] * radial[i, part, :]
                )
                g_ref[n, part, :] = lane_pairs(mass[n, part, :] * c)
        pair_azimuth(g_ref, a)

    load_mass.wait()

    @pl.loop(0, 4)
    def _(a):
        for i in range(8):
            for b in range(8):
                n, part = 8 * a + i, slice(8 * b, 8 * b + 8)
                winv[n, part, :] = lane_pairs(mass[n, part, :])
        pair_azimuth(winv, a)

    pair_axial(winv)
    pack_ends(winv, 0, 1)
    pack_rest(winv, 0, 1)

    load_fld.wait()
    load_tab.wait()
    load_azi.wait()

    @twice
    def stage_one(a):
        part = pl.ds(pl.multiple_of(8 * a, 8), 8)
        pltpu.make_async_copy(vel_h.at[:, part], vel.at[:, part], vel_sem.at[a]).wait()
        convect(fld, a)

    stage_one("ends")
    pack_ends(g_ref, 0, 0)
    pl.semaphore_wait(barrier, 26 + n_cam - 3)
    send_ends(0)
    stage_one("middle")
    pair_axial(g_ref)
    pack_rest(g_ref, 0, 0)
    send_rest(0)

    load_blk.wait()
    blk_copies = []
    for d in range(1, n_cam):
        copy = pltpu.make_async_remote_copy(
            src_ref=blk,
            dst_ref=blk_recv.at[d],
            send_sem=b_send_sem.at[d],
            recv_sem=b_recv_sem.at[d],
            device_id=peer(0, 0, d),
            device_id_type=pl.DeviceIdType.MESH,
        )
        copy.start()
        blk_copies.append(copy)

    load_cut.wait()
    load_wts.wait()

    @pl.loop(0, 8)
    def _(m):
        wide[...] = wts[m].astype(F32)
        for k in range(8):
            wts_p[m, 64 * k : 64 * k + 64, :] = wide[pl.ds(k, 64, stride=8), :].astype(BF16)
        chosen = jnp.broadcast_to(cut[pl.ds(m, 1), :].astype(F32), (128, 128)).T
        place = lax.broadcasted_iota(jnp.int32, (128, 128), 1).astype(F32)
        for q in range(4):
            cut_hot[m, :, 128 * q : 128 * q + 128] = jnp.where(
                chosen == place + 128.0 * q, 1.0, 0.0
            ).astype(BF16)

    @twice
    def stage_two(a):
        x, y = xcol[0, a], xcol[1, a]
        for i in range(8):
            for b in range(8):
                n, part = 8 * a + i, slice(8 * b, 8 * b + 8)
                factor = -STEP / total(winv, y, n, i, b)
                winv[n, part, :] = factor
                first[n, part, :] = fld[n, part, :] + factor * total(g_ref, x, n, i, b)
        convect(first, a)

    wait_for(0, "rest")
    add_rest(winv, 0, 1)
    add_rest(g_ref, 0, 0)
    stage_two("middle")
    wait_for(0, "ends")
    add_ends(winv, 0, 1)
    add_ends(g_ref, 0, 0)
    stage_two("ends")
    pack_ends(g_ref, 1, 0)
    send_ends(1)
    pair_axial(g_ref)
    pack_rest(g_ref, 1, 0)
    send_rest(1)

    for copy in blk_copies:
        copy.wait_recv()
    for d in range(n_cam):
        for t in range(2):
            if d == 0:
                ids = blk[pl.ds(2 * cam + t, 1), :]
            else:
                ids = blk_recv[d, pl.ds(2 * cam + t, 1), :]
            ids = jnp.broadcast_to(ids, (128, 128))
            for h in range(8):
                block_id = lax.broadcasted_iota(jnp.int32, (128, 128), 0) + 128 * h
                img_hot[t, 128 * h : 128 * h + 128, 128 * d : 128 * d + 128] = jnp.where(
                    ids == block_id, 1.0, 0.0
                ).astype(BF16)

    wide_lane = lax.broadcasted_iota(jnp.int32, (64, 128), 1)
    row64 = lax.broadcasted_iota(jnp.int32, (64, 128), 0)
    select = jnp.where(
        (wide_lane // 8 == row64 % 16) & ((wide_lane % 8) // 2 == row64 // 16), 1.0, 0.0
    ).astype(BF16)

    @twice
    def finish(a):
        x = xcol[0, a]
        for i in range(8):
            for b in range(8):
                n, part = 8 * a + i, slice(8 * b, 8 * b + 8)
                second = first[n, part, :] + winv[n, part, :] * total(g_ref, x, n, i, b)
                adv[n, part, :] = 0.5 * (fld[n, part, :] + second)
        for b in range(0, 8, 2):
            pieces = []
            for c in (b, b + 1):
                block = adv[pl.ds(8 * a, 8), 8 * c : 8 * c + 8, :].reshape(64, 128)
                pieces.append(jnp.where(wide_lane % 2 == 0, block, 0.0).astype(BF16))
                pieces.append(jnp.where(wide_lane % 2 == 1, block, 0.0).astype(BF16))
            out = lax.dot_general(
                select,
                jnp.concatenate(pieces, axis=0),
                (((1,), (1,)), ((), ())),
                preferred_element_type=F32,
            ).astype(BF16)
            for c in (0, 1):
                at = pl.multiple_of(128 * a + 16 * (b + c), 16)
                for h in range(4):
                    elems[pl.ds(at, 16), 128 * h : 128 * h + 128] = out[
                        16 * h : 16 * h + 16, 128 * c : 128 * c + 128
                    ]

    wait_for(1, "rest")
    add_rest(g_ref, 1, 0)
    finish("middle")
    wait_for(1, "ends")
    add_ends(g_ref, 1, 0)
    finish("ends")

    v_copies = []
    for d in sorted(range(1, n_cam), key=lambda d: -min(d, n_cam - d)) + [0]:
        q = lax.rem(cam + d, n_cam)
        for t in range(2):
            m = 2 * q + t
            picked = jnp.dot(cut_hot[m], elems[...], preferred_element_type=F32).astype(BF16)
            value = jnp.dot(picked, wts_p[m], preferred_element_type=F32).astype(BF16)
            if d:
                v_send[d, t] = value
            else:
                v_recv[0, t] = value
        if d:
            copy = pltpu.make_async_remote_copy(
                src_ref=v_send.at[d],
                dst_ref=v_recv.at[d],
                send_sem=v_send_sem.at[d],
                recv_sem=v_recv_sem.at[d],
                device_id=peer(0, 0, d),
                device_id_type=pl.DeviceIdType.MESH,
            )
            copy.start()
            v_copies.append(copy)

    for copy in copies + blk_copies:
        copy.wait_send()
    for copy in v_copies:
        copy.wait_recv()
    for copy in v_copies:
        copy.wait_send()


def write_kernel(adv, values, img_hot, adv_h, img_h, img, sem):
    result = pltpu.make_async_copy(adv, adv_h, sem.at[0])
    result.start()
    n_cam = values.shape[0]
    copies = []
    for t in range(2):
        slots = jnp.concatenate([values[d, t] for d in range(n_cam)], axis=0)
        for h in range(2):
            part = pl.ds(h * (NBLK // 2), NBLK // 2)
            img[t, part] = jnp.dot(img_hot[t, part], slots, preferred_element_type=F32)
            copy = pltpu.make_async_copy(
                img.at[t, part], img_h.at[t, part], sem.at[1 + 2 * t + h]
            )
            copy.start()
            copies.append(copy)
    for copy in copies:
        copy.wait()
    result.wait()


def face_buffers(kinds):
    shapes = [
        (2, kinds, 64, 128),
        (2, kinds, 8, 128),
        (2, kinds, 32, 128),
        (4, kinds, 8, 128),
        (2, kinds, 8, 128),
        (2, kinds, 64, 128),
        (2, 2, kinds, 8, 128),
        (2, 2, kinds, 8, 128),
        (2, 2, 2, kinds, 8, 128),
        (2, kinds, 32, 128),
        (2, 4, kinds, 8, 128),
        (2, 2, kinds, 8, 128),
    ]
    return tuple(pltpu.VMEM(shape, F32) for shape in shapes)


def per_device(sizes, scalar, velocity, lumped_mass, pixel_weights, cut_element, pixel_block):
    n_cam = sizes[0]
    flat = (32, 64, 128)
    hbm = pl.BlockSpec(memory_space=pltpu.HBM)
    big = pltpu.VMEM(flat, F32)
    dma = pltpu.SemaphoreType.DMA
    on_chip = pl.BlockSpec(memory_space=pltpu.VMEM)
    outputs = (
        pltpu.VMEM(flat, F32),
        pltpu.VMEM((n_cam, 2, 128, 128), BF16),
        pltpu.VMEM((2, NBLK, 128 * n_cam), BF16),
    )
    operands = (
        scalar.reshape(flat),
        velocity.reshape((3,) + flat),
        lumped_mass.reshape(flat),
        pixel_weights,
        cut_element,
        pixel_block,
        jnp.asarray(radial_matrix()),
        jnp.asarray(azimuth_table()),
    )
    results = pl.pallas_call(
        functools.partial(kernel, sizes),
        out_shape=outputs,
        in_specs=[hbm] * 8,
        out_specs=(on_chip,) * 3,
        scratch_shapes=[
            big,
            pltpu.VMEM((3,) + flat, F32),
            big,
            pltpu.VMEM((8, 512, 128), BF16),
            pltpu.VMEM((8, 128), jnp.int32),
            pltpu.VMEM((8, 128), jnp.int32),
            pltpu.VMEM((256, 256), BF16),
            pltpu.VMEM((8, 8, 128), F32),
            big,
            big,
            big,
            pltpu.VMEM((8, 64, 128), F32),
            face_buffers(2),
            face_buffers(1),
            pltpu.VMEM((2, 4, 8, 128), F32),
            pltpu.VMEM((512, 128), F32),
            pltpu.VMEM((8, 512, 128), BF16),
            pltpu.VMEM((8, 128, 512), BF16),
            pltpu.VMEM((512, 512), BF16),
            pltpu.VMEM((n_cam, 2, 128, 128), BF16),
            pltpu.VMEM((n_cam, 8, 128), jnp.int32),
            dma((7,)),
            dma((4,)),
            dma((52,)),
            dma((52,)),
            dma((n_cam,)),
            dma((n_cam,)),
            dma((n_cam,)),
            dma((n_cam,)),
        ],
        compiler_params=pltpu.CompilerParams(
            collective_id=0, has_side_effects=True, vmem_limit_bytes=40 * 1024 * 1024
        ),
    )(*[pltpu.with_memory_space_constraint(x, pltpu.HBM) for x in operands])
    advected, images = pl.pallas_call(
        write_kernel,
        out_shape=(
            jax.ShapeDtypeStruct(flat, F32),
            jax.ShapeDtypeStruct((2, NBLK, 128), F32),
        ),
        in_specs=[on_chip] * 3,
        out_specs=(hbm, hbm),
        scratch_shapes=[pltpu.VMEM((2, NBLK, 128), F32), dma((5,))],
        compiler_params=pltpu.CompilerParams(vmem_limit_bytes=16 * 1024 * 1024),
    )(*[pltpu.with_memory_space_constraint(x, pltpu.VMEM) for x in results])
    return advected.reshape(scalar.shape), images


def solution(mesh):
    sizes = tuple(mesh.shape[name] for name in ("cam", "ex", "ey"))
    placed = (
        P("ex", None, "ey", None, "cam"),
        P(None, "ex", None, "ey", None, "cam"),
        P("ex", None, "ey", None, "cam"),
        P(),
        P(None, ("cam", "ex", "ey")),
        P(None, ("cam", "ex", "ey")),
    )
    return jax.shard_map(
        functools.partial(per_device, sizes),
        mesh=mesh,
        in_specs=placed,
        out_specs=(P("ex", None, "ey", None, "cam"), P("cam", ("ex", "ey"), None)),
        check_vma=False,
    )
```

```python
import functools

import jax
import jax.numpy as jnp
import ml_dtypes
import numpy as np
from jax import lax
from jax.experimental import pallas as pl
from jax.experimental.pallas import tpu as pltpu
from jax.sharding import PartitionSpec as P

NBLK = 1024
STEP = 0.01
F32 = jnp.float32
BF16 = jnp.bfloat16


def legendre_seven(points):
    previous = points * 0.0 + 1.0
    current = points * 1.0
    for order in range(1, 7):
        following = ((2 * order + 1) * points * current - order * previous) / (order + 1)
        previous = current
        current = following
    return current


def gll_derivative():
    degree = 7
    gll_nodes = np.array(
        [
            -1.0,
            -0.8717401485096066,
            -0.5917001814331423,
            -0.2092992179024789,
            0.2092992179024789,
            0.5917001814331423,
            0.8717401485096066,
            1.0,
        ]
    )
    values = legendre_seven(gll_nodes)
    derivative = np.zeros((degree + 1, degree + 1))
    for target in range(degree + 1):
        for source in range(degree + 1):
            if target != source:
                derivative[target, source] = values[target] / (
                    values[source] * (gll_nodes[target] - gll_nodes[source])
                )
    derivative[0, 0] = -degree * (degree + 1) / 4.0
    derivative[degree, degree] = degree * (degree + 1) / 4.0
    return derivative


DERIV = gll_derivative()


def radial_matrix():
    table = np.kron(np.eye(16), DERIV.T).astype(np.float32)
    high = table.astype(ml_dtypes.bfloat16)
    low = (table - high.astype(np.float32)).astype(ml_dtypes.bfloat16)
    return np.block([[high, low], [high, np.zeros_like(low)]])


def azimuth_table():
    rows = np.arange(8)
    shifts = np.stack([DERIV[rows, (rows + d) % 8] for d in range(8)])
    return np.broadcast_to(shifts[:, :, None], (8, 8, 128)).astype(np.float32)


AXIAL = (1, 2, 0, 3)

SIGNS = [
    (sx, sy, sz)
    for sx in (-1, 0, 1)
    for sy in (-1, 0, 1)
    for sz in (-1, 0, 1)
    if (sx, sy, sz) != (0, 0, 0)
]


def kernel(
    sizes,
    scalar_h,
    vel_h,
    mass_h,
    wts_h,
    cut_h,
    blk_h,
    tab_h,
    azi_h,
    adv,
    v_recv,
    img_hot,
    fld,
    vel,
    mass,
    wts,
    cut,
    blk,
    tab,
    azi,
    g_ref,
    first,
    winv,
    radial,
    faces_one,
    faces_two,
    xcol,
    wide,
    wts_p,
    cut_hot,
    elems,
    v_send,
    blk_recv,
    in_sem,
    vel_sem,
    send_sem,
    recv_sem,
    v_send_sem,
    v_recv_sem,
    b_send_sem,
    b_recv_sem,
):
    n_cam, n_ex, n_ey = sizes
    cam, ex, ey = lax.axis_index("cam"), lax.axis_index("ex"), lax.axis_index("ey")
    faces = (faces_one, faces_two)

    def peer(sx, sy, sz):
        return {
            "cam": lax.rem(cam + (sz + n_cam), n_cam),
            "ex": lax.rem(ex + (sx + n_ex), n_ex),
            "ey": lax.rem(ey + (sy + n_ey), n_ey),
        }

    def load(src, dst, sem):
        copy = pltpu.make_async_copy(src, dst, sem)
        copy.start()
        return copy

    load_mass = load(mass_h, mass, in_sem.at[0])
    load_fld = load(scalar_h, fld, in_sem.at[1])
    load_tab = load(tab_h, tab, in_sem.at[2])
    load_azi = load(azi_h, azi, in_sem.at[3])
    for a in (0, 3, 1, 2):
        load(vel_h.at[:, pl.ds(8 * a, 8)], vel.at[:, pl.ds(8 * a, 8)], vel_sem.at[a])
    load_blk = load(blk_h, blk, in_sem.at[4])
    load_cut = load(cut_h, cut, in_sem.at[5])
    load_wts = load(wts_h, wts, in_sem.at[6])

    peers = {s: peer(*s) for s in SIGNS}
    barrier = pltpu.get_barrier_semaphore()
    for s in sorted(SIGNS, key=lambda s: -abs(s[0])):
        pl.semaphore_signal(barrier, inc=1, device_id=peers[s], device_id_type=pl.DeviceIdType.MESH)
    for d in range(2, n_cam - 1):
        pl.semaphore_signal(
            barrier, inc=1, device_id=peer(0, 0, d), device_id_type=pl.DeviceIdType.MESH
        )

    lane = lax.broadcasted_iota(jnp.int32, (8, 128), 1)
    sub = lax.broadcasted_iota(jnp.int32, (8, 128), 0)
    even = lane % 2 == 0
    take_next = (lane % 8 == 7) & (lane != 127)
    take_prev = (lane % 8 == 0) & (lane != 0)
    edge = (lane == 0) | (lane == 127)
    zero = jnp.zeros((8, 128), F32)
    has_upper, has_lower = cam < n_cam - 1, cam > 0
    from_upper = jnp.where(has_upper, 1.0, 0.0).astype(F32)
    from_lower = jnp.where(has_lower, 1.0, 0.0).astype(F32)
    keep = jnp.where(even, jnp.full((8, 128), from_upper), jnp.full((8, 128), from_lower)) > 0.5

    def lane_pairs(g):
        return (
            g
            + jnp.where(take_next, pltpu.roll(g, 127, 1), zero)
            + jnp.where(take_prev, pltpu.roll(g, 1, 1), zero)
        )

    def twice(body):
        def outer(which):
            @pl.loop(0, 2)
            def _(t):
                body(3 * t if which == "ends" else 1 + t)

        return outer

    copies = []

    def send(src, dst, e, group, slot, s):
        copy = pltpu.make_async_remote_copy(
            src_ref=src,
            dst_ref=dst,
            send_sem=send_sem.at[slot],
            recv_sem=recv_sem.at[slot],
            device_id=peers[s],
            device_id_type=pl.DeviceIdType.MESH,
        )
        copies.append((e, group, s[2], copy))
        if s[2] == 0:
            copy.start()

    def toward(sz, body):
        pl.when(has_upper if sz > 0 else has_lower)(body)

    def launch(sz, body):
        first_new = len(copies)
        body()
        chosen = [copy for _, _, _, copy in copies[first_new:]]

        def start():
            for copy in chosen:
                copy.start()

        toward(sz, start)

    def wait_all(e, groups, received):
        for sz in (0, -1, 1):
            chosen = [c for at, group, z, c in copies if at == e and group in groups and z == sz]

            def body(chosen=chosen):
                for copy in chosen:
                    if received:
                        copy.wait_recv()
                    else:
                        copy.wait_send()

            if sz == 0:
                body()
            else:
                toward(-sz if received else sz, body)

    def pair_azimuth(ref, a):
        for i in range(8):
            n = 8 * a + i
            both = ref[n, pl.ds(7, 7, stride=8), :] + ref[n, pl.ds(8, 7, stride=8), :]
            ref[n, pl.ds(7, 7, stride=8), :] = both
            ref[n, pl.ds(8, 7, stride=8), :] = both

    def pair_axial(ref):
        for a in range(3):
            both = ref[8 * a + 7] + ref[8 * a + 8]
            ref[8 * a + 7] = both
            ref[8 * a + 8] = both

    def gather_columns(pieces):
        parts = [zero] * 4
        for at, (spot, piece) in enumerate(pieces):
            here = (lane == 2 * spot) | (lane == 2 * spot + 1)
            parts[at % 4] = jnp.where(here, pltpu.roll(piece, 2 * spot + 1, 1), parts[at % 4])
        return (parts[0] + parts[1]) + (parts[2] + parts[3])

    def pair_plane(plane):
        both = plane[pl.ds(7, 7, stride=8), :] + plane[pl.ds(8, 7, stride=8), :]
        plane[pl.ds(7, 7, stride=8), :] = both
        plane[pl.ds(8, 7, stride=8), :] = both

    def pack_ends(e, kind):
        plane, tile = faces[e][0], faces[e][1]
        for px in (0, 1):
            tile[px, kind] = gather_columns(
                [(56 * px + b, plane[px, kind, 8 * b : 8 * b + 8, :]) for b in range(8)]
            )

    def send_ends(e):
        plane, tile, _, _, _, r_plane, r_xy, r_xz, r_xyz, _, _, _ = faces[e]
        base = 30 * e
        for px in (0, 1):
            sx = 2 * px - 1
            send(plane.at[px], r_plane.at[px], e, "ends", base + px, (sx, 0, 0))
            for py in (0, 1):
                send(
                    plane.at[px, :, pl.ds(56 * py, 8)],
                    r_xy.at[px, py],
                    e,
                    "ends",
                    base + 2 + 2 * px + py,
                    (sx, 2 * py - 1, 0),
                )
        for pz in (0, 1):
            sz = 2 * pz - 1

            def body(pz=pz, sz=sz):
                for px in (0, 1):
                    sx = 2 * px - 1
                    slot = base + 6 + 6 * pz + 3 * px
                    send(tile.at[px], r_xz.at[px, pz], e, "ends", slot, (sx, 0, sz))
                    for py in (0, 1):
                        send(
                            tile.at[px],
                            r_xyz.at[px, py, pz],
                            e,
                            "ends",
                            slot + 1 + py,
                            (sx, 2 * py - 1, sz),
                        )

            launch(sz, body)

    def pack_columns(ref, e, kind, half):
        cols = faces[e][3]

        @pl.loop(0, 2)
        def _(t):
            a = 3 * t if half else 1 + t
            cols[2 * half + t, kind] = gather_columns(
                [
                    (8 * i + b, ref[8 * a + i, 8 * b : 8 * b + 8, :])
                    for i in range(8)
                    for b in range(8)
                ]
            )

    def send_columns(e, half):
        cols, r_cols = faces[e][3], faces[e][10]
        for pz in (0, 1):
            sz = 2 * pz - 1

            def body(pz=pz, sz=sz):
                part = pl.ds(2 * half, 2)
                send(
                    cols.at[part],
                    r_cols.at[pz, part],
                    e,
                    "rest",
                    30 * e + 18 + 2 * pz + half,
                    (0, 0, sz),
                )

            launch(sz, body)

    def pack_lines(e, kind):
        cols, lines = faces[e][3], faces[e][4]
        low, high = zero, zero
        for at in range(4):
            low = jnp.where(sub == at, jnp.broadcast_to(cols[at, kind, 0:1, :], (8, 128)), low)
            high = jnp.where(sub == at, jnp.broadcast_to(cols[at, kind, 7:8, :], (8, 128)), high)
        lines[0, kind] = low
        lines[1, kind] = high

    def send_lines(e):
        lines, r_yz = faces[e][4], faces[e][11]
        for pz in (0, 1):
            sz = 2 * pz - 1

            def body(pz=pz, sz=sz):
                for py in (0, 1):
                    send(
                        lines.at[py],
                        r_yz.at[py, pz],
                        e,
                        "rest",
                        30 * e + 22 + 2 * pz + py,
                        (0, 2 * py - 1, sz),
                    )

            launch(sz, body)

    def pack_rows(ref, e, kind):
        rows = faces[e][2]
        for n in range(32):
            rows[0, kind, n : n + 1, :] = ref[n, 0:1, :]
            rows[1, kind, n : n + 1, :] = ref[n, 63:64, :]

    def send_rows(e):
        rows, r_rows = faces[e][2], faces[e][9]
        for py in (0, 1):
            send(rows.at[py], r_rows.at[py], e, "rest", 30 * e + 26 + py, (0, 2 * py - 1, 0))

    def across_azimuth(t, py):
        t = pltpu.roll(t, 114 if py else 14, 1)
        return jnp.where((lane % 16 < 2) if py else (lane % 16 >= 14), t, zero)

    def swap(q):
        return jnp.where(keep, jnp.where(even, pltpu.roll(q, 127, 1), pltpu.roll(q, 1, 1)), zero)

    def add_rest(ref, e, kind):
        r_rows, r_cols, r_yz = faces[e][9:12]
        for n in range(32):
            after, before = r_rows[1, kind, n : n + 1, :], r_rows[0, kind, n : n + 1, :]
            if 0 < n < 31 and n % 8 in (0, 7):
                other = n + 1 if n % 8 == 7 else n - 1
                after = after + r_rows[1, kind, other : other + 1, :]
                before = before + r_rows[0, kind, other : other + 1, :]
            ref[n, 0:1, :] = ref[n, 0:1, :] + after
            ref[n, 63:64, :] = ref[n, 63:64, :] + before
        across = [
            across_azimuth(jnp.where(even, r_yz[py, 1, kind], r_yz[py, 0, kind]), py)
            for py in (0, 1)
        ]
        found = [None] * 4
        for at, a in enumerate(AXIAL):
            q = jnp.where(even, r_cols[1, at, kind], r_cols[0, at, kind])
            q = q + jnp.where(sub == 0, jnp.broadcast_to(across[1][at : at + 1, :], (8, 128)), zero)
            q = q + jnp.where(sub == 7, jnp.broadcast_to(across[0][at : at + 1, :], (8, 128)), zero)
            found[a] = q
        for a in range(4):
            q = found[a]
            if a < 3:
                q = q + jnp.where(lane >= 112, pltpu.roll(found[a + 1], 112, 1), zero)
            if a > 0:
                q = q + jnp.where(lane < 16, pltpu.roll(found[a - 1], 16, 1), zero)
            xcol[kind, a] = swap(q)

    def add_ends(ref, e, kind):
        r_plane, r_xy, r_xz, r_xyz = faces[e][5:9]
        for px in (0, 1):
            n, a = (0, 0) if px else (31, 3)
            ref[n] = ref[n] + r_plane[px, kind]
            for py in (0, 1):
                row, got = (0, 7) if py else (63, 0)
                ref[n, row : row + 1, :] = (
                    ref[n, row : row + 1, :] + r_xy[px, py, kind, got : got + 1, :]
                )
            q = jnp.where(even, r_xz[px, 1, kind], r_xz[px, 0, kind])
            for py in (0, 1):
                c = jnp.where(even, r_xyz[px, py, 1, kind], r_xyz[px, py, 0, kind])
                c = pltpu.roll(across_azimuth(c, py), 1 if py else 7, 0)
                q = q + jnp.where(sub == (0 if py else 7), c, zero)
            if px:
                q = jnp.where(lane < 16, pltpu.roll(q, 16, 1), zero)
            else:
                q = jnp.where(lane >= 112, pltpu.roll(q, 112, 1), zero)
            xcol[kind, a] = xcol[kind, a] + swap(q)

    def total(ref, x, n, i, b):
        spot = 8 * i + b
        return ref[n, 8 * b : 8 * b + 8, :] + jnp.where(
            edge, pltpu.roll(x, 127 - 2 * spot, 1), zero
        )

    def along_radius(block):
        high = block.astype(BF16)
        low = (block - high.astype(F32)).astype(BF16)
        both = jnp.dot(
            jnp.concatenate([high, low], axis=1), tab[...], preferred_element_type=F32
        )
        return both[:, :128] + both[:, 128:]

    def along_azimuth(f):
        turned = azi[0] * f
        for d in range(1, 8):
            turned = turned + azi[d] * pltpu.roll(f, 8 - d, 0)
        return turned

    def convect_plane(src, e, px):
        n, i = 31 * px, 7 * px
        plane = faces[e][0].at[px, 0]
        turning = along_radius(src[n])
        for b in range(8):
            part = slice(8 * b, 8 * b + 8)
            axial = None
            for p in range(8):
                term = float(DERIV[i, p]) * src[n - i + p, part, :]
                axial = term if axial is None else axial + term
            c = (
                vel[0, n, part, :] * axial
                + vel[1, n, part, :] * along_azimuth(src[n, part, :])
                + vel[2, n, part, :] * turning[part, :]
            )
            plane[part, :] = lane_pairs(mass[n, part, :] * c)
        pair_plane(plane)

    def convect(src, a):
        radial[...] = along_radius(src[pl.ds(8 * a, 8)].reshape(512, 128)).reshape(8, 64, 128)
        for b in range(8):
            part = slice(8 * b, 8 * b + 8)
            f = [src[8 * a + i, part, :] for i in range(8)]
            plus = [f[p] + f[7 - p] for p in range(4)]
            minus = [f[p] - f[7 - p] for p in range(4)]
            axial = [None] * 8
            for i in range(4):
                x = y = None
                for p in range(4):
                    alpha = float((DERIV[i, p] + DERIV[i, 7 - p]) / 2)
                    beta = float((DERIV[i, p] - DERIV[i, 7 - p]) / 2)
                    x = alpha * plus[p] if x is None else x + alpha * plus[p]
                    y = beta * minus[p] if y is None else y + beta * minus[p]
                axial[i] = x + y
                axial[7 - i] = y - x
            for i in range(8):
                n = 8 * a + i
                c = (
                    vel[0, n, part, :] * axial[i]
                    + vel[1, n, part, :] * along_azimuth(f[i])
                    + vel[2, n, part, :] * radial[i, part, :]
                )
                g_ref[n, part, :] = lane_pairs(mass[n, part, :] * c)
        pair_azimuth(g_ref, a)

    for pz in (0, 1):

        @pl.when(jnp.logical_not(has_lower if pz else has_upper))
        def _(pz=pz):
            for _, _, _, _, _, _, _, r_xz, r_xyz, _, r_cols, r_yz in faces:
                r_cols[pz] = jnp.zeros(r_cols.shape[1:], F32)
                for px in (0, 1):
                    r_xz[px, pz] = jnp.zeros(r_xz.shape[2:], F32)
                    r_yz[px, pz] = jnp.zeros(r_yz.shape[2:], F32)
                    for py in (0, 1):
                        r_xyz[px, py, pz] = jnp.zeros(r_xyz.shape[3:], F32)

    load_mass.wait()

    @pl.loop(0, 4)
    def _(a):
        for i in range(8):
            for b in range(8):
                n, part = 8 * a + i, slice(8 * b, 8 * b + 8)
                winv[n, part, :] = lane_pairs(mass[n, part, :])
        pair_azimuth(winv, a)

    for px in (0, 1):
        faces[0][0][px, 1] = winv[31 * px]
    pack_ends(0, 1)
    for half in (0, 1):
        pack_columns(winv, 0, 1, half)
    pack_lines(0, 1)
    pack_rows(winv, 0, 1)
    pair_axial(winv)

    load_fld.wait()
    load_tab.wait()
    load_azi.wait()

    def wait_velocity(a):
        part = pl.ds(8 * a, 8)
        pltpu.make_async_copy(vel_h.at[:, part], vel.at[:, part], vel_sem.at[a]).wait()

    for px in (0, 1):
        wait_velocity(3 * px)
        convect_plane(fld, 0, px)
    pack_ends(0, 0)
    pl.semaphore_wait(barrier, 26 + n_cam - 3)
    send_ends(0)
    wait_velocity(1)
    wait_velocity(2)

    @twice
    def stage_one(a):
        convect(fld, a)

    stage_one("middle")
    pack_columns(g_ref, 0, 0, 0)
    send_columns(0, 0)
    stage_one("ends")
    pack_columns(g_ref, 0, 0, 1)
    send_columns(0, 1)
    pack_lines(0, 0)
    send_lines(0)
    pack_rows(g_ref, 0, 0)
    send_rows(0)
    pair_axial(g_ref)

    load_blk.wait()
    blk_copies = []
    for d in range(1, n_cam):
        copy = pltpu.make_async_remote_copy(
            src_ref=blk,
            dst_ref=blk_recv.at[d],
            send_sem=b_send_sem.at[d],
            recv_sem=b_recv_sem.at[d],
            device_id=peer(0, 0, d),
            device_id_type=pl.DeviceIdType.MESH,
        )
        copy.start()
        blk_copies.append(copy)

    load_cut.wait()
    load_wts.wait()

    @pl.loop(0, 8)
    def _(m):
        wide[...] = wts[m].astype(F32)
        for k in range(8):
            wts_p[m, 64 * k : 64 * k + 64, :] = wide[pl.ds(k, 64, stride=8), :].astype(BF16)
        chosen = jnp.broadcast_to(cut[pl.ds(m, 1), :].astype(F32), (128, 128)).T
        place = lax.broadcasted_iota(jnp.int32, (128, 128), 1).astype(F32)
        for q in range(4):
            cut_hot[m // 2, pl.ds(128 * (m % 2), 128), 128 * q : 128 * q + 128] = jnp.where(
                chosen == place + 128.0 * q, 1.0, 0.0
            ).astype(BF16)

    @twice
    def step_one(a):
        x, y = xcol[0, a], xcol[1, a]
        for i in range(8):
            for b in range(8):
                n, part = 8 * a + i, slice(8 * b, 8 * b + 8)
                factor = -STEP / total(winv, y, n, i, b)
                winv[n, part, :] = factor
                first[n, part, :] = fld[n, part, :] + factor * total(g_ref, x, n, i, b)

    @twice
    def stage_two(a):
        convect(first, a)

    wait_all(0, ("rest",), True)
    add_rest(winv, 0, 1)
    add_rest(g_ref, 0, 0)
    step_one("middle")
    stage_two("middle")
    pack_columns(g_ref, 1, 0, 0)
    send_columns(1, 0)
    wait_all(0, ("ends",), True)
    add_ends(winv, 0, 1)
    add_ends(g_ref, 0, 0)
    step_one("ends")
    for px in (0, 1):
        convect_plane(first, 1, px)
    pack_ends(1, 0)
    send_ends(1)
    stage_two("ends")
    pack_columns(g_ref, 1, 0, 1)
    send_columns(1, 1)
    pack_lines(1, 0)
    send_lines(1)
    pack_rows(g_ref, 1, 0)
    send_rows(1)
    pair_axial(g_ref)

    for copy in blk_copies:
        copy.wait_recv()
    for d in range(n_cam):
        for t in range(2):
            if d == 0:
                ids = blk[pl.ds(2 * cam + t, 1), :]
            else:
                ids = blk_recv[d, pl.ds(2 * cam + t, 1), :]
            ids = jnp.broadcast_to(ids, (128, 128))
            for h in range(8):
                block_id = lax.broadcasted_iota(jnp.int32, (128, 128), 0) + 128 * h
                img_hot[t, 128 * h : 128 * h + 128, 128 * d : 128 * d + 128] = jnp.where(
                    ids == block_id, 1.0, 0.0
                ).astype(BF16)

    wide_lane = lax.broadcasted_iota(jnp.int32, (64, 128), 1)
    row64 = lax.broadcasted_iota(jnp.int32, (64, 128), 0)
    select = jnp.where(
        (wide_lane // 8 == row64 % 16) & ((wide_lane % 8) // 2 == row64 // 16), 1.0, 0.0
    ).astype(BF16)

    @twice
    def finish(a):
        x = xcol[0, a]
        for i in range(8):
            for b in range(8):
                n, part = 8 * a + i, slice(8 * b, 8 * b + 8)
                second = first[n, part, :] + winv[n, part, :] * total(g_ref, x, n, i, b)
                adv[n, part, :] = 0.5 * (fld[n, part, :] + second)
        for b in range(0, 8, 2):
            pieces = []
            for c in (b, b + 1):
                block = adv[pl.ds(8 * a, 8), 8 * c : 8 * c + 8, :].reshape(64, 128)
                pieces.append(jnp.where(wide_lane % 2 == 0, block, 0.0).astype(BF16))
                pieces.append(jnp.where(wide_lane % 2 == 1, block, 0.0).astype(BF16))
            out = lax.dot_general(
                select,
                jnp.concatenate(pieces, axis=0),
                (((1,), (1,)), ((), ())),
                preferred_element_type=F32,
            ).astype(BF16)
            for c in (0, 1):
                at = pl.multiple_of(128 * a + 16 * (b + c), 16)
                for h in range(4):
                    elems[pl.ds(at, 16), 128 * h : 128 * h + 128] = out[
                        16 * h : 16 * h + 16, 128 * c : 128 * c + 128
                    ]

    wait_all(1, ("rest",), True)
    add_rest(g_ref, 1, 0)
    finish("middle")
    wait_all(1, ("ends",), True)
    add_ends(g_ref, 1, 0)
    finish("ends")

    v_copies = []
    for d in sorted(range(1, n_cam), key=lambda d: -min(d, n_cam - d)) + [0]:
        q = lax.rem(cam + d, n_cam)
        picked = jnp.dot(cut_hot[q], elems[...], preferred_element_type=F32).astype(BF16)
        for t in range(2):
            value = jnp.dot(
                picked[128 * t : 128 * t + 128], wts_p[2 * q + t], preferred_element_type=F32
            ).astype(BF16)
            if d:
                v_send[d, t] = value
            else:
                v_recv[0, t] = value
        if d:
            copy = pltpu.make_async_remote_copy(
                src_ref=v_send.at[d],
                dst_ref=v_recv.at[d],
                send_sem=v_send_sem.at[d],
                recv_sem=v_recv_sem.at[d],
                device_id=peer(0, 0, d),
                device_id_type=pl.DeviceIdType.MESH,
            )
            copy.start()
            v_copies.append(copy)

    for e in (0, 1):
        wait_all(e, ("ends", "rest"), False)
    for copy in blk_copies:
        copy.wait_send()
    for copy in v_copies:
        copy.wait_recv()
    for copy in v_copies:
        copy.wait_send()


def write_kernel(adv, values, img_hot, adv_h, img_h, img, sem):
    result = pltpu.make_async_copy(adv, adv_h, sem.at[0])
    result.start()
    n_cam = values.shape[0]
    copies = []
    for t in range(2):
        slots = jnp.concatenate([values[d, t] for d in range(n_cam)], axis=0)
        for h in range(2):
            part = pl.ds(h * (NBLK // 2), NBLK // 2)
            img[t, part] = jnp.dot(img_hot[t, part], slots, preferred_element_type=F32)
            copy = pltpu.make_async_copy(
                img.at[t, part], img_h.at[t, part], sem.at[1 + 2 * t + h]
            )
            copy.start()
            copies.append(copy)
    for copy in copies:
        copy.wait()
    result.wait()


def face_buffers(kinds):
    shapes = [
        (2, kinds, 64, 128),
        (2, kinds, 8, 128),
        (2, kinds, 32, 128),
        (4, kinds, 8, 128),
        (2, kinds, 8, 128),
        (2, kinds, 64, 128),
        (2, 2, kinds, 8, 128),
        (2, 2, kinds, 8, 128),
        (2, 2, 2, kinds, 8, 128),
        (2, kinds, 32, 128),
        (2, 4, kinds, 8, 128),
        (2, 2, kinds, 8, 128),
    ]
    return tuple(pltpu.VMEM(shape, F32) for shape in shapes)


def per_device(sizes, scalar, velocity, lumped_mass, pixel_weights, cut_element, pixel_block):
    n_cam = sizes[0]
    flat = (32, 64, 128)
    hbm = pl.BlockSpec(memory_space=pltpu.HBM)
    big = pltpu.VMEM(flat, F32)
    dma = pltpu.SemaphoreType.DMA
    on_chip = pl.BlockSpec(memory_space=pltpu.VMEM)
    outputs = (
        pltpu.VMEM(flat, F32),
        pltpu.VMEM((n_cam, 2, 128, 128), BF16),
        pltpu.VMEM((2, NBLK, 128 * n_cam), BF16),
    )
    operands = (
        scalar.reshape(flat),
        velocity.reshape((3,) + flat),
        lumped_mass.reshape(flat),
        pixel_weights,
        cut_element,
        pixel_block,
        jnp.asarray(radial_matrix()),
        jnp.asarray(azimuth_table()),
    )
    results = pl.pallas_call(
        functools.partial(kernel, sizes),
        out_shape=outputs,
        in_specs=[hbm] * 8,
        out_specs=(on_chip,) * 3,
        scratch_shapes=[
            big,
            pltpu.VMEM((3,) + flat, F32),
            big,
            pltpu.VMEM((8, 512, 128), BF16),
            pltpu.VMEM((8, 128), jnp.int32),
            pltpu.VMEM((8, 128), jnp.int32),
            pltpu.VMEM((256, 256), BF16),
            pltpu.VMEM((8, 8, 128), F32),
            big,
            big,
            big,
            pltpu.VMEM((8, 64, 128), F32),
            face_buffers(2),
            face_buffers(1),
            pltpu.VMEM((2, 4, 8, 128), F32),
            pltpu.VMEM((512, 128), F32),
            pltpu.VMEM((8, 512, 128), BF16),
            pltpu.VMEM((4, 256, 512), BF16),
            pltpu.VMEM((512, 512), BF16),
            pltpu.VMEM((n_cam, 2, 128, 128), BF16),
            pltpu.VMEM((n_cam, 8, 128), jnp.int32),
            dma((7,)),
            dma((4,)),
            dma((58,)),
            dma((58,)),
            dma((n_cam,)),
            dma((n_cam,)),
            dma((n_cam,)),
            dma((n_cam,)),
        ],
        compiler_params=pltpu.CompilerParams(
            collective_id=0, has_side_effects=True, vmem_limit_bytes=40 * 1024 * 1024
        ),
    )(*[pltpu.with_memory_space_constraint(x, pltpu.HBM) for x in operands])
    advected, images = pl.pallas_call(
        write_kernel,
        out_shape=(
            jax.ShapeDtypeStruct(flat, F32),
            jax.ShapeDtypeStruct((2, NBLK, 128), F32),
        ),
        in_specs=[on_chip] * 3,
        out_specs=(hbm, hbm),
        scratch_shapes=[pltpu.VMEM((2, NBLK, 128), F32), dma((5,))],
        compiler_params=pltpu.CompilerParams(vmem_limit_bytes=16 * 1024 * 1024),
    )(*[pltpu.with_memory_space_constraint(x, pltpu.VMEM) for x in results])
    return advected.reshape(scalar.shape), images


def solution(mesh):
    sizes = tuple(mesh.shape[name] for name in ("cam", "ex", "ey"))
    placed = (
        P("ex", None, "ey", None, "cam"),
        P(None, "ex", None, "ey", None, "cam"),
        P("ex", None, "ey", None, "cam"),
        P(),
        P(None, ("cam", "ex", "ey")),
        P(None, ("cam", "ex", "ey")),
    )
    return jax.shard_map(
        functools.partial(per_device, sizes),
        mesh=mesh,
        in_specs=placed,
        out_specs=(P("ex", None, "ey", None, "cam"), P("cam", ("ex", "ey"), None)),
        check_vma=False,
    )
```

```python
import functools

import jax
import jax.numpy as jnp
import ml_dtypes
import numpy as np
from jax import lax
from jax.experimental import pallas as pl
from jax.experimental.pallas import tpu as pltpu
from jax.sharding import PartitionSpec as P

NBLK = 1024
STEP = 0.01
F32 = jnp.float32
BF16 = jnp.bfloat16


def legendre_seven(points):
    previous = points * 0.0 + 1.0
    current = points * 1.0
    for order in range(1, 7):
        following = ((2 * order + 1) * points * current - order * previous) / (order + 1)
        previous = current
        current = following
    return current


def gll_derivative():
    degree = 7
    gll_nodes = np.array(
        [
            -1.0,
            -0.8717401485096066,
            -0.5917001814331423,
            -0.2092992179024789,
            0.2092992179024789,
            0.5917001814331423,
            0.8717401485096066,
            1.0,
        ]
    )
    values = legendre_seven(gll_nodes)
    derivative = np.zeros((degree + 1, degree + 1))
    for target in range(degree + 1):
        for source in range(degree + 1):
            if target != source:
                derivative[target, source] = values[target] / (
                    values[source] * (gll_nodes[target] - gll_nodes[source])
                )
    derivative[0, 0] = -degree * (degree + 1) / 4.0
    derivative[degree, degree] = degree * (degree + 1) / 4.0
    return derivative


DERIV = gll_derivative()


def radial_matrix():
    table = np.kron(np.eye(16), DERIV.T).astype(np.float32)
    high = table.astype(ml_dtypes.bfloat16)
    low = (table - high.astype(np.float32)).astype(ml_dtypes.bfloat16)
    return np.block([[high, low], [high, np.zeros_like(low)]])


def cross_matrix():
    table = np.concatenate([np.kron(np.eye(8), DERIV), np.kron(DERIV, np.eye(8))])
    table = table.astype(np.float32)
    high = table.astype(ml_dtypes.bfloat16)
    low = (table - high.astype(np.float32)).astype(ml_dtypes.bfloat16)
    return np.concatenate([high, high, low], axis=1)


def azimuth_table():
    rows = np.arange(8)
    shifts = np.stack([DERIV[rows, (rows + d) % 8] for d in range(8)])
    return np.broadcast_to(shifts[:, :, None], (8, 8, 128)).astype(np.float32)


AXIAL = (1, 2, 0, 3)

SIGNS = [
    (sx, sy, sz)
    for sx in (-1, 0, 1)
    for sy in (-1, 0, 1)
    for sz in (-1, 0, 1)
    if (sx, sy, sz) != (0, 0, 0)
]


def kernel(
    sizes,
    scalar_h,
    vel_h,
    mass_h,
    wts_h,
    cut_h,
    blk_h,
    tab_h,
    azi_h,
    cross_h,
    adv,
    v_recv,
    img_hot,
    fld,
    vel,
    mass,
    wts,
    cut,
    blk,
    tab,
    azi,
    cross,
    g_ref,
    first,
    winv,
    radial,
    faces_one,
    faces_two,
    xcol,
    wide,
    wts_p,
    cut_hot,
    elems,
    v_send,
    blk_recv,
    in_sem,
    vel_sem,
    send_sem,
    recv_sem,
    v_send_sem,
    v_recv_sem,
    b_send_sem,
    b_recv_sem,
):
    n_cam, n_ex, n_ey = sizes
    cam, ex, ey = lax.axis_index("cam"), lax.axis_index("ex"), lax.axis_index("ey")
    faces = (faces_one, faces_two)

    def beside(at, size):
        return {
            0: at,
            1: jnp.where(at == size - 1, 0, at + 1),
            -1: jnp.where(at == 0, size - 1, at - 1),
        }

    cams, exs, eys = beside(cam, n_cam), beside(ex, n_ex), beside(ey, n_ey)
    peers = {s: {"cam": cams[s[2]], "ex": exs[s[0]], "ey": eys[s[1]]} for s in SIGNS}

    def camera_owner(d):
        return jnp.where(cam + d >= n_cam, cam + d - n_cam, cam + d)

    def along_cam(d):
        return {"cam": camera_owner(d), "ex": ex, "ey": ey}

    def load(src, dst, sem):
        copy = pltpu.make_async_copy(src, dst, sem)
        copy.start()
        return copy

    load_mass = load(mass_h, mass, in_sem.at[0])
    load_fld = load(scalar_h, fld, in_sem.at[1])
    load_tab = load(tab_h, tab, in_sem.at[2])
    load_azi = load(azi_h, azi, in_sem.at[3])
    load_cross = load(cross_h, cross, in_sem.at[7])

    def load_vel(a):
        load(vel_h.at[:, pl.ds(8 * a, 8)], vel.at[:, pl.ds(8 * a, 8)], vel_sem.at[a])

    load_vel(0)
    load_vel(3)
    barrier = pltpu.get_barrier_semaphore()
    for s in sorted(SIGNS, key=lambda s: (-abs(s[0]), -abs(s[2]), -abs(s[1]))):
        pl.semaphore_signal(barrier, inc=1, device_id=peers[s], device_id_type=pl.DeviceIdType.MESH)
    for d in range(2, n_cam - 1):
        pl.semaphore_signal(
            barrier, inc=1, device_id=along_cam(d), device_id_type=pl.DeviceIdType.MESH
        )
    load_vel(1)
    load_vel(2)
    load_blk = load(blk_h, blk, in_sem.at[4])
    load_cut = load(cut_h, cut, in_sem.at[5])
    load_wts = load(wts_h, wts, in_sem.at[6])

    lane = lax.broadcasted_iota(jnp.int32, (8, 128), 1)
    sub = lax.broadcasted_iota(jnp.int32, (8, 128), 0)
    even = lane % 2 == 0
    take_next = (lane % 8 == 7) & (lane != 127)
    take_prev = (lane % 8 == 0) & (lane != 0)
    edge = (lane == 0) | (lane == 127)
    zero = jnp.zeros((8, 128), F32)
    has_upper, has_lower = cam < n_cam - 1, cam > 0
    from_upper = jnp.where(has_upper, 1.0, 0.0).astype(F32)
    from_lower = jnp.where(has_lower, 1.0, 0.0).astype(F32)
    keep = jnp.where(even, jnp.full((8, 128), from_upper), jnp.full((8, 128), from_lower)) > 0.5

    def lane_pairs(g):
        return (
            g
            + jnp.where(take_next, pltpu.roll(g, 127, 1), zero)
            + jnp.where(take_prev, pltpu.roll(g, 1, 1), zero)
        )

    def twice(body):
        def outer(which):
            @pl.loop(0, 2)
            def _(t):
                body(3 * t if which == "ends" else 1 + t)

        return outer

    copies = []

    def send(src, dst, e, group, slot, s):
        copy = pltpu.make_async_remote_copy(
            src_ref=src,
            dst_ref=dst,
            send_sem=send_sem.at[slot],
            recv_sem=recv_sem.at[slot],
            device_id=peers[s],
            device_id_type=pl.DeviceIdType.MESH,
        )
        copies.append((e, group, s[2], copy))
        if s[2] == 0:
            copy.start()

    def toward(sz, body):
        pl.when(has_upper if sz > 0 else has_lower)(body)

    def launch(sz, body):
        first_new = len(copies)
        body()
        chosen = [copy for _, _, _, copy in copies[first_new:]]

        def start():
            for copy in chosen:
                copy.start()

        toward(sz, start)

    def wait_all(e, groups, received):
        for sz in (0, -1, 1):
            chosen = [c for at, group, z, c in copies if at == e and group in groups and z == sz]

            def body(chosen=chosen):
                for copy in chosen:
                    if received:
                        copy.wait_recv()
                    else:
                        copy.wait_send()

            if sz == 0:
                body()
            else:
                toward(-sz if received else sz, body)

    def pair_azimuth(ref, a):
        for i in range(8):
            n = 8 * a + i
            both = ref[n, pl.ds(7, 7, stride=8), :] + ref[n, pl.ds(8, 7, stride=8), :]
            ref[n, pl.ds(7, 7, stride=8), :] = both
            ref[n, pl.ds(8, 7, stride=8), :] = both

    def pair_axial(ref):
        for a in range(3):
            both = ref[8 * a + 7] + ref[8 * a + 8]
            ref[8 * a + 7] = both
            ref[8 * a + 8] = both

    def gather_columns(pieces):
        parts = [zero] * 4
        for at, (spot, piece) in enumerate(pieces):
            here = (lane == 2 * spot) | (lane == 2 * spot + 1)
            parts[at % 4] = jnp.where(here, pltpu.roll(piece, 2 * spot + 1, 1), parts[at % 4])
        return (parts[0] + parts[1]) + (parts[2] + parts[3])

    def pair_plane(plane):
        both = plane[pl.ds(7, 7, stride=8), :] + plane[pl.ds(8, 7, stride=8), :]
        plane[pl.ds(7, 7, stride=8), :] = both
        plane[pl.ds(8, 7, stride=8), :] = both

    def pack_ends(e, kind):
        plane, tile = faces[e][0], faces[e][1]
        for px in (0, 1):
            tile[px, kind] = gather_columns(
                [(56 * px + b, plane[px, kind, 8 * b : 8 * b + 8, :]) for b in range(8)]
            )

    def send_ends(e):
        plane, tile, _, _, _, r_plane, r_xy, r_xz, r_xyz, _, _, _ = faces[e]
        base = 30 * e
        for px in (0, 1):
            sx = 2 * px - 1
            send(plane.at[px], r_plane.at[px], e, "ends", base + px, (sx, 0, 0))
            for py in (0, 1):
                send(
                    plane.at[px, :, pl.ds(56 * py, 8)],
                    r_xy.at[px, py],
                    e,
                    "ends",
                    base + 2 + 2 * px + py,
                    (sx, 2 * py - 1, 0),
                )
        for pz in (0, 1):
            sz = 2 * pz - 1

            def body(pz=pz, sz=sz):
                for px in (0, 1):
                    sx = 2 * px - 1
                    slot = base + 6 + 6 * pz + 3 * px
                    send(tile.at[px], r_xz.at[px, pz], e, "ends", slot, (sx, 0, sz))
                    for py in (0, 1):
                        send(
                            tile.at[px],
                            r_xyz.at[px, py, pz],
                            e,
                            "ends",
                            slot + 1 + py,
                            (sx, 2 * py - 1, sz),
                        )

            launch(sz, body)

    def pack_columns(ref, e, kind, half):
        cols = faces[e][3]

        @pl.loop(0, 2)
        def _(t):
            a = 3 * t if half else 1 + t
            cols[2 * half + t, kind] = gather_columns(
                [
                    (8 * i + b, ref[8 * a + i, 8 * b : 8 * b + 8, :])
                    for i in range(8)
                    for b in range(8)
                ]
            )

    def send_columns(e, half):
        cols, r_cols = faces[e][3], faces[e][10]
        for pz in (0, 1):
            sz = 2 * pz - 1

            def body(pz=pz, sz=sz):
                part = pl.ds(2 * half, 2)
                send(
                    cols.at[part],
                    r_cols.at[pz, part],
                    e,
                    "rest",
                    30 * e + 18 + 2 * pz + half,
                    (0, 0, sz),
                )

            launch(sz, body)

    def pack_lines(e, kind):
        cols, lines = faces[e][3], faces[e][4]
        low, high = zero, zero
        for at in range(4):
            low = jnp.where(sub == at, jnp.broadcast_to(cols[at, kind, 0:1, :], (8, 128)), low)
            high = jnp.where(sub == at, jnp.broadcast_to(cols[at, kind, 7:8, :], (8, 128)), high)
        lines[0, kind] = low
        lines[1, kind] = high

    def send_lines(e):
        lines, r_yz = faces[e][4], faces[e][11]
        for pz in (0, 1):
            sz = 2 * pz - 1

            def body(pz=pz, sz=sz):
                for py in (0, 1):
                    send(
                        lines.at[py],
                        r_yz.at[py, pz],
                        e,
                        "rest",
                        30 * e + 22 + 2 * pz + py,
                        (0, 2 * py - 1, sz),
                    )

            launch(sz, body)

    def pack_rows(ref, e, kind):
        rows = faces[e][2]
        for n in range(32):
            rows[0, kind, n : n + 1, :] = ref[n, 0:1, :]
            rows[1, kind, n : n + 1, :] = ref[n, 63:64, :]

    def send_rows(e):
        rows, r_rows = faces[e][2], faces[e][9]
        for py in (0, 1):
            send(rows.at[py], r_rows.at[py], e, "rest", 30 * e + 26 + py, (0, 2 * py - 1, 0))

    def across_azimuth(t, py):
        t = pltpu.roll(t, 114 if py else 14, 1)
        return jnp.where((lane % 16 < 2) if py else (lane % 16 >= 14), t, zero)

    def swap(q):
        return jnp.where(keep, jnp.where(even, pltpu.roll(q, 127, 1), pltpu.roll(q, 1, 1)), zero)

    def add_rest(ref, e, kind):
        r_rows, r_cols, r_yz = faces[e][9:12]
        for n in range(32):
            after, before = r_rows[1, kind, n : n + 1, :], r_rows[0, kind, n : n + 1, :]
            if 0 < n < 31 and n % 8 in (0, 7):
                other = n + 1 if n % 8 == 7 else n - 1
                after = after + r_rows[1, kind, other : other + 1, :]
                before = before + r_rows[0, kind, other : other + 1, :]
            ref[n, 0:1, :] = ref[n, 0:1, :] + after
            ref[n, 63:64, :] = ref[n, 63:64, :] + before
        across = [
            across_azimuth(jnp.where(even, r_yz[py, 1, kind], r_yz[py, 0, kind]), py)
            for py in (0, 1)
        ]
        found = [None] * 4
        for at, a in enumerate(AXIAL):
            q = jnp.where(even, r_cols[1, at, kind], r_cols[0, at, kind])
            q = q + jnp.where(sub == 0, jnp.broadcast_to(across[1][at : at + 1, :], (8, 128)), zero)
            q = q + jnp.where(sub == 7, jnp.broadcast_to(across[0][at : at + 1, :], (8, 128)), zero)
            found[a] = q
        for a in range(4):
            q = found[a]
            if a < 3:
                q = q + jnp.where(lane >= 112, pltpu.roll(found[a + 1], 112, 1), zero)
            if a > 0:
                q = q + jnp.where(lane < 16, pltpu.roll(found[a - 1], 16, 1), zero)
            xcol[kind, a] = swap(q)

    def add_ends(ref, e, kind):
        r_plane, r_xy, r_xz, r_xyz = faces[e][5:9]
        for px in (0, 1):
            n, a = (0, 0) if px else (31, 3)
            ref[n] = ref[n] + r_plane[px, kind]
            for py in (0, 1):
                row, got = (0, 7) if py else (63, 0)
                ref[n, row : row + 1, :] = (
                    ref[n, row : row + 1, :] + r_xy[px, py, kind, got : got + 1, :]
                )
            q = jnp.where(even, r_xz[px, 1, kind], r_xz[px, 0, kind])
            for py in (0, 1):
                c = jnp.where(even, r_xyz[px, py, 1, kind], r_xyz[px, py, 0, kind])
                c = pltpu.roll(across_azimuth(c, py), 1 if py else 7, 0)
                q = q + jnp.where(sub == (0 if py else 7), c, zero)
            if px:
                q = jnp.where(lane < 16, pltpu.roll(q, 16, 1), zero)
            else:
                q = jnp.where(lane >= 112, pltpu.roll(q, 112, 1), zero)
            xcol[kind, a] = xcol[kind, a] + swap(q)

    def total(ref, x, n, i, b):
        spot = 8 * i + b
        return ref[n, 8 * b : 8 * b + 8, :] + jnp.where(
            edge, pltpu.roll(x, 127 - 2 * spot, 1), zero
        )

    def along_radius(block):
        high = block.astype(BF16)
        low = (block - high.astype(F32)).astype(BF16)
        both = jnp.dot(
            jnp.concatenate([high, low], axis=1), tab[...], preferred_element_type=F32
        )
        return both[:, :128] + both[:, 128:]

    def along_azimuth(f):
        turned = azi[0] * f
        for d in range(1, 8):
            turned = turned + azi[d] * pltpu.roll(f, 8 - d, 0)
        return turned

    def convect_plane(src, e, px):
        n, i = 31 * px, 7 * px
        plane = faces[e][0].at[px, 0]
        turning = along_radius(src[n])
        for b in range(8):
            part = slice(8 * b, 8 * b + 8)
            axial = None
            for p in range(8):
                term = float(DERIV[i, p]) * src[n - i + p, part, :]
                axial = term if axial is None else axial + term
            c = (
                vel[0, n, part, :] * axial
                + vel[1, n, part, :] * along_azimuth(src[n, part, :])
                + vel[2, n, part, :] * turning[part, :]
            )
            plane[part, :] = lane_pairs(mass[n, part, :] * c)
        pair_plane(plane)

    def convect(src, a):
        radial[...] = along_radius(src[pl.ds(8 * a, 8)].reshape(512, 128)).reshape(8, 64, 128)
        for b in range(0, 8, 2):
            pieces = []
            for d in (b, b + 1):
                block = src[pl.ds(8 * a, 8), 8 * d : 8 * d + 8, :].reshape(64, 128)
                high = block.astype(BF16)
                low = (block - high.astype(F32)).astype(BF16)
                pieces.append(jnp.concatenate([high, low, high], axis=0))
            both = jnp.dot(
                cross[...], jnp.concatenate(pieces, axis=1), preferred_element_type=F32
            )
            for d in (0, 1):
                part = slice(8 * (b + d), 8 * (b + d) + 8)
                lanes = slice(128 * d, 128 * d + 128)
                for i in range(8):
                    n = 8 * a + i
                    c = (
                        vel[0, n, part, :] * both[64 + 8 * i : 72 + 8 * i, lanes]
                        + vel[1, n, part, :] * both[8 * i : 8 * i + 8, lanes]
                        + vel[2, n, part, :] * radial[i, part, :]
                    )
                    g_ref[n, part, :] = lane_pairs(mass[n, part, :] * c)
        pair_azimuth(g_ref, a)

    for pz in (0, 1):

        @pl.when(jnp.logical_not(has_lower if pz else has_upper))
        def _(pz=pz):
            for _, _, _, _, _, _, _, r_xz, r_xyz, _, r_cols, r_yz in faces:
                r_cols[pz] = jnp.zeros(r_cols.shape[1:], F32)
                for px in (0, 1):
                    r_xz[px, pz] = jnp.zeros(r_xz.shape[2:], F32)
                    r_yz[px, pz] = jnp.zeros(r_yz.shape[2:], F32)
                    for py in (0, 1):
                        r_xyz[px, py, pz] = jnp.zeros(r_xyz.shape[3:], F32)

    load_mass.wait()

    @pl.loop(0, 4)
    def _(a):
        for i in range(8):
            for b in range(8):
                n, part = 8 * a + i, slice(8 * b, 8 * b + 8)
                winv[n, part, :] = lane_pairs(mass[n, part, :])
        pair_azimuth(winv, a)

    for px in (0, 1):
        faces[0][0][px, 1] = winv[31 * px]
    pack_ends(0, 1)
    for half in (0, 1):
        pack_columns(winv, 0, 1, half)
    pack_lines(0, 1)
    pack_rows(winv, 0, 1)
    pair_axial(winv)

    load_fld.wait()
    load_tab.wait()
    load_azi.wait()
    load_cross.wait()

    def wait_velocity(a):
        part = pl.ds(8 * a, 8)
        pltpu.make_async_copy(vel_h.at[:, part], vel.at[:, part], vel_sem.at[a]).wait()

    for px in (0, 1):
        wait_velocity(3 * px)
        convect_plane(fld, 0, px)
    pack_ends(0, 0)
    pl.semaphore_wait(barrier, 26 + n_cam - 3)
    send_ends(0)
    wait_velocity(1)
    wait_velocity(2)

    @twice
    def stage_one(a):
        convect(fld, a)

    stage_one("middle")
    pack_columns(g_ref, 0, 0, 0)
    send_columns(0, 0)
    stage_one("ends")
    pack_columns(g_ref, 0, 0, 1)
    send_columns(0, 1)
    pack_lines(0, 0)
    send_lines(0)
    pack_rows(g_ref, 0, 0)
    send_rows(0)
    pair_axial(g_ref)

    load_blk.wait()
    blk_copies = []
    for d in range(1, n_cam):
        copy = pltpu.make_async_remote_copy(
            src_ref=blk,
            dst_ref=blk_recv.at[d],
            send_sem=b_send_sem.at[d],
            recv_sem=b_recv_sem.at[d],
            device_id=along_cam(d),
            device_id_type=pl.DeviceIdType.MESH,
        )
        copy.start()
        blk_copies.append(copy)

    load_cut.wait()
    load_wts.wait()

    @pl.loop(0, 8)
    def _(m):
        wide[...] = wts[m].astype(F32)
        for k in range(8):
            wts_p[m, 64 * k : 64 * k + 64, :] = wide[pl.ds(k, 64, stride=8), :].astype(BF16)
        chosen = jnp.broadcast_to(cut[pl.ds(m, 1), :].astype(F32), (128, 128)).T
        place = lax.broadcasted_iota(jnp.int32, (128, 128), 1).astype(F32)
        for q in range(4):
            cut_hot[m // 2, pl.ds(128 * (m % 2), 128), 128 * q : 128 * q + 128] = jnp.where(
                chosen == place + 128.0 * q, 1.0, 0.0
            ).astype(BF16)

    @twice
    def step_one(a):
        x, y = xcol[0, a], xcol[1, a]
        for i in range(8):
            for b in range(8):
                n, part = 8 * a + i, slice(8 * b, 8 * b + 8)
                factor = -STEP * pl.reciprocal(total(winv, y, n, i, b))
                winv[n, part, :] = factor
                first[n, part, :] = fld[n, part, :] + factor * total(g_ref, x, n, i, b)

    @twice
    def stage_two(a):
        convect(first, a)

    wait_all(0, ("ends", "rest"), True)
    for ref, kind in ((winv, 1), (g_ref, 0)):
        add_rest(ref, 0, kind)
        add_ends(ref, 0, kind)
    step_one("ends")
    for px in (0, 1):
        convect_plane(first, 1, px)
    pack_ends(1, 0)
    send_ends(1)
    step_one("middle")
    stage_two("middle")
    pack_columns(g_ref, 1, 0, 0)
    send_columns(1, 0)
    stage_two("ends")
    pack_columns(g_ref, 1, 0, 1)
    send_columns(1, 1)
    pack_lines(1, 0)
    send_lines(1)
    pack_rows(g_ref, 1, 0)
    send_rows(1)
    pair_axial(g_ref)

    for copy in blk_copies:
        copy.wait_recv()
    for d in range(n_cam):
        for t in range(2):
            if d == 0:
                ids = blk[pl.ds(2 * cam + t, 1), :]
            else:
                ids = blk_recv[d, pl.ds(2 * cam + t, 1), :]
            ids = jnp.broadcast_to(ids, (128, 128))
            for h in range(8):
                block_id = lax.broadcasted_iota(jnp.int32, (128, 128), 0) + 128 * h
                img_hot[t, 128 * h : 128 * h + 128, 128 * d : 128 * d + 128] = jnp.where(
                    ids == block_id, 1.0, 0.0
                ).astype(BF16)

    wide_lane = lax.broadcasted_iota(jnp.int32, (64, 128), 1)
    row64 = lax.broadcasted_iota(jnp.int32, (64, 128), 0)
    select = jnp.where(
        (wide_lane // 8 == row64 % 16) & ((wide_lane % 8) // 2 == row64 // 16), 1.0, 0.0
    ).astype(BF16)

    @twice
    def finish(a):
        x = xcol[0, a]
        for i in range(8):
            for b in range(8):
                n, part = 8 * a + i, slice(8 * b, 8 * b + 8)
                second = first[n, part, :] + winv[n, part, :] * total(g_ref, x, n, i, b)
                adv[n, part, :] = 0.5 * (fld[n, part, :] + second)
        for b in range(0, 8, 2):
            pieces = []
            for c in (b, b + 1):
                block = adv[pl.ds(8 * a, 8), 8 * c : 8 * c + 8, :].reshape(64, 128)
                pieces.append(jnp.where(wide_lane % 2 == 0, block, 0.0).astype(BF16))
                pieces.append(jnp.where(wide_lane % 2 == 1, block, 0.0).astype(BF16))
            out = lax.dot_general(
                select,
                jnp.concatenate(pieces, axis=0),
                (((1,), (1,)), ((), ())),
                preferred_element_type=F32,
            ).astype(BF16)
            for c in (0, 1):
                at = pl.multiple_of(128 * a + 16 * (b + c), 16)
                for h in range(4):
                    elems[pl.ds(at, 16), 128 * h : 128 * h + 128] = out[
                        16 * h : 16 * h + 16, 128 * c : 128 * c + 128
                    ]

    wait_all(1, ("rest",), True)
    add_rest(g_ref, 1, 0)
    finish("middle")
    wait_all(1, ("ends",), True)
    add_ends(g_ref, 1, 0)
    finish("ends")

    v_copies = []
    for d in sorted(range(1, n_cam), key=lambda d: -min(d, n_cam - d)) + [0]:
        q = camera_owner(d)
        picked = jnp.dot(cut_hot[q], elems[...], preferred_element_type=F32).astype(BF16)
        for t in range(2):
            value = jnp.dot(
                picked[128 * t : 128 * t + 128], wts_p[2 * q + t], preferred_element_type=F32
            ).astype(BF16)
            if d:
                v_send[d, t] = value
            else:
                v_recv[0, t] = value
        if d:
            copy = pltpu.make_async_remote_copy(
                src_ref=v_send.at[d],
                dst_ref=v_recv.at[d],
                send_sem=v_send_sem.at[d],
                recv_sem=v_recv_sem.at[d],
                device_id=along_cam(d),
                device_id_type=pl.DeviceIdType.MESH,
            )
            copy.start()
            v_copies.append(copy)

    for e in (0, 1):
        wait_all(e, ("ends", "rest"), False)
    for copy in blk_copies:
        copy.wait_send()
    for copy in v_copies:
        copy.wait_recv()
    for copy in v_copies:
        copy.wait_send()


def write_kernel(adv, values, img_hot, adv_h, img_h, img, sem):
    result = pltpu.make_async_copy(adv, adv_h, sem.at[0])
    result.start()
    n_cam = values.shape[0]
    copies = []
    for t in range(2):
        slots = jnp.concatenate([values[d, t] for d in range(n_cam)], axis=0)
        for h in range(2):
            part = pl.ds(h * (NBLK // 2), NBLK // 2)
            img[t, part] = jnp.dot(img_hot[t, part], slots, preferred_element_type=F32)
            copy = pltpu.make_async_copy(
                img.at[t, part], img_h.at[t, part], sem.at[1 + 2 * t + h]
            )
            copy.start()
            copies.append(copy)
    for copy in copies:
        copy.wait()
    result.wait()


def face_buffers(kinds):
    shapes = [
        (2, kinds, 64, 128),
        (2, kinds, 8, 128),
        (2, kinds, 32, 128),
        (4, kinds, 8, 128),
        (2, kinds, 8, 128),
        (2, kinds, 64, 128),
        (2, 2, kinds, 8, 128),
        (2, 2, kinds, 8, 128),
        (2, 2, 2, kinds, 8, 128),
        (2, kinds, 32, 128),
        (2, 4, kinds, 8, 128),
        (2, 2, kinds, 8, 128),
    ]
    return tuple(pltpu.VMEM(shape, F32) for shape in shapes)


def per_device(sizes, scalar, velocity, lumped_mass, pixel_weights, cut_element, pixel_block):
    n_cam = sizes[0]
    flat = (32, 64, 128)
    hbm = pl.BlockSpec(memory_space=pltpu.HBM)
    big = pltpu.VMEM(flat, F32)
    dma = pltpu.SemaphoreType.DMA
    on_chip = pl.BlockSpec(memory_space=pltpu.VMEM)
    outputs = (
        pltpu.VMEM(flat, F32),
        pltpu.VMEM((n_cam, 2, 128, 128), BF16),
        pltpu.VMEM((2, NBLK, 128 * n_cam), BF16),
    )
    operands = (
        scalar.reshape(flat),
        velocity.reshape((3,) + flat),
        lumped_mass.reshape(flat),
        pixel_weights,
        cut_element,
        pixel_block,
        jnp.asarray(radial_matrix()),
        jnp.asarray(azimuth_table()),
        jnp.asarray(cross_matrix()),
    )
    results = pl.pallas_call(
        functools.partial(kernel, sizes),
        out_shape=outputs,
        in_specs=[hbm] * 9,
        out_specs=(on_chip,) * 3,
        scratch_shapes=[
            big,
            pltpu.VMEM((3,) + flat, F32),
            big,
            pltpu.VMEM((8, 512, 128), BF16),
            pltpu.VMEM((8, 128), jnp.int32),
            pltpu.VMEM((8, 128), jnp.int32),
            pltpu.VMEM((256, 256), BF16),
            pltpu.VMEM((8, 8, 128), F32),
            pltpu.VMEM((128, 192), BF16),
            big,
            big,
            big,
            pltpu.VMEM((8, 64, 128), F32),
            face_buffers(2),
            face_buffers(1),
            pltpu.VMEM((2, 4, 8, 128), F32),
            pltpu.VMEM((512, 128), F32),
            pltpu.VMEM((8, 512, 128), BF16),
            pltpu.VMEM((4, 256, 512), BF16),
            pltpu.VMEM((512, 512), BF16),
            pltpu.VMEM((n_cam, 2, 128, 128), BF16),
            pltpu.VMEM((n_cam, 8, 128), jnp.int32),
            dma((8,)),
            dma((4,)),
            dma((58,)),
            dma((58,)),
            dma((n_cam,)),
            dma((n_cam,)),
            dma((n_cam,)),
            dma((n_cam,)),
        ],
        compiler_params=pltpu.CompilerParams(
            collective_id=0, has_side_effects=True, vmem_limit_bytes=40 * 1024 * 1024
        ),
    )(*[pltpu.with_memory_space_constraint(x, pltpu.HBM) for x in operands])
    advected, images = pl.pallas_call(
        write_kernel,
        out_shape=(
            jax.ShapeDtypeStruct(flat, F32),
            jax.ShapeDtypeStruct((2, NBLK, 128), F32),
        ),
        in_specs=[on_chip] * 3,
        out_specs=(hbm, hbm),
        scratch_shapes=[pltpu.VMEM((2, NBLK, 128), F32), dma((5,))],
        compiler_params=pltpu.CompilerParams(vmem_limit_bytes=16 * 1024 * 1024),
    )(*[pltpu.with_memory_space_constraint(x, pltpu.VMEM) for x in results])
    return advected.reshape(scalar.shape), images


def solution(mesh):
    sizes = tuple(mesh.shape[name] for name in ("cam", "ex", "ey"))
    placed = (
        P("ex", None, "ey", None, "cam"),
        P(None, "ex", None, "ey", None, "cam"),
        P("ex", None, "ey", None, "cam"),
        P(),
        P(None, ("cam", "ex", "ey")),
        P(None, ("cam", "ex", "ey")),
    )
    return jax.shard_map(
        functools.partial(per_device, sizes),
        mesh=mesh,
        in_specs=placed,
        out_specs=(P("ex", None, "ey", None, "cam"), P("cam", ("ex", "ey"), None)),
        check_vma=False,
    )
```

```python
import functools

import jax
import jax.numpy as jnp
import ml_dtypes
import numpy as np
from jax import lax
from jax.experimental import pallas as pl
from jax.experimental.pallas import tpu as pltpu
from jax.sharding import PartitionSpec as P

NBLK = 1024
STEP = 0.01
F32 = jnp.float32
BF16 = jnp.bfloat16


def legendre_seven(points):
    previous = points * 0.0 + 1.0
    current = points * 1.0
    for order in range(1, 7):
        following = ((2 * order + 1) * points * current - order * previous) / (order + 1)
        previous = current
        current = following
    return current


def gll_derivative():
    degree = 7
    gll_nodes = np.array(
        [
            -1.0,
            -0.8717401485096066,
            -0.5917001814331423,
            -0.2092992179024789,
            0.2092992179024789,
            0.5917001814331423,
            0.8717401485096066,
            1.0,
        ]
    )
    values = legendre_seven(gll_nodes)
    derivative = np.zeros((degree + 1, degree + 1))
    for target in range(degree + 1):
        for source in range(degree + 1):
            if target != source:
                derivative[target, source] = values[target] / (
                    values[source] * (gll_nodes[target] - gll_nodes[source])
                )
    derivative[0, 0] = -degree * (degree + 1) / 4.0
    derivative[degree, degree] = degree * (degree + 1) / 4.0
    return derivative


DERIV = gll_derivative()


def radial_matrix():
    table = np.kron(np.eye(16), DERIV.T).astype(np.float32)
    high = table.astype(ml_dtypes.bfloat16)
    low = (table - high.astype(np.float32)).astype(ml_dtypes.bfloat16)
    return np.block([[high, low], [high, np.zeros_like(low)]])


def cross_matrix():
    table = np.concatenate([np.kron(np.eye(8), DERIV), np.kron(DERIV, np.eye(8))])
    table = table.astype(np.float32)
    high = table.astype(ml_dtypes.bfloat16)
    low = (table - high.astype(np.float32)).astype(ml_dtypes.bfloat16)
    return np.concatenate([high, high, low], axis=1)


def azimuth_table():
    rows = np.arange(8)
    shifts = np.stack([DERIV[rows, (rows + d) % 8] for d in range(8)])
    return np.broadcast_to(shifts[:, :, None], (8, 8, 128)).astype(np.float32)


AXIAL = (1, 2, 0, 3)

SIGNS = [
    (sx, sy, sz)
    for sx in (-1, 0, 1)
    for sy in (-1, 0, 1)
    for sz in (-1, 0, 1)
    if (sx, sy, sz) != (0, 0, 0)
]


def kernel(
    sizes,
    scalar_h,
    vel_h,
    mass_h,
    wts_h,
    cut_h,
    blk_h,
    tab_h,
    azi_h,
    cross_h,
    adv,
    v_recv,
    img_hot,
    fld,
    vel,
    mass,
    wts,
    cut,
    blk,
    tab,
    azi,
    cross,
    g_ref,
    first,
    winv,
    radial,
    faces_one,
    faces_two,
    xcol,
    wide,
    wts_p,
    cut_hot,
    elems,
    v_send,
    blk_recv,
    in_sem,
    vel_sem,
    send_sem,
    recv_sem,
    v_send_sem,
    v_recv_sem,
    b_send_sem,
    b_recv_sem,
):
    n_cam, n_ex, n_ey = sizes
    cam, ex, ey = lax.axis_index("cam"), lax.axis_index("ex"), lax.axis_index("ey")
    faces = (faces_one, faces_two)

    def beside(at, size):
        return {
            0: at,
            1: jnp.where(at == size - 1, 0, at + 1),
            -1: jnp.where(at == 0, size - 1, at - 1),
        }

    cams, exs, eys = beside(cam, n_cam), beside(ex, n_ex), beside(ey, n_ey)
    peers = {s: {"cam": cams[s[2]], "ex": exs[s[0]], "ey": eys[s[1]]} for s in SIGNS}

    def camera_owner(d):
        return jnp.where(cam + d >= n_cam, cam + d - n_cam, cam + d)

    def along_cam(d):
        return {"cam": camera_owner(d), "ex": ex, "ey": ey}

    def load(src, dst, sem):
        copy = pltpu.make_async_copy(src, dst, sem)
        copy.start()
        return copy

    load_mass = load(mass_h, mass, in_sem.at[0])
    load_fld = load(scalar_h, fld, in_sem.at[1])
    load_tab = load(tab_h, tab, in_sem.at[2])
    load_azi = load(azi_h, azi, in_sem.at[3])
    load_cross = load(cross_h, cross, in_sem.at[7])

    def load_vel(a):
        load(vel_h.at[:, pl.ds(8 * a, 8)], vel.at[:, pl.ds(8 * a, 8)], vel_sem.at[a])

    load_vel(0)
    load_vel(3)
    barrier = pltpu.get_barrier_semaphore()
    for s in sorted(SIGNS, key=lambda s: (-abs(s[0]), -abs(s[2]), -abs(s[1]))):
        pl.semaphore_signal(barrier, inc=1, device_id=peers[s], device_id_type=pl.DeviceIdType.MESH)
    for d in range(2, n_cam - 1):
        pl.semaphore_signal(
            barrier, inc=1, device_id=along_cam(d), device_id_type=pl.DeviceIdType.MESH
        )
    load_vel(1)
    load_vel(2)
    load_blk = load(blk_h, blk, in_sem.at[4])
    load_cut = load(cut_h, cut, in_sem.at[5])
    load_wts = load(wts_h, wts, in_sem.at[6])

    lane = lax.broadcasted_iota(jnp.int32, (8, 128), 1)
    sub = lax.broadcasted_iota(jnp.int32, (8, 128), 0)
    even = lane % 2 == 0
    take_next = (lane % 8 == 7) & (lane != 127)
    take_prev = (lane % 8 == 0) & (lane != 0)
    edge = (lane == 0) | (lane == 127)
    zero = jnp.zeros((8, 128), F32)
    has_upper, has_lower = cam < n_cam - 1, cam > 0
    from_upper = jnp.where(has_upper, 1.0, 0.0).astype(F32)
    from_lower = jnp.where(has_lower, 1.0, 0.0).astype(F32)
    keep = jnp.where(even, jnp.full((8, 128), from_upper), jnp.full((8, 128), from_lower)) > 0.5

    def lane_pairs(g):
        return (
            g
            + jnp.where(take_next, pltpu.roll(g, 127, 1), zero)
            + jnp.where(take_prev, pltpu.roll(g, 1, 1), zero)
        )

    def twice(body):
        def outer(which):
            @pl.loop(0, 2)
            def _(t):
                body(*((3 * t, 2 + t) if which == "ends" else (1 + t, t)))

        return outer

    copies = []

    def send(src, dst, e, group, slot, s):
        copy = pltpu.make_async_remote_copy(
            src_ref=src,
            dst_ref=dst,
            send_sem=send_sem.at[slot],
            recv_sem=recv_sem.at[slot],
            device_id=peers[s],
            device_id_type=pl.DeviceIdType.MESH,
        )
        copies.append((e, group, s[2], copy))
        if s[2] == 0:
            copy.start()

    def toward(sz, body):
        pl.when(has_upper if sz > 0 else has_lower)(body)

    def launch(sz, body):
        first_new = len(copies)
        body()
        chosen = [copy for _, _, _, copy in copies[first_new:]]

        def start():
            for copy in chosen:
                copy.start()

        toward(sz, start)

    def wait_all(e, groups, received):
        for sz in (0, -1, 1):
            chosen = [c for at, group, z, c in copies if at == e and group in groups and z == sz]

            def body(chosen=chosen):
                for copy in chosen:
                    if received:
                        copy.wait_recv()
                    else:
                        copy.wait_send()

            if sz == 0:
                body()
            else:
                toward(-sz if received else sz, body)

    def pair_azimuth(ref, a):
        for i in range(8):
            n = 8 * a + i
            both = ref[n, pl.ds(7, 7, stride=8), :] + ref[n, pl.ds(8, 7, stride=8), :]
            ref[n, pl.ds(7, 7, stride=8), :] = both
            ref[n, pl.ds(8, 7, stride=8), :] = both

    def pair_axial(ref):
        for a in range(3):
            both = ref[8 * a + 7] + ref[8 * a + 8]
            ref[8 * a + 7] = both
            ref[8 * a + 8] = both

    def gather_columns(pieces):
        parts = [zero] * 4
        for at, (spot, piece) in enumerate(pieces):
            here = (lane == 2 * spot) | (lane == 2 * spot + 1)
            parts[at % 4] = jnp.where(here, pltpu.roll(piece, 2 * spot + 1, 1), parts[at % 4])
        return (parts[0] + parts[1]) + (parts[2] + parts[3])

    def pair_plane(plane):
        both = plane[pl.ds(7, 7, stride=8), :] + plane[pl.ds(8, 7, stride=8), :]
        plane[pl.ds(7, 7, stride=8), :] = both
        plane[pl.ds(8, 7, stride=8), :] = both

    def pack_ends(e, kind):
        plane, tile = faces[e][0], faces[e][1]
        for px in (0, 1):
            tile[px, kind] = gather_columns(
                [(56 * px + b, plane[px, kind, 8 * b : 8 * b + 8, :]) for b in range(8)]
            )

    def send_ends(e):
        plane, tile, _, _, _, r_plane, r_xy, r_xz, r_xyz, _, _, _ = faces[e]
        base = 30 * e
        for px in (0, 1):
            sx = 2 * px - 1
            send(plane.at[px], r_plane.at[px], e, "ends", base + px, (sx, 0, 0))
            for py in (0, 1):
                send(
                    plane.at[px, :, pl.ds(56 * py, 8)],
                    r_xy.at[px, py],
                    e,
                    "ends",
                    base + 2 + 2 * px + py,
                    (sx, 2 * py - 1, 0),
                )
        for pz in (0, 1):
            sz = 2 * pz - 1

            def body(pz=pz, sz=sz):
                for px in (0, 1):
                    sx = 2 * px - 1
                    slot = base + 6 + 6 * pz + 3 * px
                    send(tile.at[px], r_xz.at[px, pz], e, "ends", slot, (sx, 0, sz))
                    for py in (0, 1):
                        send(
                            tile.at[px],
                            r_xyz.at[px, py, pz],
                            e,
                            "ends",
                            slot + 1 + py,
                            (sx, 2 * py - 1, sz),
                        )

            launch(sz, body)

    def pick(parts, spot, piece):
        here = (lane == 2 * spot) | (lane == 2 * spot + 1)
        parts[spot % 4] = jnp.where(here, pltpu.roll(piece, 2 * spot + 1, 1), parts[spot % 4])

    def put_columns(parts, e, kind, slot):
        q = (parts[0] + parts[1]) + (parts[2] + parts[3])
        after = pltpu.roll(pltpu.roll(q, 126, 1), 7, 0)
        before = pltpu.roll(pltpu.roll(q, 2, 1), 1, 0)
        q = q + jnp.where((sub == 7) & (lane % 16 < 14), after, zero)
        q = q + jnp.where((sub == 0) & (lane % 16 >= 2), before, zero)
        faces[e][3][slot, kind] = q

    def send_columns(e, half):
        cols, r_cols = faces[e][3], faces[e][10]
        for pz in (0, 1):
            sz = 2 * pz - 1

            def body(pz=pz, sz=sz):
                part = pl.ds(2 * half, 2)
                send(
                    cols.at[part],
                    r_cols.at[pz, part],
                    e,
                    "rest",
                    30 * e + 18 + 2 * pz + half,
                    (0, 0, sz),
                )

            launch(sz, body)

    def pack_lines(e, kind):
        cols, lines = faces[e][3], faces[e][4]
        low, high = zero, zero
        for at in range(4):
            low = jnp.where(sub == at, jnp.broadcast_to(cols[at, kind, 0:1, :], (8, 128)), low)
            high = jnp.where(sub == at, jnp.broadcast_to(cols[at, kind, 7:8, :], (8, 128)), high)
        lines[0, kind] = low
        lines[1, kind] = high

    def send_lines(e):
        lines, r_yz = faces[e][4], faces[e][11]
        for pz in (0, 1):
            sz = 2 * pz - 1

            def body(pz=pz, sz=sz):
                for py in (0, 1):
                    send(
                        lines.at[py],
                        r_yz.at[py, pz],
                        e,
                        "rest",
                        30 * e + 22 + 2 * pz + py,
                        (0, 2 * py - 1, sz),
                    )

            launch(sz, body)

    def pack_rows(ref, e, kind):
        rows = faces[e][2]
        for n in range(32):
            rows[0, kind, n : n + 1, :] = ref[n, 0:1, :]
            rows[1, kind, n : n + 1, :] = ref[n, 63:64, :]

    def send_rows(e):
        rows, r_rows = faces[e][2], faces[e][9]
        for py in (0, 1):
            send(rows.at[py], r_rows.at[py], e, "rest", 30 * e + 26 + py, (0, 2 * py - 1, 0))

    def across_azimuth(t, py):
        t = pltpu.roll(t, 114 if py else 14, 1)
        return jnp.where((lane % 16 < 2) if py else (lane % 16 >= 14), t, zero)

    def swap(q):
        return jnp.where(keep, jnp.where(even, pltpu.roll(q, 127, 1), pltpu.roll(q, 1, 1)), zero)

    def add_rest(ref, e, kind):
        r_rows, r_cols, r_yz = faces[e][9:12]
        for n in range(32):
            after, before = r_rows[1, kind, n : n + 1, :], r_rows[0, kind, n : n + 1, :]
            if 0 < n < 31 and n % 8 in (0, 7):
                other = n + 1 if n % 8 == 7 else n - 1
                after = after + r_rows[1, kind, other : other + 1, :]
                before = before + r_rows[0, kind, other : other + 1, :]
            ref[n, 0:1, :] = ref[n, 0:1, :] + after
            ref[n, 63:64, :] = ref[n, 63:64, :] + before
        across = [
            across_azimuth(jnp.where(even, r_yz[py, 1, kind], r_yz[py, 0, kind]), py)
            for py in (0, 1)
        ]
        found = [None] * 4
        for at, a in enumerate(AXIAL):
            q = jnp.where(even, r_cols[1, at, kind], r_cols[0, at, kind])
            q = q + jnp.where(sub == 0, jnp.broadcast_to(across[1][at : at + 1, :], (8, 128)), zero)
            q = q + jnp.where(sub == 7, jnp.broadcast_to(across[0][at : at + 1, :], (8, 128)), zero)
            found[a] = q
        for a in range(4):
            q = found[a]
            if a < 3:
                q = q + jnp.where(lane >= 112, pltpu.roll(found[a + 1], 112, 1), zero)
            if a > 0:
                q = q + jnp.where(lane < 16, pltpu.roll(found[a - 1], 16, 1), zero)
            xcol[kind, a] = swap(q)

    def add_ends(ref, e, kind):
        r_plane, r_xy, r_xz, r_xyz = faces[e][5:9]
        for px in (0, 1):
            n, a = (0, 0) if px else (31, 3)
            ref[n] = ref[n] + r_plane[px, kind]
            for py in (0, 1):
                row, got = (0, 7) if py else (63, 0)
                ref[n, row : row + 1, :] = (
                    ref[n, row : row + 1, :] + r_xy[px, py, kind, got : got + 1, :]
                )
            q = jnp.where(even, r_xz[px, 1, kind], r_xz[px, 0, kind])
            for py in (0, 1):
                c = jnp.where(even, r_xyz[px, py, 1, kind], r_xyz[px, py, 0, kind])
                c = pltpu.roll(across_azimuth(c, py), 1 if py else 7, 0)
                q = q + jnp.where(sub == (0 if py else 7), c, zero)
            if px:
                q = jnp.where(lane < 16, pltpu.roll(q, 16, 1), zero)
            else:
                q = jnp.where(lane >= 112, pltpu.roll(q, 112, 1), zero)
            xcol[kind, a] = xcol[kind, a] + swap(q)

    def total(ref, x, n, i, b):
        spot = 8 * i + b
        return ref[n, 8 * b : 8 * b + 8, :] + jnp.where(
            edge, pltpu.roll(x, 127 - 2 * spot, 1), zero
        )

    def along_radius(block):
        high = block.astype(BF16)
        low = (block - high.astype(F32)).astype(BF16)
        both = jnp.dot(
            jnp.concatenate([high, low], axis=1), tab[...], preferred_element_type=F32
        )
        return both[:, :128] + both[:, 128:]

    def along_azimuth(f):
        turned = azi[0] * f
        for d in range(1, 8):
            turned = turned + azi[d] * pltpu.roll(f, 8 - d, 0)
        return turned

    def convect_plane(src, e, px):
        n, i = 31 * px, 7 * px
        plane = faces[e][0].at[px, 0]
        turning = along_radius(src[n])
        for b in range(8):
            part = slice(8 * b, 8 * b + 8)
            axial = None
            for p in range(8):
                term = float(DERIV[i, p]) * src[n - i + p, part, :]
                axial = term if axial is None else axial + term
            c = (
                vel[0, n, part, :] * axial
                + vel[1, n, part, :] * along_azimuth(src[n, part, :])
                + vel[2, n, part, :] * turning[part, :]
            )
            plane[part, :] = lane_pairs(mass[n, part, :] * c)
        pair_plane(plane)

    def convect(src, a, e, slot):
        parts = [zero] * 4
        radial[...] = along_radius(src[pl.ds(8 * a, 8)].reshape(512, 128)).reshape(8, 64, 128)
        for b in range(0, 8, 2):
            pieces = []
            for d in (b, b + 1):
                block = src[pl.ds(8 * a, 8), 8 * d : 8 * d + 8, :].reshape(64, 128)
                high = block.astype(BF16)
                low = (block - high.astype(F32)).astype(BF16)
                pieces.append(jnp.concatenate([high, low, high], axis=0))
            both = jnp.dot(
                cross[...], jnp.concatenate(pieces, axis=1), preferred_element_type=F32
            )
            for d in (0, 1):
                part = slice(8 * (b + d), 8 * (b + d) + 8)
                lanes = slice(128 * d, 128 * d + 128)
                for i in range(8):
                    n = 8 * a + i
                    c = (
                        vel[0, n, part, :] * both[64 + 8 * i : 72 + 8 * i, lanes]
                        + vel[1, n, part, :] * both[8 * i : 8 * i + 8, lanes]
                        + vel[2, n, part, :] * radial[i, part, :]
                    )
                    g = mass[n, part, :] * c
                    pick(parts, 8 * i + b + d, g)
                    g_ref[n, part, :] = lane_pairs(g)
        put_columns(parts, e, 0, slot)
        pair_azimuth(g_ref, a)

    for pz in (0, 1):

        @pl.when(jnp.logical_not(has_lower if pz else has_upper))
        def _(pz=pz):
            for _, _, _, _, _, _, _, r_xz, r_xyz, _, r_cols, r_yz in faces:
                r_cols[pz] = jnp.zeros(r_cols.shape[1:], F32)
                for px in (0, 1):
                    r_xz[px, pz] = jnp.zeros(r_xz.shape[2:], F32)
                    r_yz[px, pz] = jnp.zeros(r_yz.shape[2:], F32)
                    for py in (0, 1):
                        r_xyz[px, py, pz] = jnp.zeros(r_xyz.shape[3:], F32)

    load_mass.wait()

    @twice
    def sum_mass(a, slot):
        parts = [zero] * 4
        for i in range(8):
            for b in range(8):
                n, part = 8 * a + i, slice(8 * b, 8 * b + 8)
                pick(parts, 8 * i + b, mass[n, part, :])
                winv[n, part, :] = lane_pairs(mass[n, part, :])
        put_columns(parts, 0, 1, slot)
        pair_azimuth(winv, a)

    sum_mass("ends")
    sum_mass("middle")
    for px in (0, 1):
        faces[0][0][px, 1] = winv[31 * px]
    pack_ends(0, 1)
    pack_lines(0, 1)
    pack_rows(winv, 0, 1)
    pair_axial(winv)

    load_fld.wait()
    load_tab.wait()
    load_azi.wait()
    load_cross.wait()

    def wait_velocity(a):
        part = pl.ds(8 * a, 8)
        pltpu.make_async_copy(vel_h.at[:, part], vel.at[:, part], vel_sem.at[a]).wait()

    for px in (0, 1):
        wait_velocity(3 * px)
        convect_plane(fld, 0, px)
    pack_ends(0, 0)
    pl.semaphore_wait(barrier, 26 + n_cam - 3)
    send_ends(0)
    wait_velocity(1)
    wait_velocity(2)

    @twice
    def stage_one(a, slot):
        convect(fld, a, 0, slot)

    stage_one("middle")
    send_columns(0, 0)
    stage_one("ends")
    send_columns(0, 1)
    pack_lines(0, 0)
    send_lines(0)
    pack_rows(g_ref, 0, 0)
    send_rows(0)
    pair_axial(g_ref)

    load_blk.wait()
    blk_copies = []
    for d in range(1, n_cam):
        copy = pltpu.make_async_remote_copy(
            src_ref=blk,
            dst_ref=blk_recv.at[d],
            send_sem=b_send_sem.at[d],
            recv_sem=b_recv_sem.at[d],
            device_id=along_cam(d),
            device_id_type=pl.DeviceIdType.MESH,
        )
        copy.start()
        blk_copies.append(copy)

    load_cut.wait()
    load_wts.wait()

    @pl.loop(0, 8)
    def _(m):
        wide[...] = wts[m].astype(F32)
        for k in range(8):
            wts_p[m, 64 * k : 64 * k + 64, :] = wide[pl.ds(k, 64, stride=8), :].astype(BF16)
        chosen = jnp.broadcast_to(cut[pl.ds(m, 1), :].astype(F32), (128, 128)).T
        place = lax.broadcasted_iota(jnp.int32, (128, 128), 1).astype(F32)
        for q in range(4):
            cut_hot[m // 2, pl.ds(128 * (m % 2), 128), 128 * q : 128 * q + 128] = jnp.where(
                chosen == place + 128.0 * q, 1.0, 0.0
            ).astype(BF16)

    @twice
    def step_one(a, _):
        x, y = xcol[0, a], xcol[1, a]
        for i in range(8):
            for b in range(8):
                n, part = 8 * a + i, slice(8 * b, 8 * b + 8)
                factor = -STEP * pl.reciprocal(total(winv, y, n, i, b))
                winv[n, part, :] = factor
                first[n, part, :] = fld[n, part, :] + factor * total(g_ref, x, n, i, b)

    @twice
    def stage_two(a, slot):
        convect(first, a, 1, slot)

    wait_all(0, ("ends", "rest"), True)
    for ref, kind in ((winv, 1), (g_ref, 0)):
        add_rest(ref, 0, kind)
        add_ends(ref, 0, kind)
    step_one("ends")
    for px in (0, 1):
        convect_plane(first, 1, px)
    pack_ends(1, 0)
    send_ends(1)
    step_one("middle")
    stage_two("middle")
    send_columns(1, 0)
    stage_two("ends")
    send_columns(1, 1)
    pack_lines(1, 0)
    send_lines(1)
    pack_rows(g_ref, 1, 0)
    send_rows(1)
    pair_axial(g_ref)

    for copy in blk_copies:
        copy.wait_recv()
    for d in range(n_cam):
        for t in range(2):
            if d == 0:
                ids = blk[pl.ds(2 * cam + t, 1), :]
            else:
                ids = blk_recv[d, pl.ds(2 * cam + t, 1), :]
            ids = jnp.broadcast_to(ids, (128, 128))
            for h in range(8):
                block_id = lax.broadcasted_iota(jnp.int32, (128, 128), 0) + 128 * h
                img_hot[t, 128 * h : 128 * h + 128, 128 * d : 128 * d + 128] = jnp.where(
                    ids == block_id, 1.0, 0.0
                ).astype(BF16)

    wide_lane = lax.broadcasted_iota(jnp.int32, (64, 128), 1)
    row64 = lax.broadcasted_iota(jnp.int32, (64, 128), 0)
    select = jnp.where(
        (wide_lane // 8 == row64 % 16) & ((wide_lane % 8) // 2 == row64 // 16), 1.0, 0.0
    ).astype(BF16)

    @twice
    def finish(a, _):
        x = xcol[0, a]
        for i in range(8):
            for b in range(8):
                n, part = 8 * a + i, slice(8 * b, 8 * b + 8)
                second = first[n, part, :] + winv[n, part, :] * total(g_ref, x, n, i, b)
                adv[n, part, :] = 0.5 * (fld[n, part, :] + second)
        for b in range(0, 8, 2):
            pieces = []
            for c in (b, b + 1):
                block = adv[pl.ds(8 * a, 8), 8 * c : 8 * c + 8, :].reshape(64, 128)
                pieces.append(jnp.where(wide_lane % 2 == 0, block, 0.0).astype(BF16))
                pieces.append(jnp.where(wide_lane % 2 == 1, block, 0.0).astype(BF16))
            out = lax.dot_general(
                select,
                jnp.concatenate(pieces, axis=0),
                (((1,), (1,)), ((), ())),
                preferred_element_type=F32,
            ).astype(BF16)
            for c in (0, 1):
                at = pl.multiple_of(128 * a + 16 * (b + c), 16)
                for h in range(4):
                    elems[pl.ds(at, 16), 128 * h : 128 * h + 128] = out[
                        16 * h : 16 * h + 16, 128 * c : 128 * c + 128
                    ]

    wait_all(1, ("rest",), True)
    add_rest(g_ref, 1, 0)
    finish("middle")
    wait_all(1, ("ends",), True)
    add_ends(g_ref, 1, 0)
    finish("ends")

    v_copies = []
    for d in sorted(range(1, n_cam), key=lambda d: -min(d, n_cam - d)) + [0]:
        q = camera_owner(d)
        picked = jnp.dot(cut_hot[q], elems[...], preferred_element_type=F32).astype(BF16)
        for t in range(2):
            value = jnp.dot(
                picked[128 * t : 128 * t + 128], wts_p[2 * q + t], preferred_element_type=F32
            ).astype(BF16)
            if d:
                v_send[d, t] = value
            else:
                v_recv[0, t] = value
        if d:
            copy = pltpu.make_async_remote_copy(
                src_ref=v_send.at[d],
                dst_ref=v_recv.at[d],
                send_sem=v_send_sem.at[d],
                recv_sem=v_recv_sem.at[d],
                device_id=along_cam(d),
                device_id_type=pl.DeviceIdType.MESH,
            )
            copy.start()
            v_copies.append(copy)

    for e in (0, 1):
        wait_all(e, ("ends", "rest"), False)
    for copy in blk_copies:
        copy.wait_send()
    for copy in v_copies:
        copy.wait_recv()
    for copy in v_copies:
        copy.wait_send()


def write_kernel(adv, values, img_hot, adv_h, img_h, img, sem):
    result = pltpu.make_async_copy(adv, adv_h, sem.at[0])
    result.start()
    n_cam = values.shape[0]
    copies = []
    for t in range(2):
        slots = jnp.concatenate([values[d, t] for d in range(n_cam)], axis=0)
        for h in range(2):
            part = pl.ds(h * (NBLK // 2), NBLK // 2)
            img[t, part] = jnp.dot(img_hot[t, part], slots, preferred_element_type=F32)
            copy = pltpu.make_async_copy(
                img.at[t, part], img_h.at[t, part], sem.at[1 + 2 * t + h]
            )
            copy.start()
            copies.append(copy)
    for copy in copies:
        copy.wait()
    result.wait()


def face_buffers(kinds):
    shapes = [
        (2, kinds, 64, 128),
        (2, kinds, 8, 128),
        (2, kinds, 32, 128),
        (4, kinds, 8, 128),
        (2, kinds, 8, 128),
        (2, kinds, 64, 128),
        (2, 2, kinds, 8, 128),
        (2, 2, kinds, 8, 128),
        (2, 2, 2, kinds, 8, 128),
        (2, kinds, 32, 128),
        (2, 4, kinds, 8, 128),
        (2, 2, kinds, 8, 128),
    ]
    return tuple(pltpu.VMEM(shape, F32) for shape in shapes)


def per_device(sizes, scalar, velocity, lumped_mass, pixel_weights, cut_element, pixel_block):
    n_cam = sizes[0]
    flat = (32, 64, 128)
    hbm = pl.BlockSpec(memory_space=pltpu.HBM)
    big = pltpu.VMEM(flat, F32)
    dma = pltpu.SemaphoreType.DMA
    on_chip = pl.BlockSpec(memory_space=pltpu.VMEM)
    outputs = (
        pltpu.VMEM(flat, F32),
        pltpu.VMEM((n_cam, 2, 128, 128), BF16),
        pltpu.VMEM((2, NBLK, 128 * n_cam), BF16),
    )
    operands = (
        scalar.reshape(flat),
        velocity.reshape((3,) + flat),
        lumped_mass.reshape(flat),
        pixel_weights,
        cut_element,
        pixel_block,
        jnp.asarray(radial_matrix()),
        jnp.asarray(azimuth_table()),
        jnp.asarray(cross_matrix()),
    )
    results = pl.pallas_call(
        functools.partial(kernel, sizes),
        out_shape=outputs,
        in_specs=[hbm] * 9,
        out_specs=(on_chip,) * 3,
        scratch_shapes=[
            big,
            pltpu.VMEM((3,) + flat, F32),
            big,
            pltpu.VMEM((8, 512, 128), BF16),
            pltpu.VMEM((8, 128), jnp.int32),
            pltpu.VMEM((8, 128), jnp.int32),
            pltpu.VMEM((256, 256), BF16),
            pltpu.VMEM((8, 8, 128), F32),
            pltpu.VMEM((128, 192), BF16),
            big,
            big,
            big,
            pltpu.VMEM((8, 64, 128), F32),
            face_buffers(2),
            face_buffers(1),
            pltpu.VMEM((2, 4, 8, 128), F32),
            pltpu.VMEM((512, 128), F32),
            pltpu.VMEM((8, 512, 128), BF16),
            pltpu.VMEM((4, 256, 512), BF16),
            pltpu.VMEM((512, 512), BF16),
            pltpu.VMEM((n_cam, 2, 128, 128), BF16),
            pltpu.VMEM((n_cam, 8, 128), jnp.int32),
            dma((8,)),
            dma((4,)),
            dma((58,)),
            dma((58,)),
            dma((n_cam,)),
            dma((n_cam,)),
            dma((n_cam,)),
            dma((n_cam,)),
        ],
        compiler_params=pltpu.CompilerParams(
            collective_id=0, has_side_effects=True, vmem_limit_bytes=40 * 1024 * 1024
        ),
    )(*[pltpu.with_memory_space_constraint(x, pltpu.HBM) for x in operands])
    advected, images = pl.pallas_call(
        write_kernel,
        out_shape=(
            jax.ShapeDtypeStruct(flat, F32),
            jax.ShapeDtypeStruct((2, NBLK, 128), F32),
        ),
        in_specs=[on_chip] * 3,
        out_specs=(hbm, hbm),
        scratch_shapes=[pltpu.VMEM((2, NBLK, 128), F32), dma((5,))],
        compiler_params=pltpu.CompilerParams(vmem_limit_bytes=16 * 1024 * 1024),
    )(*[pltpu.with_memory_space_constraint(x, pltpu.VMEM) for x in results])
    return advected.reshape(scalar.shape), images


def solution(mesh):
    sizes = tuple(mesh.shape[name] for name in ("cam", "ex", "ey"))
    placed = (
        P("ex", None, "ey", None, "cam"),
        P(None, "ex", None, "ey", None, "cam"),
        P("ex", None, "ey", None, "cam"),
        P(),
        P(None, ("cam", "ex", "ey")),
        P(None, ("cam", "ex", "ey")),
    )
    return jax.shard_map(
        functools.partial(per_device, sizes),
        mesh=mesh,
        in_specs=placed,
        out_specs=(P("ex", None, "ey", None, "cam"), P("cam", ("ex", "ey"), None)),
        check_vma=False,
    )
```

```python
import functools

import jax
import jax.numpy as jnp
import ml_dtypes
import numpy as np
from jax import lax
from jax.experimental import pallas as pl
from jax.experimental.pallas import tpu as pltpu
from jax.sharding import PartitionSpec as P

NBLK = 1024
STEP = 0.01
F32 = jnp.float32
BF16 = jnp.bfloat16


def legendre_seven(points):
    previous = points * 0.0 + 1.0
    current = points * 1.0
    for order in range(1, 7):
        following = ((2 * order + 1) * points * current - order * previous) / (order + 1)
        previous = current
        current = following
    return current


def gll_derivative():
    degree = 7
    gll_nodes = np.array(
        [
            -1.0,
            -0.8717401485096066,
            -0.5917001814331423,
            -0.2092992179024789,
            0.2092992179024789,
            0.5917001814331423,
            0.8717401485096066,
            1.0,
        ]
    )
    values = legendre_seven(gll_nodes)
    derivative = np.zeros((degree + 1, degree + 1))
    for target in range(degree + 1):
        for source in range(degree + 1):
            if target != source:
                derivative[target, source] = values[target] / (
                    values[source] * (gll_nodes[target] - gll_nodes[source])
                )
    derivative[0, 0] = -degree * (degree + 1) / 4.0
    derivative[degree, degree] = degree * (degree + 1) / 4.0
    return derivative


DERIV = gll_derivative()


def radial_matrix():
    table = np.kron(np.eye(16), DERIV.T).astype(np.float32)
    high = table.astype(ml_dtypes.bfloat16)
    low = (table - high.astype(np.float32)).astype(ml_dtypes.bfloat16)
    return np.block([[high, low], [high, np.zeros_like(low)]])


def cross_matrix():
    table = np.concatenate([np.kron(np.eye(8), DERIV), np.kron(DERIV, np.eye(8))])
    table = table.astype(np.float32)
    high = table.astype(ml_dtypes.bfloat16)
    low = (table - high.astype(np.float32)).astype(ml_dtypes.bfloat16)
    return np.concatenate([high, high, low], axis=1)


def azimuth_table():
    rows = np.arange(8)
    shifts = np.stack([DERIV[rows, (rows + d) % 8] for d in range(8)])
    return np.broadcast_to(shifts[:, :, None], (8, 8, 128)).astype(np.float32)


AXIAL = (1, 2, 0, 3)

SIGNS = [
    (sx, sy, sz)
    for sx in (-1, 0, 1)
    for sy in (-1, 0, 1)
    for sz in (-1, 0, 1)
    if (sx, sy, sz) != (0, 0, 0)
]


def kernel(
    sizes,
    scalar_h,
    vel_h,
    mass_h,
    wts_h,
    cut_h,
    blk_h,
    tab_h,
    azi_h,
    cross_h,
    adv,
    v_recv,
    img_hot,
    fld,
    vel,
    side,
    mass,
    wts,
    cut,
    blk,
    tab,
    azi,
    cross,
    g_ref,
    first,
    winv,
    radial,
    faces_one,
    faces_two,
    xcol,
    wide,
    wts_p,
    cut_hot,
    elems,
    v_send,
    blk_recv,
    in_sem,
    vel_sem,
    send_sem,
    recv_sem,
    v_send_sem,
    v_recv_sem,
    b_send_sem,
    b_recv_sem,
):
    n_cam, n_ex, n_ey = sizes
    cam, ex, ey = lax.axis_index("cam"), lax.axis_index("ex"), lax.axis_index("ey")
    faces = (faces_one, faces_two)

    def beside(at, size):
        return {
            0: at,
            1: jnp.where(at == size - 1, 0, at + 1),
            -1: jnp.where(at == 0, size - 1, at - 1),
        }

    cams, exs, eys = beside(cam, n_cam), beside(ex, n_ex), beside(ey, n_ey)
    peers = {s: {"cam": cams[s[2]], "ex": exs[s[0]], "ey": eys[s[1]]} for s in SIGNS}

    def camera_owner(d):
        return jnp.where(cam + d >= n_cam, cam + d - n_cam, cam + d)

    def along_cam(d):
        return {"cam": camera_owner(d), "ex": ex, "ey": ey}

    def load(src, dst, sem):
        copy = pltpu.make_async_copy(src, dst, sem)
        copy.start()
        return copy

    load_mass = load(mass_h, mass, in_sem.at[0])
    load_fld = load(scalar_h, fld, in_sem.at[1])
    load_tab = load(tab_h, tab, in_sem.at[2])
    load_azi = load(azi_h, azi, in_sem.at[3])
    load_cross = load(cross_h, cross, in_sem.at[7])

    def load_vel(a):
        load(vel_h.at[:, pl.ds(8 * a, 8)], vel.at[:, pl.ds(8 * a, 8)], vel_sem.at[a])

    load_sides = [
        load(vel_h.at[:, pl.ds(31 * px, 1)], side.at[px], vel_sem.at[4 + px]) for px in (0, 1)
    ]
    barrier = pltpu.get_barrier_semaphore()
    for s in sorted(SIGNS, key=lambda s: (-abs(s[0]), -abs(s[2]), -abs(s[1]))):
        pl.semaphore_signal(barrier, inc=1, device_id=peers[s], device_id_type=pl.DeviceIdType.MESH)
    for d in range(2, n_cam - 1):
        pl.semaphore_signal(
            barrier, inc=1, device_id=along_cam(d), device_id_type=pl.DeviceIdType.MESH
        )
    load_blk = load(blk_h, blk, in_sem.at[4])
    load_cut = load(cut_h, cut, in_sem.at[5])

    lane = lax.broadcasted_iota(jnp.int32, (8, 128), 1)
    sub = lax.broadcasted_iota(jnp.int32, (8, 128), 0)
    even = lane % 2 == 0
    take_next = (lane % 8 == 7) & (lane != 127)
    take_prev = (lane % 8 == 0) & (lane != 0)
    edge = (lane == 0) | (lane == 127)
    zero = jnp.zeros((8, 128), F32)
    has_upper, has_lower = cam < n_cam - 1, cam > 0
    from_upper = jnp.where(has_upper, 1.0, 0.0).astype(F32)
    from_lower = jnp.where(has_lower, 1.0, 0.0).astype(F32)
    keep = jnp.where(even, jnp.full((8, 128), from_upper), jnp.full((8, 128), from_lower)) > 0.5

    def lane_pairs(g):
        return (
            g
            + jnp.where(take_next, pltpu.roll(g, 127, 1), zero)
            + jnp.where(take_prev, pltpu.roll(g, 1, 1), zero)
        )

    def twice(body):
        def outer(which):
            @pl.loop(0, 2)
            def _(t):
                body(*((3 * t, 2 + t) if which == "ends" else (1 + t, t)))

        return outer

    copies = []

    def send(src, dst, e, group, slot, s):
        copy = pltpu.make_async_remote_copy(
            src_ref=src,
            dst_ref=dst,
            send_sem=send_sem.at[slot],
            recv_sem=recv_sem.at[slot],
            device_id=peers[s],
            device_id_type=pl.DeviceIdType.MESH,
        )
        copies.append((e, group, s[2], copy))
        if s[2] == 0:
            copy.start()

    def toward(sz, body):
        pl.when(has_upper if sz > 0 else has_lower)(body)

    def launch(sz, body):
        first_new = len(copies)
        body()
        chosen = [copy for _, _, _, copy in copies[first_new:]]

        def start():
            for copy in chosen:
                copy.start()

        toward(sz, start)

    def wait_all(e, groups, received):
        for sz in (0, -1, 1):
            chosen = [c for at, group, z, c in copies if at == e and group in groups and z == sz]

            def body(chosen=chosen):
                for copy in chosen:
                    if received:
                        copy.wait_recv()
                    else:
                        copy.wait_send()

            if sz == 0:
                body()
            else:
                toward(-sz if received else sz, body)

    def pair_azimuth(ref, a):
        for i in range(8):
            n = 8 * a + i
            both = ref[n, pl.ds(7, 7, stride=8), :] + ref[n, pl.ds(8, 7, stride=8), :]
            ref[n, pl.ds(7, 7, stride=8), :] = both
            ref[n, pl.ds(8, 7, stride=8), :] = both

    def pair_axial(ref):
        for a in range(3):
            both = ref[8 * a + 7] + ref[8 * a + 8]
            ref[8 * a + 7] = both
            ref[8 * a + 8] = both

    def gather_columns(pieces):
        parts = [zero] * 4
        for at, (spot, piece) in enumerate(pieces):
            here = (lane == 2 * spot) | (lane == 2 * spot + 1)
            parts[at % 4] = jnp.where(here, pltpu.roll(piece, 2 * spot + 1, 1), parts[at % 4])
        return (parts[0] + parts[1]) + (parts[2] + parts[3])

    def pair_plane(plane):
        both = plane[pl.ds(7, 7, stride=8), :] + plane[pl.ds(8, 7, stride=8), :]
        plane[pl.ds(7, 7, stride=8), :] = both
        plane[pl.ds(8, 7, stride=8), :] = both

    def pack_ends(e, kind):
        plane, tile = faces[e][0], faces[e][1]
        for px in (0, 1):
            tile[px, kind] = gather_columns(
                [(56 * px + b, plane[px, kind, 8 * b : 8 * b + 8, :]) for b in range(8)]
            )

    def send_ends(e):
        plane, tile, _, _, _, r_plane, r_xy, r_xz, r_xyz, _, _, _ = faces[e]
        base = 30 * e
        for px in (0, 1):
            sx = 2 * px - 1
            send(plane.at[px], r_plane.at[px], e, "ends", base + px, (sx, 0, 0))
            for py in (0, 1):
                send(
                    plane.at[px, :, pl.ds(56 * py, 8)],
                    r_xy.at[px, py],
                    e,
                    "ends",
                    base + 2 + 2 * px + py,
                    (sx, 2 * py - 1, 0),
                )
        for pz in (0, 1):
            sz = 2 * pz - 1

            def body(pz=pz, sz=sz):
                for px in (0, 1):
                    sx = 2 * px - 1
                    slot = base + 6 + 6 * pz + 3 * px
                    send(tile.at[px], r_xz.at[px, pz], e, "ends", slot, (sx, 0, sz))
                    for py in (0, 1):
                        send(
                            tile.at[px],
                            r_xyz.at[px, py, pz],
                            e,
                            "ends",
                            slot + 1 + py,
                            (sx, 2 * py - 1, sz),
                        )

            launch(sz, body)

    def pick(parts, spot, piece):
        here = (lane == 2 * spot) | (lane == 2 * spot + 1)
        parts[spot % 4] = jnp.where(here, pltpu.roll(piece, 2 * spot + 1, 1), parts[spot % 4])

    def put_columns(parts, e, kind, slot):
        q = (parts[0] + parts[1]) + (parts[2] + parts[3])
        after = pltpu.roll(pltpu.roll(q, 126, 1), 7, 0)
        before = pltpu.roll(pltpu.roll(q, 2, 1), 1, 0)
        q = q + jnp.where((sub == 7) & (lane % 16 < 14), after, zero)
        q = q + jnp.where((sub == 0) & (lane % 16 >= 2), before, zero)
        faces[e][3][slot, kind] = q

    def send_columns(e, half):
        cols, r_cols = faces[e][3], faces[e][10]
        for pz in (0, 1):
            sz = 2 * pz - 1

            def body(pz=pz, sz=sz):
                part = pl.ds(2 * half, 2)
                send(
                    cols.at[part],
                    r_cols.at[pz, part],
                    e,
                    "rest",
                    30 * e + 18 + 2 * pz + half,
                    (0, 0, sz),
                )

            launch(sz, body)

    def pack_lines(e, kind):
        cols, lines = faces[e][3], faces[e][4]
        low, high = zero, zero
        for at in range(4):
            low = jnp.where(sub == at, jnp.broadcast_to(cols[at, kind, 0:1, :], (8, 128)), low)
            high = jnp.where(sub == at, jnp.broadcast_to(cols[at, kind, 7:8, :], (8, 128)), high)
        lines[0, kind] = low
        lines[1, kind] = high

    def send_lines(e):
        lines, r_yz = faces[e][4], faces[e][11]
        for pz in (0, 1):
            sz = 2 * pz - 1

            def body(pz=pz, sz=sz):
                for py in (0, 1):
                    send(
                        lines.at[py],
                        r_yz.at[py, pz],
                        e,
                        "rest",
                        30 * e + 22 + 2 * pz + py,
                        (0, 2 * py - 1, sz),
                    )

            launch(sz, body)

    def pack_rows(ref, e, kind):
        rows = faces[e][2]
        for n in range(32):
            rows[0, kind, n : n + 1, :] = ref[n, 0:1, :]
            rows[1, kind, n : n + 1, :] = ref[n, 63:64, :]

    def send_rows(e):
        rows, r_rows = faces[e][2], faces[e][9]
        for py in (0, 1):
            send(rows.at[py], r_rows.at[py], e, "rest", 30 * e + 26 + py, (0, 2 * py - 1, 0))

    def across_azimuth(t, py):
        t = pltpu.roll(t, 114 if py else 14, 1)
        return jnp.where((lane % 16 < 2) if py else (lane % 16 >= 14), t, zero)

    def swap(q):
        return jnp.where(keep, jnp.where(even, pltpu.roll(q, 127, 1), pltpu.roll(q, 1, 1)), zero)

    def add_rest(ref, e, kind):
        r_rows, r_cols, r_yz = faces[e][9:12]
        for n in range(32):
            after, before = r_rows[1, kind, n : n + 1, :], r_rows[0, kind, n : n + 1, :]
            if 0 < n < 31 and n % 8 in (0, 7):
                other = n + 1 if n % 8 == 7 else n - 1
                after = after + r_rows[1, kind, other : other + 1, :]
                before = before + r_rows[0, kind, other : other + 1, :]
            ref[n, 0:1, :] = ref[n, 0:1, :] + after
            ref[n, 63:64, :] = ref[n, 63:64, :] + before
        across = [
            across_azimuth(jnp.where(even, r_yz[py, 1, kind], r_yz[py, 0, kind]), py)
            for py in (0, 1)
        ]
        found = [None] * 4
        for at, a in enumerate(AXIAL):
            q = jnp.where(even, r_cols[1, at, kind], r_cols[0, at, kind])
            q = q + jnp.where(sub == 0, jnp.broadcast_to(across[1][at : at + 1, :], (8, 128)), zero)
            q = q + jnp.where(sub == 7, jnp.broadcast_to(across[0][at : at + 1, :], (8, 128)), zero)
            found[a] = q
        for a in range(4):
            q = found[a]
            if a < 3:
                q = q + jnp.where(lane >= 112, pltpu.roll(found[a + 1], 112, 1), zero)
            if a > 0:
                q = q + jnp.where(lane < 16, pltpu.roll(found[a - 1], 16, 1), zero)
            xcol[kind, a] = swap(q)

    def add_ends(ref, e, kind):
        r_plane, r_xy, r_xz, r_xyz = faces[e][5:9]
        for px in (0, 1):
            n, a = (0, 0) if px else (31, 3)
            ref[n] = ref[n] + r_plane[px, kind]
            for py in (0, 1):
                row, got = (0, 7) if py else (63, 0)
                ref[n, row : row + 1, :] = (
                    ref[n, row : row + 1, :] + r_xy[px, py, kind, got : got + 1, :]
                )
            q = jnp.where(even, r_xz[px, 1, kind], r_xz[px, 0, kind])
            for py in (0, 1):
                c = jnp.where(even, r_xyz[px, py, 1, kind], r_xyz[px, py, 0, kind])
                c = pltpu.roll(across_azimuth(c, py), 1 if py else 7, 0)
                q = q + jnp.where(sub == (0 if py else 7), c, zero)
            if px:
                q = jnp.where(lane < 16, pltpu.roll(q, 16, 1), zero)
            else:
                q = jnp.where(lane >= 112, pltpu.roll(q, 112, 1), zero)
            xcol[kind, a] = xcol[kind, a] + swap(q)

    def total(ref, x, n, i, b):
        spot = 8 * i + b
        return ref[n, 8 * b : 8 * b + 8, :] + jnp.where(
            edge, pltpu.roll(x, 127 - 2 * spot, 1), zero
        )

    def along_radius(block):
        high = block.astype(BF16)
        low = (block - high.astype(F32)).astype(BF16)
        both = jnp.dot(
            jnp.concatenate([high, low], axis=1), tab[...], preferred_element_type=F32
        )
        return both[:, :128] + both[:, 128:]

    def along_azimuth(f):
        turned = azi[0] * f
        for d in range(1, 8):
            turned = turned + azi[d] * pltpu.roll(f, 8 - d, 0)
        return turned

    def convect_plane(src, e, px):
        n, i = 31 * px, 7 * px
        plane = faces[e][0].at[px, 0]
        turning = along_radius(src[n])
        for b in range(8):
            part = slice(8 * b, 8 * b + 8)
            axial = None
            for p in range(8):
                term = float(DERIV[i, p]) * src[n - i + p, part, :]
                axial = term if axial is None else axial + term
            c = (
                side[px, 0, 0, part, :] * axial
                + side[px, 1, 0, part, :] * along_azimuth(src[n, part, :])
                + side[px, 2, 0, part, :] * turning[part, :]
            )
            plane[part, :] = lane_pairs(mass[n, part, :] * c)
        pair_plane(plane)

    def convect(src, a, e, slot):
        parts = [zero] * 4
        radial[...] = along_radius(src[pl.ds(8 * a, 8)].reshape(512, 128)).reshape(8, 64, 128)
        for b in range(0, 8, 2):
            pieces = []
            for d in (b, b + 1):
                block = src[pl.ds(8 * a, 8), 8 * d : 8 * d + 8, :].reshape(64, 128)
                high = block.astype(BF16)
                low = (block - high.astype(F32)).astype(BF16)
                pieces.append(jnp.concatenate([high, low, high], axis=0))
            both = jnp.dot(
                cross[...], jnp.concatenate(pieces, axis=1), preferred_element_type=F32
            )
            for d in (0, 1):
                part = slice(8 * (b + d), 8 * (b + d) + 8)
                lanes = slice(128 * d, 128 * d + 128)
                for i in range(8):
                    n = 8 * a + i
                    c = (
                        vel[0, n, part, :] * both[64 + 8 * i : 72 + 8 * i, lanes]
                        + vel[1, n, part, :] * both[8 * i : 8 * i + 8, lanes]
                        + vel[2, n, part, :] * radial[i, part, :]
                    )
                    g = mass[n, part, :] * c
                    pick(parts, 8 * i + b + d, g)
                    g_ref[n, part, :] = lane_pairs(g)
        put_columns(parts, e, 0, slot)
        pair_azimuth(g_ref, a)

    for pz in (0, 1):

        @pl.when(jnp.logical_not(has_lower if pz else has_upper))
        def _(pz=pz):
            for _, _, _, _, _, _, _, r_xz, r_xyz, _, r_cols, r_yz in faces:
                r_cols[pz] = jnp.zeros(r_cols.shape[1:], F32)
                for px in (0, 1):
                    r_xz[px, pz] = jnp.zeros(r_xz.shape[2:], F32)
                    r_yz[px, pz] = jnp.zeros(r_yz.shape[2:], F32)
                    for py in (0, 1):
                        r_xyz[px, py, pz] = jnp.zeros(r_xyz.shape[3:], F32)

    load_mass.wait()
    for a in (1, 2, 0, 3):
        load_vel(a)
    load_wts = load(wts_h, wts, in_sem.at[6])

    @twice
    def sum_mass(a, slot):
        parts = [zero] * 4
        for i in range(8):
            for b in range(8):
                n, part = 8 * a + i, slice(8 * b, 8 * b + 8)
                pick(parts, 8 * i + b, mass[n, part, :])
                winv[n, part, :] = lane_pairs(mass[n, part, :])
        put_columns(parts, 0, 1, slot)
        pair_azimuth(winv, a)

    sum_mass("ends")
    sum_mass("middle")
    for px in (0, 1):
        faces[0][0][px, 1] = winv[31 * px]
    pack_ends(0, 1)
    pack_lines(0, 1)
    pack_rows(winv, 0, 1)
    pair_axial(winv)

    load_fld.wait()
    load_tab.wait()
    load_azi.wait()
    load_cross.wait()

    def wait_velocity(a):
        part = pl.ds(8 * a, 8)
        pltpu.make_async_copy(vel_h.at[:, part], vel.at[:, part], vel_sem.at[a]).wait()

    for px in (0, 1):
        load_sides[px].wait()
        convect_plane(fld, 0, px)
    pack_ends(0, 0)
    pl.semaphore_wait(barrier, 26 + n_cam - 3)
    send_ends(0)
    for a in range(4):
        wait_velocity(a)

    @twice
    def stage_one(a, slot):
        convect(fld, a, 0, slot)

    stage_one("middle")
    send_columns(0, 0)
    stage_one("ends")
    send_columns(0, 1)
    pack_lines(0, 0)
    send_lines(0)
    pack_rows(g_ref, 0, 0)
    send_rows(0)
    pair_axial(g_ref)

    load_blk.wait()
    blk_copies = []
    for d in range(1, n_cam):
        copy = pltpu.make_async_remote_copy(
            src_ref=blk,
            dst_ref=blk_recv.at[d],
            send_sem=b_send_sem.at[d],
            recv_sem=b_recv_sem.at[d],
            device_id=along_cam(d),
            device_id_type=pl.DeviceIdType.MESH,
        )
        copy.start()
        blk_copies.append(copy)

    load_cut.wait()
    load_wts.wait()

    @pl.loop(0, 8)
    def _(m):
        wide[...] = wts[m].astype(F32)
        for k in range(8):
            wts_p[m, 64 * k : 64 * k + 64, :] = wide[pl.ds(k, 64, stride=8), :].astype(BF16)
        chosen = jnp.broadcast_to(cut[pl.ds(m, 1), :].astype(F32), (128, 128)).T
        place = lax.broadcasted_iota(jnp.int32, (128, 128), 1).astype(F32)
        for q in range(4):
            cut_hot[m // 2, pl.ds(128 * (m % 2), 128), 128 * q : 128 * q + 128] = jnp.where(
                chosen == place + 128.0 * q, 1.0, 0.0
            ).astype(BF16)

    @twice
    def step_one(a, _):
        x, y = xcol[0, a], xcol[1, a]
        for i in range(8):
            for b in range(8):
                n, part = 8 * a + i, slice(8 * b, 8 * b + 8)
                factor = -STEP * pl.reciprocal(total(winv, y, n, i, b))
                winv[n, part, :] = factor
                first[n, part, :] = fld[n, part, :] + factor * total(g_ref, x, n, i, b)

    @twice
    def stage_two(a, slot):
        convect(first, a, 1, slot)

    wait_all(0, ("ends", "rest"), True)
    for ref, kind in ((winv, 1), (g_ref, 0)):
        add_rest(ref, 0, kind)
        add_ends(ref, 0, kind)
    step_one("ends")
    for px in (0, 1):
        convect_plane(first, 1, px)
    pack_ends(1, 0)
    send_ends(1)
    step_one("middle")
    stage_two("middle")
    send_columns(1, 0)
    stage_two("ends")
    send_columns(1, 1)
    pack_lines(1, 0)
    send_lines(1)
    pack_rows(g_ref, 1, 0)
    send_rows(1)
    pair_axial(g_ref)

    for copy in blk_copies:
        copy.wait_recv()
    for d in range(n_cam):
        for t in range(2):
            if d == 0:
                ids = blk[pl.ds(2 * cam + t, 1), :]
            else:
                ids = blk_recv[d, pl.ds(2 * cam + t, 1), :]
            ids = jnp.broadcast_to(ids, (128, 128))
            for h in range(8):
                block_id = lax.broadcasted_iota(jnp.int32, (128, 128), 0) + 128 * h
                img_hot[t, 128 * h : 128 * h + 128, 128 * d : 128 * d + 128] = jnp.where(
                    ids == block_id, 1.0, 0.0
                ).astype(BF16)

    wide_lane = lax.broadcasted_iota(jnp.int32, (64, 128), 1)
    row64 = lax.broadcasted_iota(jnp.int32, (64, 128), 0)
    select = jnp.where(
        (wide_lane // 8 == row64 % 16) & ((wide_lane % 8) // 2 == row64 // 16), 1.0, 0.0
    ).astype(BF16)

    @twice
    def finish(a, _):
        x = xcol[0, a]
        for i in range(8):
            for b in range(8):
                n, part = 8 * a + i, slice(8 * b, 8 * b + 8)
                second = first[n, part, :] + winv[n, part, :] * total(g_ref, x, n, i, b)
                adv[n, part, :] = 0.5 * (fld[n, part, :] + second)
        for b in range(0, 8, 2):
            pieces = []
            for c in (b, b + 1):
                block = adv[pl.ds(8 * a, 8), 8 * c : 8 * c + 8, :].reshape(64, 128)
                pieces.append(jnp.where(wide_lane % 2 == 0, block, 0.0).astype(BF16))
                pieces.append(jnp.where(wide_lane % 2 == 1, block, 0.0).astype(BF16))
            out = lax.dot_general(
                select,
                jnp.concatenate(pieces, axis=0),
                (((1,), (1,)), ((), ())),
                preferred_element_type=F32,
            ).astype(BF16)
            for c in (0, 1):
                at = pl.multiple_of(128 * a + 16 * (b + c), 16)
                for h in range(4):
                    elems[pl.ds(at, 16), 128 * h : 128 * h + 128] = out[
                        16 * h : 16 * h + 16, 128 * c : 128 * c + 128
                    ]

    wait_all(1, ("rest",), True)
    add_rest(g_ref, 1, 0)
    finish("middle")
    wait_all(1, ("ends",), True)
    add_ends(g_ref, 1, 0)
    finish("ends")

    v_copies = []
    for d in sorted(range(1, n_cam), key=lambda d: -min(d, n_cam - d)) + [0]:
        q = camera_owner(d)
        picked = jnp.dot(cut_hot[q], elems[...], preferred_element_type=F32).astype(BF16)
        for t in range(2):
            value = jnp.dot(
                picked[128 * t : 128 * t + 128], wts_p[2 * q + t], preferred_element_type=F32
            ).astype(BF16)
            if d:
                v_send[d, t] = value
            else:
                v_recv[0, t] = value
        if d:
            copy = pltpu.make_async_remote_copy(
                src_ref=v_send.at[d],
                dst_ref=v_recv.at[d],
                send_sem=v_send_sem.at[d],
                recv_sem=v_recv_sem.at[d],
                device_id=along_cam(d),
                device_id_type=pl.DeviceIdType.MESH,
            )
            copy.start()
            v_copies.append(copy)

    for e in (0, 1):
        wait_all(e, ("ends", "rest"), False)
    for copy in blk_copies:
        copy.wait_send()
    for copy in v_copies:
        copy.wait_recv()
    for copy in v_copies:
        copy.wait_send()


def write_kernel(adv, values, img_hot, adv_h, img_h, img, sem):
    result = pltpu.make_async_copy(adv, adv_h, sem.at[0])
    result.start()
    n_cam = values.shape[0]
    copies = []
    for t in range(2):
        slots = jnp.concatenate([values[d, t] for d in range(n_cam)], axis=0)
        for h in range(2):
            part = pl.ds(h * (NBLK // 2), NBLK // 2)
            img[t, part] = jnp.dot(img_hot[t, part], slots, preferred_element_type=F32)
            copy = pltpu.make_async_copy(
                img.at[t, part], img_h.at[t, part], sem.at[1 + 2 * t + h]
            )
            copy.start()
            copies.append(copy)
    for copy in copies:
        copy.wait()
    result.wait()


def face_buffers(kinds):
    shapes = [
        (2, kinds, 64, 128),
        (2, kinds, 8, 128),
        (2, kinds, 32, 128),
        (4, kinds, 8, 128),
        (2, kinds, 8, 128),
        (2, kinds, 64, 128),
        (2, 2, kinds, 8, 128),
        (2, 2, kinds, 8, 128),
        (2, 2, 2, kinds, 8, 128),
        (2, kinds, 32, 128),
        (2, 4, kinds, 8, 128),
        (2, 2, kinds, 8, 128),
    ]
    return tuple(pltpu.VMEM(shape, F32) for shape in shapes)


def per_device(sizes, scalar, velocity, lumped_mass, pixel_weights, cut_element, pixel_block):
    n_cam = sizes[0]
    flat = (32, 64, 128)
    hbm = pl.BlockSpec(memory_space=pltpu.HBM)
    big = pltpu.VMEM(flat, F32)
    dma = pltpu.SemaphoreType.DMA
    on_chip = pl.BlockSpec(memory_space=pltpu.VMEM)
    outputs = (
        pltpu.VMEM(flat, F32),
        pltpu.VMEM((n_cam, 2, 128, 128), BF16),
        pltpu.VMEM((2, NBLK, 128 * n_cam), BF16),
    )
    operands = (
        scalar.reshape(flat),
        velocity.reshape((3,) + flat),
        lumped_mass.reshape(flat),
        pixel_weights,
        cut_element,
        pixel_block,
        jnp.asarray(radial_matrix()),
        jnp.asarray(azimuth_table()),
        jnp.asarray(cross_matrix()),
    )
    results = pl.pallas_call(
        functools.partial(kernel, sizes),
        out_shape=outputs,
        in_specs=[hbm] * 9,
        out_specs=(on_chip,) * 3,
        scratch_shapes=[
            big,
            pltpu.VMEM((3,) + flat, F32),
            pltpu.VMEM((2, 3, 1, 64, 128), F32),
            big,
            pltpu.VMEM((8, 512, 128), BF16),
            pltpu.VMEM((8, 128), jnp.int32),
            pltpu.VMEM((8, 128), jnp.int32),
            pltpu.VMEM((256, 256), BF16),
            pltpu.VMEM((8, 8, 128), F32),
            pltpu.VMEM((128, 192), BF16),
            big,
            big,
            big,
            pltpu.VMEM((8, 64, 128), F32),
            face_buffers(2),
            face_buffers(1),
            pltpu.VMEM((2, 4, 8, 128), F32),
            pltpu.VMEM((512, 128), F32),
            pltpu.VMEM((8, 512, 128), BF16),
            pltpu.VMEM((4, 256, 512), BF16),
            pltpu.VMEM((512, 512), BF16),
            pltpu.VMEM((n_cam, 2, 128, 128), BF16),
            pltpu.VMEM((n_cam, 8, 128), jnp.int32),
            dma((8,)),
            dma((6,)),
            dma((58,)),
            dma((58,)),
            dma((n_cam,)),
            dma((n_cam,)),
            dma((n_cam,)),
            dma((n_cam,)),
        ],
        compiler_params=pltpu.CompilerParams(
            collective_id=0, has_side_effects=True, vmem_limit_bytes=40 * 1024 * 1024
        ),
    )(*[pltpu.with_memory_space_constraint(x, pltpu.HBM) for x in operands])
    advected, images = pl.pallas_call(
        write_kernel,
        out_shape=(
            jax.ShapeDtypeStruct(flat, F32),
            jax.ShapeDtypeStruct((2, NBLK, 128), F32),
        ),
        in_specs=[on_chip] * 3,
        out_specs=(hbm, hbm),
        scratch_shapes=[pltpu.VMEM((2, NBLK, 128), F32), dma((5,))],
        compiler_params=pltpu.CompilerParams(vmem_limit_bytes=16 * 1024 * 1024),
    )(*[pltpu.with_memory_space_constraint(x, pltpu.VMEM) for x in results])
    return advected.reshape(scalar.shape), images


def solution(mesh):
    sizes = tuple(mesh.shape[name] for name in ("cam", "ex", "ey"))
    placed = (
        P("ex", None, "ey", None, "cam"),
        P(None, "ex", None, "ey", None, "cam"),
        P("ex", None, "ey", None, "cam"),
        P(),
        P(None, ("cam", "ex", "ey")),
        P(None, ("cam", "ex", "ey")),
    )
    return jax.shard_map(
        functools.partial(per_device, sizes),
        mesh=mesh,
        in_specs=placed,
        out_specs=(P("ex", None, "ey", None, "cam"), P("cam", ("ex", "ey"), None)),
        check_vma=False,
    )
```

```python
import functools

import jax
import jax.numpy as jnp
import ml_dtypes
import numpy as np
from jax import lax
from jax.experimental import pallas as pl
from jax.experimental.pallas import tpu as pltpu
from jax.sharding import PartitionSpec as P

NBLK = 1024
STEP = 0.01
F32 = jnp.float32
BF16 = jnp.bfloat16


def legendre_seven(points):
    previous = points * 0.0 + 1.0
    current = points * 1.0
    for order in range(1, 7):
        following = ((2 * order + 1) * points * current - order * previous) / (order + 1)
        previous = current
        current = following
    return current


def gll_derivative():
    degree = 7
    gll_nodes = np.array(
        [
            -1.0,
            -0.8717401485096066,
            -0.5917001814331423,
            -0.2092992179024789,
            0.2092992179024789,
            0.5917001814331423,
            0.8717401485096066,
            1.0,
        ]
    )
    values = legendre_seven(gll_nodes)
    derivative = np.zeros((degree + 1, degree + 1))
    for target in range(degree + 1):
        for source in range(degree + 1):
            if target != source:
                derivative[target, source] = values[target] / (
                    values[source] * (gll_nodes[target] - gll_nodes[source])
                )
    derivative[0, 0] = -degree * (degree + 1) / 4.0
    derivative[degree, degree] = degree * (degree + 1) / 4.0
    return derivative


DERIV = gll_derivative()


def radial_matrix():
    table = np.kron(np.eye(16), DERIV.T).astype(np.float32)
    high = table.astype(ml_dtypes.bfloat16)
    low = (table - high.astype(np.float32)).astype(ml_dtypes.bfloat16)
    return np.block([[high, low], [high, np.zeros_like(low)]])


def cross_matrix():
    table = np.concatenate([np.kron(np.eye(8), DERIV), np.kron(DERIV, np.eye(8))])
    table = table.astype(np.float32)
    high = table.astype(ml_dtypes.bfloat16)
    low = (table - high.astype(np.float32)).astype(ml_dtypes.bfloat16)
    return np.concatenate([high, high, low], axis=1)


def azimuth_table():
    rows = np.arange(8)
    shifts = np.stack([DERIV[rows, (rows + d) % 8] for d in range(8)])
    return np.broadcast_to(shifts[:, :, None], (8, 8, 128)).astype(np.float32)


AXIAL = (1, 2, 0, 3)

SIGNS = [
    (sx, sy, sz)
    for sx in (-1, 0, 1)
    for sy in (-1, 0, 1)
    for sz in (-1, 0, 1)
    if (sx, sy, sz) != (0, 0, 0)
]


def kernel(
    sizes,
    scalar_h,
    vel_h,
    mass_h,
    wts_h,
    cut_h,
    blk_h,
    tab_h,
    azi_h,
    cross_h,
    adv,
    v_recv,
    img_hot,
    fld,
    vel,
    side,
    mass,
    wts,
    cut,
    blk,
    tab,
    azi,
    cross,
    g_ref,
    first,
    winv,
    radial,
    faces_one,
    faces_two,
    xcol,
    wide,
    wts_p,
    cut_hot,
    elems,
    v_send,
    blk_recv,
    in_sem,
    vel_sem,
    send_sem,
    recv_sem,
    v_send_sem,
    v_recv_sem,
    b_send_sem,
    b_recv_sem,
):
    n_cam, n_ex, n_ey = sizes
    cam, ex, ey = lax.axis_index("cam"), lax.axis_index("ex"), lax.axis_index("ey")
    faces = (faces_one, faces_two)

    def beside(at, size):
        return {
            0: at,
            1: jnp.where(at == size - 1, 0, at + 1),
            -1: jnp.where(at == 0, size - 1, at - 1),
        }

    cams, exs, eys = beside(cam, n_cam), beside(ex, n_ex), beside(ey, n_ey)
    peers = {s: {"cam": cams[s[2]], "ex": exs[s[0]], "ey": eys[s[1]]} for s in SIGNS}

    def camera_owner(d):
        return jnp.where(cam + d >= n_cam, cam + d - n_cam, cam + d)

    def along_cam(d):
        return {"cam": camera_owner(d), "ex": ex, "ey": ey}

    def load(src, dst, sem):
        copy = pltpu.make_async_copy(src, dst, sem)
        copy.start()
        return copy

    load_mass = load(mass_h, mass, in_sem.at[0])
    load_fld = load(scalar_h, fld, in_sem.at[1])
    load_tab = load(tab_h, tab, in_sem.at[2])
    load_azi = load(azi_h, azi, in_sem.at[3])
    load_cross = load(cross_h, cross, in_sem.at[7])

    def load_vel(a):
        load(vel_h.at[:, pl.ds(8 * a, 8)], vel.at[:, pl.ds(8 * a, 8)], vel_sem.at[a])

    load_sides = [
        load(vel_h.at[:, pl.ds(31 * px, 1)], side.at[px], vel_sem.at[4 + px]) for px in (0, 1)
    ]
    barrier = pltpu.get_barrier_semaphore()
    for s in sorted(SIGNS, key=lambda s: (-abs(s[0]), -abs(s[2]), -abs(s[1]))):
        pl.semaphore_signal(barrier, inc=1, device_id=peers[s], device_id_type=pl.DeviceIdType.MESH)
    for d in range(2, n_cam - 1):
        pl.semaphore_signal(
            barrier, inc=1, device_id=along_cam(d), device_id_type=pl.DeviceIdType.MESH
        )
    load_blk = load(blk_h, blk, in_sem.at[4])
    load_cut = load(cut_h, cut, in_sem.at[5])

    lane = lax.broadcasted_iota(jnp.int32, (8, 128), 1)
    sub = lax.broadcasted_iota(jnp.int32, (8, 128), 0)
    even = lane % 2 == 0
    take_next = (lane % 8 == 7) & (lane != 127)
    take_prev = (lane % 8 == 0) & (lane != 0)
    edge = (lane == 0) | (lane == 127)
    zero = jnp.zeros((8, 128), F32)
    has_upper, has_lower = cam < n_cam - 1, cam > 0
    from_upper = jnp.where(has_upper, 1.0, 0.0).astype(F32)
    from_lower = jnp.where(has_lower, 1.0, 0.0).astype(F32)
    keep = jnp.where(even, jnp.full((8, 128), from_upper), jnp.full((8, 128), from_lower)) > 0.5

    def lane_pairs(g):
        return (
            g
            + jnp.where(take_next, pltpu.roll(g, 127, 1), zero)
            + jnp.where(take_prev, pltpu.roll(g, 1, 1), zero)
        )

    def twice(body):
        def outer(which):
            @pl.loop(0, 2)
            def _(t):
                body(*((3 * t, 2 + t) if which == "ends" else (1 + t, t)))

        return outer

    copies = []

    def send(src, dst, e, group, slot, s):
        copy = pltpu.make_async_remote_copy(
            src_ref=src,
            dst_ref=dst,
            send_sem=send_sem.at[slot],
            recv_sem=recv_sem.at[slot],
            device_id=peers[s],
            device_id_type=pl.DeviceIdType.MESH,
        )
        copies.append((e, group, s[2], copy))
        if s[2] == 0:
            copy.start()

    def toward(sz, body):
        pl.when(has_upper if sz > 0 else has_lower)(body)

    def launch(sz, body):
        first_new = len(copies)
        body()
        chosen = [copy for _, _, _, copy in copies[first_new:]]

        def start():
            for copy in chosen:
                copy.start()

        toward(sz, start)

    def wait_all(e, groups, received):
        for sz in (0, -1, 1):
            chosen = [c for at, group, z, c in copies if at == e and group in groups and z == sz]

            def body(chosen=chosen):
                for copy in chosen:
                    if received:
                        copy.wait_recv()
                    else:
                        copy.wait_send()

            if sz == 0:
                body()
            else:
                toward(-sz if received else sz, body)

    def pair_azimuth(ref, a):
        for i in range(8):
            n = 8 * a + i
            both = ref[n, pl.ds(7, 7, stride=8), :] + ref[n, pl.ds(8, 7, stride=8), :]
            ref[n, pl.ds(7, 7, stride=8), :] = both
            ref[n, pl.ds(8, 7, stride=8), :] = both

    def pair_axial(ref):
        for a in range(3):
            both = ref[8 * a + 7] + ref[8 * a + 8]
            ref[8 * a + 7] = both
            ref[8 * a + 8] = both

    def gather_columns(pieces):
        parts = [zero] * 4
        for at, (spot, piece) in enumerate(pieces):
            here = (lane == 2 * spot) | (lane == 2 * spot + 1)
            parts[at % 4] = jnp.where(here, pltpu.roll(piece, 2 * spot + 1, 1), parts[at % 4])
        return (parts[0] + parts[1]) + (parts[2] + parts[3])

    def pair_plane(plane):
        both = plane[pl.ds(7, 7, stride=8), :] + plane[pl.ds(8, 7, stride=8), :]
        plane[pl.ds(7, 7, stride=8), :] = both
        plane[pl.ds(8, 7, stride=8), :] = both

    def pack_ends(e, kind):
        plane, tile = faces[e][0], faces[e][1]
        for px in (0, 1):
            tile[px, kind] = gather_columns(
                [(56 * px + b, plane[px, kind, 8 * b : 8 * b + 8, :]) for b in range(8)]
            )

    def send_ends(e):
        plane, r_plane, r_xy = faces[e][0], faces[e][5], faces[e][6]
        base = 30 * e
        for px in (0, 1):
            sx = 2 * px - 1
            send(plane.at[px], r_plane.at[px], e, "ends", base + px, (sx, 0, 0))
            for py in (0, 1):
                send(
                    plane.at[px, :, pl.ds(56 * py, 8)],
                    r_xy.at[px, py],
                    e,
                    "ends",
                    base + 2 + 2 * px + py,
                    (sx, 2 * py - 1, 0),
                )

    def send_end_columns(e):
        tile, r_xz, r_xyz = faces[e][1], faces[e][7], faces[e][8]
        base = 30 * e
        for pz in (0, 1):
            sz = 2 * pz - 1

            def body(pz=pz, sz=sz):
                for px in (0, 1):
                    sx = 2 * px - 1
                    slot = base + 6 + 6 * pz + 3 * px
                    send(tile.at[px], r_xz.at[px, pz], e, "ends", slot, (sx, 0, sz))
                    for py in (0, 1):
                        send(
                            tile.at[px],
                            r_xyz.at[px, py, pz],
                            e,
                            "ends",
                            slot + 1 + py,
                            (sx, 2 * py - 1, sz),
                        )

            launch(sz, body)

    def pick(parts, spot, piece):
        here = (lane == 2 * spot) | (lane == 2 * spot + 1)
        parts[spot % 4] = jnp.where(here, pltpu.roll(piece, 2 * spot + 1, 1), parts[spot % 4])

    def put_columns(parts, e, kind, slot):
        q = (parts[0] + parts[1]) + (parts[2] + parts[3])
        after = pltpu.roll(pltpu.roll(q, 126, 1), 7, 0)
        before = pltpu.roll(pltpu.roll(q, 2, 1), 1, 0)
        q = q + jnp.where((sub == 7) & (lane % 16 < 14), after, zero)
        q = q + jnp.where((sub == 0) & (lane % 16 >= 2), before, zero)
        faces[e][3][slot, kind] = q

    def send_columns(e, half):
        cols, r_cols = faces[e][3], faces[e][10]
        for pz in (0, 1):
            sz = 2 * pz - 1

            def body(pz=pz, sz=sz):
                part = pl.ds(2 * half, 2)
                send(
                    cols.at[part],
                    r_cols.at[pz, part],
                    e,
                    "rest",
                    30 * e + 18 + 2 * pz + half,
                    (0, 0, sz),
                )

            launch(sz, body)

    def pack_lines(e, kind):
        cols, lines = faces[e][3], faces[e][4]
        low, high = zero, zero
        for at in range(4):
            low = jnp.where(sub == at, jnp.broadcast_to(cols[at, kind, 0:1, :], (8, 128)), low)
            high = jnp.where(sub == at, jnp.broadcast_to(cols[at, kind, 7:8, :], (8, 128)), high)
        lines[0, kind] = low
        lines[1, kind] = high

    def send_lines(e):
        lines, r_yz = faces[e][4], faces[e][11]
        for pz in (0, 1):
            sz = 2 * pz - 1

            def body(pz=pz, sz=sz):
                for py in (0, 1):
                    send(
                        lines.at[py],
                        r_yz.at[py, pz],
                        e,
                        "rest",
                        30 * e + 22 + 2 * pz + py,
                        (0, 2 * py - 1, sz),
                    )

            launch(sz, body)

    def pack_rows(ref, e, kind):
        rows = faces[e][2]
        for n in range(32):
            rows[0, kind, n : n + 1, :] = ref[n, 0:1, :]
            rows[1, kind, n : n + 1, :] = ref[n, 63:64, :]

    def send_rows(e):
        rows, r_rows = faces[e][2], faces[e][9]
        for py in (0, 1):
            send(rows.at[py], r_rows.at[py], e, "rest", 30 * e + 26 + py, (0, 2 * py - 1, 0))

    def across_azimuth(t, py):
        t = pltpu.roll(t, 114 if py else 14, 1)
        return jnp.where((lane % 16 < 2) if py else (lane % 16 >= 14), t, zero)

    def swap(q):
        return jnp.where(keep, jnp.where(even, pltpu.roll(q, 127, 1), pltpu.roll(q, 1, 1)), zero)

    def add_rest(ref, e, kind):
        r_rows, r_cols, r_yz = faces[e][9:12]
        for n in range(32):
            after, before = r_rows[1, kind, n : n + 1, :], r_rows[0, kind, n : n + 1, :]
            if 0 < n < 31 and n % 8 in (0, 7):
                other = n + 1 if n % 8 == 7 else n - 1
                after = after + r_rows[1, kind, other : other + 1, :]
                before = before + r_rows[0, kind, other : other + 1, :]
            ref[n, 0:1, :] = ref[n, 0:1, :] + after
            ref[n, 63:64, :] = ref[n, 63:64, :] + before
        across = [
            across_azimuth(jnp.where(even, r_yz[py, 1, kind], r_yz[py, 0, kind]), py)
            for py in (0, 1)
        ]
        found = [None] * 4
        for at, a in enumerate(AXIAL):
            q = jnp.where(even, r_cols[1, at, kind], r_cols[0, at, kind])
            q = q + jnp.where(sub == 0, jnp.broadcast_to(across[1][at : at + 1, :], (8, 128)), zero)
            q = q + jnp.where(sub == 7, jnp.broadcast_to(across[0][at : at + 1, :], (8, 128)), zero)
            found[a] = q
        for a in range(4):
            q = found[a]
            if a < 3:
                q = q + jnp.where(lane >= 112, pltpu.roll(found[a + 1], 112, 1), zero)
            if a > 0:
                q = q + jnp.where(lane < 16, pltpu.roll(found[a - 1], 16, 1), zero)
            xcol[kind, a] = swap(q)

    def add_ends(ref, e, kind):
        r_plane, r_xy, r_xz, r_xyz = faces[e][5:9]
        for px in (0, 1):
            n, a = (0, 0) if px else (31, 3)
            ref[n] = ref[n] + r_plane[px, kind]
            for py in (0, 1):
                row, got = (0, 7) if py else (63, 0)
                ref[n, row : row + 1, :] = (
                    ref[n, row : row + 1, :] + r_xy[px, py, kind, got : got + 1, :]
                )
            q = jnp.where(even, r_xz[px, 1, kind], r_xz[px, 0, kind])
            for py in (0, 1):
                c = jnp.where(even, r_xyz[px, py, 1, kind], r_xyz[px, py, 0, kind])
                c = pltpu.roll(across_azimuth(c, py), 1 if py else 7, 0)
                q = q + jnp.where(sub == (0 if py else 7), c, zero)
            if px:
                q = jnp.where(lane < 16, pltpu.roll(q, 16, 1), zero)
            else:
                q = jnp.where(lane >= 112, pltpu.roll(q, 112, 1), zero)
            xcol[kind, a] = xcol[kind, a] + swap(q)

    def total(ref, x, n, i, b):
        spot = 8 * i + b
        return ref[n, 8 * b : 8 * b + 8, :] + jnp.where(
            edge, pltpu.roll(x, 127 - 2 * spot, 1), zero
        )

    def along_radius(block):
        high = block.astype(BF16)
        low = (block - high.astype(F32)).astype(BF16)
        both = jnp.dot(
            jnp.concatenate([high, low], axis=1), tab[...], preferred_element_type=F32
        )
        return both[:, :128] + both[:, 128:]

    def along_azimuth(f):
        turned = azi[0] * f
        for d in range(1, 8):
            turned = turned + azi[d] * pltpu.roll(f, 8 - d, 0)
        return turned

    def convect_plane(src, e, px):
        n, i = 31 * px, 7 * px
        plane = faces[e][0].at[px, 0]
        turning = along_radius(src[n])
        for b in range(8):
            part = slice(8 * b, 8 * b + 8)
            axial = None
            for p in range(8):
                term = float(DERIV[i, p]) * src[n - i + p, part, :]
                axial = term if axial is None else axial + term
            c = (
                side[px, 0, 0, part, :] * axial
                + side[px, 1, 0, part, :] * along_azimuth(src[n, part, :])
                + side[px, 2, 0, part, :] * turning[part, :]
            )
            plane[part, :] = lane_pairs(mass[n, part, :] * c)
        pair_plane(plane)

    def convect(src, a, e, slot):
        parts = [zero] * 4
        radial[...] = along_radius(src[pl.ds(8 * a, 8)].reshape(512, 128)).reshape(8, 64, 128)
        for b in range(0, 8, 2):
            pieces = []
            for d in (b, b + 1):
                block = src[pl.ds(8 * a, 8), 8 * d : 8 * d + 8, :].reshape(64, 128)
                high = block.astype(BF16)
                low = (block - high.astype(F32)).astype(BF16)
                pieces.append(jnp.concatenate([high, low, high], axis=0))
            both = jnp.dot(
                cross[...], jnp.concatenate(pieces, axis=1), preferred_element_type=F32
            )
            for d in (0, 1):
                part = slice(8 * (b + d), 8 * (b + d) + 8)
                lanes = slice(128 * d, 128 * d + 128)
                for i in range(8):
                    n = 8 * a + i
                    c = (
                        vel[0, n, part, :] * both[64 + 8 * i : 72 + 8 * i, lanes]
                        + vel[1, n, part, :] * both[8 * i : 8 * i + 8, lanes]
                        + vel[2, n, part, :] * radial[i, part, :]
                    )
                    g = mass[n, part, :] * c
                    pick(parts, 8 * i + b + d, g)
                    g_ref[n, part, :] = lane_pairs(g)
        put_columns(parts, e, 0, slot)
        pair_azimuth(g_ref, a)

    for pz in (0, 1):

        @pl.when(jnp.logical_not(has_lower if pz else has_upper))
        def _(pz=pz):
            for _, _, _, _, _, _, _, r_xz, r_xyz, _, r_cols, r_yz in faces:
                r_cols[pz] = jnp.zeros(r_cols.shape[1:], F32)
                for px in (0, 1):
                    r_xz[px, pz] = jnp.zeros(r_xz.shape[2:], F32)
                    r_yz[px, pz] = jnp.zeros(r_yz.shape[2:], F32)
                    for py in (0, 1):
                        r_xyz[px, py, pz] = jnp.zeros(r_xyz.shape[3:], F32)

    load_mass.wait()
    for a in (1, 2, 0, 3):
        load_vel(a)
    load_wts = load(wts_h, wts, in_sem.at[6])

    @twice
    def sum_mass(a, slot):
        parts = [zero] * 4
        for i in range(8):
            for b in range(8):
                n, part = 8 * a + i, slice(8 * b, 8 * b + 8)
                pick(parts, 8 * i + b, mass[n, part, :])
                winv[n, part, :] = lane_pairs(mass[n, part, :])
        put_columns(parts, 0, 1, slot)
        pair_azimuth(winv, a)

    sum_mass("ends")
    sum_mass("middle")
    for px in (0, 1):
        faces[0][0][px, 1] = winv[31 * px]
    pack_ends(0, 1)
    pack_lines(0, 1)
    pack_rows(winv, 0, 1)
    pair_axial(winv)

    load_fld.wait()
    load_tab.wait()
    load_azi.wait()
    load_cross.wait()

    def wait_velocity(a):
        part = pl.ds(8 * a, 8)
        pltpu.make_async_copy(vel_h.at[:, part], vel.at[:, part], vel_sem.at[a]).wait()

    for px in (0, 1):
        load_sides[px].wait()
        convect_plane(fld, 0, px)
    pl.semaphore_wait(barrier, 26 + n_cam - 3)
    send_ends(0)
    pack_ends(0, 0)
    send_end_columns(0)
    for a in range(4):
        wait_velocity(a)

    @twice
    def stage_one(a, slot):
        convect(fld, a, 0, slot)

    stage_one("middle")
    send_columns(0, 0)
    stage_one("ends")
    send_columns(0, 1)
    pack_lines(0, 0)
    send_lines(0)
    pack_rows(g_ref, 0, 0)
    send_rows(0)
    pair_axial(g_ref)

    load_blk.wait()
    blk_copies = []
    for d in range(1, n_cam):
        copy = pltpu.make_async_remote_copy(
            src_ref=blk,
            dst_ref=blk_recv.at[d],
            send_sem=b_send_sem.at[d],
            recv_sem=b_recv_sem.at[d],
            device_id=along_cam(d),
            device_id_type=pl.DeviceIdType.MESH,
        )
        copy.start()
        blk_copies.append(copy)

    load_cut.wait()
    load_wts.wait()

    @pl.loop(0, 8)
    def _(m):
        wide[...] = wts[m].astype(F32)
        for k in range(8):
            wts_p[m, 64 * k : 64 * k + 64, :] = wide[pl.ds(k, 64, stride=8), :].astype(BF16)
        chosen = jnp.broadcast_to(cut[pl.ds(m, 1), :].astype(F32), (128, 128)).T
        place = lax.broadcasted_iota(jnp.int32, (128, 128), 1).astype(F32)
        for q in range(4):
            cut_hot[m // 2, pl.ds(128 * (m % 2), 128), 128 * q : 128 * q + 128] = jnp.where(
                chosen == place + 128.0 * q, 1.0, 0.0
            ).astype(BF16)

    @twice
    def step_one(a, _):
        x, y = xcol[0, a], xcol[1, a]
        for i in range(8):
            for b in range(8):
                n, part = 8 * a + i, slice(8 * b, 8 * b + 8)
                factor = -STEP * pl.reciprocal(total(winv, y, n, i, b))
                winv[n, part, :] = factor
                first[n, part, :] = fld[n, part, :] + factor * total(g_ref, x, n, i, b)

    @twice
    def stage_two(a, slot):
        convect(first, a, 1, slot)

    wait_all(0, ("ends", "rest"), True)
    for ref, kind in ((winv, 1), (g_ref, 0)):
        add_rest(ref, 0, kind)
        add_ends(ref, 0, kind)
    step_one("ends")
    for px in (0, 1):
        convect_plane(first, 1, px)
    send_ends(1)
    pack_ends(1, 0)
    send_end_columns(1)
    step_one("middle")
    stage_two("middle")
    send_columns(1, 0)
    stage_two("ends")
    send_columns(1, 1)
    pack_lines(1, 0)
    send_lines(1)
    pack_rows(g_ref, 1, 0)
    send_rows(1)
    pair_axial(g_ref)

    for copy in blk_copies:
        copy.wait_recv()
    for d in range(n_cam):
        for t in range(2):
            if d == 0:
                ids = blk[pl.ds(2 * cam + t, 1), :]
            else:
                ids = blk_recv[d, pl.ds(2 * cam + t, 1), :]
            ids = jnp.broadcast_to(ids, (128, 128))
            for h in range(8):
                block_id = lax.broadcasted_iota(jnp.int32, (128, 128), 0) + 128 * h
                img_hot[t, 128 * h : 128 * h + 128, 128 * d : 128 * d + 128] = jnp.where(
                    ids == block_id, 1.0, 0.0
                ).astype(BF16)

    wide_lane = lax.broadcasted_iota(jnp.int32, (64, 128), 1)
    row64 = lax.broadcasted_iota(jnp.int32, (64, 128), 0)
    select = jnp.where(
        (wide_lane // 8 == row64 % 16) & ((wide_lane % 8) // 2 == row64 // 16), 1.0, 0.0
    ).astype(BF16)

    @twice
    def finish(a, _):
        x = xcol[0, a]
        for i in range(8):
            for b in range(8):
                n, part = 8 * a + i, slice(8 * b, 8 * b + 8)
                second = first[n, part, :] + winv[n, part, :] * total(g_ref, x, n, i, b)
                adv[n, part, :] = 0.5 * (fld[n, part, :] + second)
        for b in range(0, 8, 2):
            pieces = []
            for c in (b, b + 1):
                block = adv[pl.ds(8 * a, 8), 8 * c : 8 * c + 8, :].reshape(64, 128)
                pieces.append(jnp.where(wide_lane % 2 == 0, block, 0.0).astype(BF16))
                pieces.append(jnp.where(wide_lane % 2 == 1, block, 0.0).astype(BF16))
            out = lax.dot_general(
                select,
                jnp.concatenate(pieces, axis=0),
                (((1,), (1,)), ((), ())),
                preferred_element_type=F32,
            ).astype(BF16)
            for c in (0, 1):
                at = pl.multiple_of(128 * a + 16 * (b + c), 16)
                for h in range(4):
                    elems[pl.ds(at, 16), 128 * h : 128 * h + 128] = out[
                        16 * h : 16 * h + 16, 128 * c : 128 * c + 128
                    ]

    wait_all(1, ("rest",), True)
    add_rest(g_ref, 1, 0)
    finish("middle")
    wait_all(1, ("ends",), True)
    add_ends(g_ref, 1, 0)
    finish("ends")

    v_copies = []
    for d in sorted(range(1, n_cam), key=lambda d: -min(d, n_cam - d)) + [0]:
        q = camera_owner(d)
        picked = jnp.dot(cut_hot[q], elems[...], preferred_element_type=F32).astype(BF16)
        for t in range(2):
            value = jnp.dot(
                picked[128 * t : 128 * t + 128], wts_p[2 * q + t], preferred_element_type=F32
            ).astype(BF16)
            if d:
                v_send[d, t] = value
            else:
                v_recv[0, t] = value
        if d:
            copy = pltpu.make_async_remote_copy(
                src_ref=v_send.at[d],
                dst_ref=v_recv.at[d],
                send_sem=v_send_sem.at[d],
                recv_sem=v_recv_sem.at[d],
                device_id=along_cam(d),
                device_id_type=pl.DeviceIdType.MESH,
            )
            copy.start()
            v_copies.append(copy)

    for e in (0, 1):
        wait_all(e, ("ends", "rest"), False)
    for copy in blk_copies:
        copy.wait_send()
    for copy in v_copies:
        copy.wait_recv()
    for copy in v_copies:
        copy.wait_send()


def write_kernel(adv, values, img_hot, adv_h, img_h, img, sem):
    result = pltpu.make_async_copy(adv, adv_h, sem.at[0])
    result.start()
    n_cam = values.shape[0]
    copies = []
    for t in range(2):
        slots = jnp.concatenate([values[d, t] for d in range(n_cam)], axis=0)
        for h in range(2):
            part = pl.ds(h * (NBLK // 2), NBLK // 2)
            img[t, part] = jnp.dot(img_hot[t, part], slots, preferred_element_type=F32)
            copy = pltpu.make_async_copy(
                img.at[t, part], img_h.at[t, part], sem.at[1 + 2 * t + h]
            )
            copy.start()
            copies.append(copy)
    for copy in copies:
        copy.wait()
    result.wait()


def face_buffers(kinds):
    shapes = [
        (2, kinds, 64, 128),
        (2, kinds, 8, 128),
        (2, kinds, 32, 128),
        (4, kinds, 8, 128),
        (2, kinds, 8, 128),
        (2, kinds, 64, 128),
        (2, 2, kinds, 8, 128),
        (2, 2, kinds, 8, 128),
        (2, 2, 2, kinds, 8, 128),
        (2, kinds, 32, 128),
        (2, 4, kinds, 8, 128),
        (2, 2, kinds, 8, 128),
    ]
    return tuple(pltpu.VMEM(shape, F32) for shape in shapes)


def per_device(sizes, scalar, velocity, lumped_mass, pixel_weights, cut_element, pixel_block):
    n_cam = sizes[0]
    flat = (32, 64, 128)
    hbm = pl.BlockSpec(memory_space=pltpu.HBM)
    big = pltpu.VMEM(flat, F32)
    dma = pltpu.SemaphoreType.DMA
    on_chip = pl.BlockSpec(memory_space=pltpu.VMEM)
    outputs = (
        pltpu.VMEM(flat, F32),
        pltpu.VMEM((n_cam, 2, 128, 128), BF16),
        pltpu.VMEM((2, NBLK, 128 * n_cam), BF16),
    )
    operands = (
        scalar.reshape(flat),
        velocity.reshape((3,) + flat),
        lumped_mass.reshape(flat),
        pixel_weights,
        cut_element,
        pixel_block,
        jnp.asarray(radial_matrix()),
        jnp.asarray(azimuth_table()),
        jnp.asarray(cross_matrix()),
    )
    results = pl.pallas_call(
        functools.partial(kernel, sizes),
        out_shape=outputs,
        in_specs=[hbm] * 9,
        out_specs=(on_chip,) * 3,
        scratch_shapes=[
            big,
            pltpu.VMEM((3,) + flat, F32),
            pltpu.VMEM((2, 3, 1, 64, 128), F32),
            big,
            pltpu.VMEM((8, 512, 128), BF16),
            pltpu.VMEM((8, 128), jnp.int32),
            pltpu.VMEM((8, 128), jnp.int32),
            pltpu.VMEM((256, 256), BF16),
            pltpu.VMEM((8, 8, 128), F32),
            pltpu.VMEM((128, 192), BF16),
            big,
            big,
            big,
            pltpu.VMEM((8, 64, 128), F32),
            face_buffers(2),
            face_buffers(1),
            pltpu.VMEM((2, 4, 8, 128), F32),
            pltpu.VMEM((512, 128), F32),
            pltpu.VMEM((8, 512, 128), BF16),
            pltpu.VMEM((4, 256, 512), BF16),
            pltpu.VMEM((512, 512), BF16),
            pltpu.VMEM((n_cam, 2, 128, 128), BF16),
            pltpu.VMEM((n_cam, 8, 128), jnp.int32),
            dma((8,)),
            dma((6,)),
            dma((58,)),
            dma((58,)),
            dma((n_cam,)),
            dma((n_cam,)),
            dma((n_cam,)),
            dma((n_cam,)),
        ],
        compiler_params=pltpu.CompilerParams(
            collective_id=0, has_side_effects=True, vmem_limit_bytes=40 * 1024 * 1024
        ),
    )(*[pltpu.with_memory_space_constraint(x, pltpu.HBM) for x in operands])
    advected, images = pl.pallas_call(
        write_kernel,
        out_shape=(
            jax.ShapeDtypeStruct(flat, F32),
            jax.ShapeDtypeStruct((2, NBLK, 128), F32),
        ),
        in_specs=[on_chip] * 3,
        out_specs=(hbm, hbm),
        scratch_shapes=[pltpu.VMEM((2, NBLK, 128), F32), dma((5,))],
        compiler_params=pltpu.CompilerParams(vmem_limit_bytes=16 * 1024 * 1024),
    )(*[pltpu.with_memory_space_constraint(x, pltpu.VMEM) for x in results])
    return advected.reshape(scalar.shape), images


def solution(mesh):
    sizes = tuple(mesh.shape[name] for name in ("cam", "ex", "ey"))
    placed = (
        P("ex", None, "ey", None, "cam"),
        P(None, "ex", None, "ey", None, "cam"),
        P("ex", None, "ey", None, "cam"),
        P(),
        P(None, ("cam", "ex", "ey")),
        P(None, ("cam", "ex", "ey")),
    )
    return jax.shard_map(
        functools.partial(per_device, sizes),
        mesh=mesh,
        in_specs=placed,
        out_specs=(P("ex", None, "ey", None, "cam"), P("cam", ("ex", "ey"), None)),
        check_vma=False,
    )
```
